32 devices in a mesh: dp: 8 (over z, x), tensor: 4 (over y, core).
Axes of the slice: x: 2, y: 2, z: 4, core: 2. Of those that a mesh axis runs over, the one named last changes fastest.
Arguments:
- adapter_in: bfloat16 [1024, 16, 2048], P('tensor', 'dp'), may hold values from -6 to 6
- lengths: int32 [16], P('dp'), may hold values from 1 to 1024, as said below
- cotangent: bfloat16 [1024, 16, 1024], P('tensor', 'dp'), may hold values from -6 to 6
- adapter_weight: bfloat16 [2048, 1024], replicated, may hold values from -0.125 to 0.125
- gains: float32 [4, 1024], replicated, may hold values from 0.25 to 1.75
- query_key_value_weight: bfloat16 [1024, 3, 1024], P(None, None, 'tensor'), may hold values from -0.25 to 0.25
- attention_output_weight: bfloat16 [1024, 1024], P('tensor'), may hold values from -0.1875 to 0.1875
- gate_up_weight: bfloat16 [1024, 2, 2816], P(None, None, 'tensor'), may hold values from -0.1875 to 0.1875
- down_weight: bfloat16 [2816, 1024], P('tensor'), may hold values from -0.109375 to 0.109375
Outputs:
- block_out: bfloat16 [1024, 16, 1024], P('tensor', 'dp')
- grad_in: bfloat16 [1024, 16, 2048], P('tensor', 'dp')
- grad_adapt: float32 [2048, 1024], P(('dp', 'tensor'))
- grad_gains: float32 [4, 1024], P(None, ('dp', 'tensor'))
- grad_qkv: float32 [1024, 3, 1024], P('dp', None, 'tensor')
- grad_out: float32 [1024, 1024], P('tensor', 'dp')
- grad_gate_up: float32 [1024, 2, 2816], P('dp', None, 'tensor')
- down_weight_gradient: float32 [2816, 1024], P('tensor', 'dp')
The draws below stay inside these ranges and needn't reach their ends.
Inputs may be any that keep to these rules, and one draw needn't show every extreme that they name: `lengths`: valid tokens of each sequence, counted from its start; later positions are padding.
All inputs are finite; a program needn't handle non-finite values.
Results may differ from the reference program's by a relative error of at most 0.025.
The reference program's roundings to bfloat16 on the way count: a program that leaves them out, or rounds other values in their place, can miss the bound.
Values may be sent and summed in bfloat16 or wider, within the bound.
No kernel may reach another device: no remote copies, remote signals or barrier semaphores. Data moves between devices by JAX's collectives and lax.ppermute only.
A program may use at most 192 MiB of HBM per device.

```python
import math
import jax
import jax.numpy as jnp
from jax import lax

D = 1024
HEADS = 8
HD = 128
FF = 2816
LEN = 1024
SEQS = 2
BATCH = 16


def draw_lengths(key, part):
    pick_key, long_key, short_key, full_key = jax.random.split(key, 4)
    groups = BATCH // SEQS
    chosen = jax.random.randint(pick_key, (groups, 1), 0, SEQS)
    long_len = LEN - jax.random.randint(long_key, (groups, 1), 0, LEN // 4)
    full_group = jax.random.randint(full_key, (1, 1), 0, groups)
    long_len = jnp.where(jnp.arange(groups)[:, None] == full_group, LEN, long_len)
    short_len = jax.random.randint(short_key, (groups, SEQS), 1, LEN + 1)
    picked = jnp.where(jnp.arange(SEQS)[None, :] == chosen, long_len, short_len)
    return picked.reshape(BATCH).astype(jnp.int32)


def block_scale(stream_key, shape, pieces, least, high):
    factor_of, own = 1.0, jax.random.fold_in(stream_key, 6)
    for axis_at, parts in pieces:
        draws = jnp.exp(jax.random.uniform(jax.random.fold_in(own, axis_at), (parts,), jnp.float32, least / len(pieces), high / len(pieces)))
        factor_of = factor_of * jnp.repeat(draws, shape[axis_at] // parts).reshape([-1 if axis == axis_at else 1 for axis in range(len(shape))])
    return factor_of


def centred(rng, extent, width, reach, cuts=(), kind=jnp.bfloat16):
    drawn = jax.random.normal(rng, extent, jnp.float32) * width
    if len(cuts) > 0:
        drawn = block_scale(rng, extent, cuts, -0.22, 0.18) * drawn
    return jnp.clip(drawn, min=-reach, max=reach).astype(kind)


def setup_inputs(seed: int = 0) -> dict:
    streams_of = jax.random.split(jax.random.key(seed), 10)
    adapter_in = centred(streams_of[0], (LEN, BATCH, 2 * D), 1.0, 6.0, ((0, 4), (1, 8)))
    lengths = draw_lengths(jax.random.fold_in(streams_of[9], 71), 0)
    cotangent = centred(streams_of[2], (LEN, BATCH, D), 1.0, 6.0, ((0, 4), (1, 8)))
    adapter_weight = centred(streams_of[3], (2 * D, D), (2 * D) ** -0.5, 0.125)
    gains = jnp.clip(1.0 + 0.15 * jax.random.normal(streams_of[4], (4, D), jnp.float32), 0.25, 1.75)
    query_key_value_weight = centred(streams_of[5], (D, 3, D), (D // 2) ** -0.5, 0.25, ((2, 4),))
    attention_output_weight = centred(streams_of[6], (D, D), D ** -0.5, 0.1875, ((0, 4),))
    gate_up_weight = centred(streams_of[7], (D, 2, FF), D ** -0.5, 0.1875, ((2, 4),))
    down_weight = centred(streams_of[8], (FF, D), FF ** -0.5, 0.109375, ((0, 4),))
    return dict(adapter_in=adapter_in, lengths=lengths, cotangent=cotangent, adapter_weight=adapter_weight, gains=gains, query_key_value_weight=query_key_value_weight, attention_output_weight=attention_output_weight, gate_up_weight=gate_up_weight, down_weight=down_weight)


epsilon = 1e-06
theta_base = 50000.0
masked_score = -1e+30
exact_setting = lax.Precision.HIGHEST

@jax.custom_vjp
def low(v):
    return lax.optimization_barrier(v.astype(jnp.bfloat16)).astype(jnp.float32)

@jax.custom_vjp
def reduced_backward(v):
    return v

def low_keep(v):
    return (low(v), None)

def low_pass(kept, grad):
    return (grad,)

def back_keep(v):
    return (v, None)

def back_low(kept, grad):
    return (low(grad),)
low.defvjp(low_keep, low_pass)
reduced_backward.defvjp(back_keep, back_low)

def norm_apply(source, gain_row):
    return source * lax.rsqrt(lax.optimization_barrier(jnp.mean(source * source, axis=-1, keepdims=True)) + epsilon) * gain_row

def rotary_tables(count):
    half_size = HD // 2
    frequency = theta_base ** (-(jnp.arange(half_size, dtype=jnp.float32) * 2.0 / HD))
    angles = jnp.arange(count, dtype=jnp.float32)[:, None] * frequency[None, :]
    return (jnp.cos(angles)[None, :, None, :], jnp.sin(angles)[None, :, None, :])

def rotate(source, cosine_table, sine_table):
    half_size = source.shape[-1] // 2
    lower_half, upper_half = (source[..., :half_size], source[..., half_size:])
    return jnp.concatenate([lower_half * cosine_table - upper_half * sine_table, upper_half * cosine_table + lower_half * sine_table], axis=-1)

def attend(queries, keys_rot, values, lengths):
    seq_count, seq_len = (queries.shape[0], queries.shape[1])
    block_rows = min(512, seq_len)
    count_blocks = seq_len // block_rows
    key_index = jnp.arange(seq_len, dtype=jnp.int32)
    key_live = key_index[None, :] < lengths[:, None]
    scale_factor = HD ** (-0.5)
    query_blocks = queries.reshape(seq_count, count_blocks, block_rows, HEADS, HD).transpose(1, 0, 2, 3, 4)

    def one_block(inputs):
        query_block, offset = inputs
        query_index = offset + jnp.arange(block_rows, dtype=jnp.int32)
        raw_scores = reduced_backward(jnp.einsum('sqhe,skhe->shqk', query_block, keys_rot, precision=exact_setting) * scale_factor)
        allowed = (key_index[None, :] <= query_index[:, None])[None, None] & key_live[:, None, None, :]
        masked = jnp.where(allowed, raw_scores, masked_score)
        highest = lax.optimization_barrier(jnp.max(masked, axis=-1, keepdims=True))
        weights = jnp.exp(masked - highest)
        probabilities = low(weights / lax.optimization_barrier(jnp.sum(weights, axis=-1, keepdims=True)))
        return jnp.einsum('shqk,skhe->sqhe', probabilities, values, precision=exact_setting)
    offsets = jnp.arange(count_blocks, dtype=jnp.int32) * block_rows
    mixed = lax.map(jax.checkpoint(one_block), (query_blocks, offsets))
    return mixed.transpose(1, 0, 2, 3, 4).reshape(seq_count, seq_len, HEADS * HD)

def core_layer(input_stack, adapter_weight, gains, query_key_value_weight, attention_output_weight, gate_up_weight, down_weight, lengths):
    seq_count, seq_len = (input_stack.shape[0], input_stack.shape[1])
    latent_state = reduced_backward(jnp.einsum('azm,mt->azt', input_stack, adapter_weight, precision=exact_setting))
    first_normed = low(norm_apply(latent_state, gains[0]))
    adapter_output = reduced_backward(jnp.einsum('zoa,ahj->zohj', first_normed, query_key_value_weight, precision=exact_setting))
    cosine_table, sine_table = rotary_tables(seq_len)
    split_shape = (seq_count, seq_len, HEADS, HD)
    queries = low(rotate(adapter_output[:, :, 0].reshape(split_shape), cosine_table, sine_table))
    keys_rot = low(rotate(adapter_output[:, :, 1].reshape(split_shape), cosine_table, sine_table))
    values = low(adapter_output[:, :, 2].reshape(split_shape))
    attention_result = low(reduced_backward(attend(queries, keys_rot, values, lengths)))
    attention_projected = reduced_backward(jnp.einsum('ezc,ch->ezh', attention_result, attention_output_weight, precision=exact_setting))
    latent_mid = latent_state + norm_apply(attention_projected, gains[1])
    third_normed = low(norm_apply(latent_mid, gains[2]))
    gate_up_values = reduced_backward(jnp.einsum('zoa,ahj->zohj', third_normed, gate_up_weight, precision=exact_setting))
    hidden_state = low(jax.nn.silu(gate_up_values[:, :, 0]) * gate_up_values[:, :, 1])
    feedforward_projected = reduced_backward(jnp.einsum('ezc,ch->ezh', hidden_state, down_weight, precision=exact_setting))
    return latent_mid + norm_apply(feedforward_projected, gains[3])

def reference(adapter_in, lengths, cotangent, adapter_weight, gains, query_key_value_weight, attention_output_weight, gate_up_weight, down_weight):
    group_size = math.gcd(BATCH, max(1, 4096 // LEN))
    steps_count = BATCH // group_size
    weights_all = (adapter_weight.astype(jnp.float32), gains.astype(jnp.float32), query_key_value_weight.astype(jnp.float32), attention_output_weight.astype(jnp.float32), gate_up_weight.astype(jnp.float32), down_weight.astype(jnp.float32))

    def arrange(stacked):
        moved = jnp.swapaxes(stacked, 0, 1)
        return moved.reshape((steps_count, group_size) + moved.shape[1:])
    inputs_seq = arrange(adapter_in)
    cot_seq = arrange(cotangent)
    len_seq = lengths.reshape(steps_count, group_size)

    def one_step(totals, inputs):
        block_in, block_cot, block_len = inputs
        live_rows = (jnp.arange(LEN, dtype=jnp.int32)[None, :] < block_len[:, None]).astype(jnp.float32)[:, :, None]

        def forward_pass(layer_input, *weight_list):
            return core_layer(layer_input, *weight_list, block_len)
        block_out, pullback = jax.vjp(forward_pass, block_in.astype(jnp.float32), *weights_all)
        gradients = pullback(block_cot.astype(jnp.float32) * live_rows)
        new_totals = tuple((total_item + grad_item for total_item, grad_item in zip(totals, gradients[1:])))
        return (new_totals, (block_out.astype(jnp.bfloat16), gradients[0].astype(jnp.bfloat16)))
    start_totals = tuple((jnp.zeros_like(weight_item) for weight_item in weights_all))
    totals, (out_blocks, grad_blocks) = lax.scan(one_step, start_totals, (inputs_seq, cot_seq, len_seq))

    def restore(stacked):
        return jnp.swapaxes(stacked.reshape((BATCH,) + stacked.shape[2:]), 0, 1)
    return (restore(out_blocks), restore(grad_blocks), totals[0], totals[1], totals[2], totals[3], totals[4], totals[5])
```

```python
import functools

import jax
import jax.numpy as jnp
import numpy as np
from jax import lax
from jax.experimental import pallas as pl
from jax.experimental.pallas import tpu as pltpu
from jax.sharding import PartitionSpec as P

HD = 128
LOG2E = 1.4426950408889634
EPS = 1e-06
THETA = 50000.0
MASKED = -1e30
f32 = jnp.float32
bf16 = jnp.bfloat16
MIB = 1024 * 1024
LIGHT = pl.CostEstimate(flops=1, bytes_accessed=1, transcendentals=0)


def dot(a, b):
    return jnp.dot(a, b, preferred_element_type=f32)


def dot_nt(a, b):
    return lax.dot_general(a, b, (((1,), (1,)), ((), ())), preferred_element_type=f32)


def dot_tn(a, b):
    return lax.dot_general(a, b, (((0,), (0,)), ((), ())), preferred_element_type=f32)


def whole_call(kernel, outs, scalars, arrays, scratch=(), vmem=40, name=None):
    smem = pl.BlockSpec(memory_space=pltpu.SMEM)
    vm = pl.BlockSpec(memory_space=pltpu.VMEM)
    return pl.pallas_call(
        kernel,
        out_shape=tuple(jax.ShapeDtypeStruct(s, d) for s, d in outs),
        in_specs=[smem] * len(scalars) + [vm] * len(arrays),
        out_specs=tuple(vm for _ in outs),
        scratch_shapes=list(scratch),
        compiler_params=pltpu.CompilerParams(vmem_limit_bytes=vmem * MIB),
        cost_estimate=LIGHT,
        name=name,
    )(*scalars, *arrays)


def swap(x, axis, bit):
    n = lax.axis_size(axis)
    return lax.ppermute(x, axis, [(i, i ^ bit) for i in range(n)])


def gather_blocks(x):
    far = swap(x, "tensor", 2)
    near = swap(x, "tensor", 1)
    return [x, near, far, swap(far, "tensor", 1)]


def scatter_blocks(p0, p1, p2, p3):
    near = swap(p1, "tensor", 1)
    across = (p2.astype(f32) + swap(p3, "tensor", 1).astype(f32)).astype(bf16)
    return across, (p0, near, swap(across, "tensor", 2))


def in_hbm(x):
    return pltpu.with_memory_space_constraint(x, pltpu.HBM)


def after(x, *others):
    return lax.optimization_barrier((x,) + others)[0]


def turn_tables(turn_rows, turn_blocks, j):
    cr, sr = turn_rows[0], turn_rows[1]
    cb, sb = turn_blocks[0, j : j + 1, :], turn_blocks[1, j : j + 1, :]
    sign = jnp.where(lax.broadcasted_iota(jnp.int32, (1, HD), 1) < HD // 2, -1.0, 1.0)
    return cb * cr - sb * sr, (sb * cr + cb * sr) * sign


def attn_fwd_kernel(seq, scal, x0, x1, x2, x3, w, turn_rows, turn_blocks, wo, q, k, v, o, lse, att, *parts):
    mine, length = scal[0], scal[1 + seq]
    rows = x0.shape[0]
    heads = q.shape[0]
    for j, x in enumerate((x0, x1, x2, x3)):
        base = pl.multiple_of((mine ^ j) * rows, rows)
        c, s = turn_tables(turn_rows, turn_blocks, j)
        for n, ref in ((0, q), (1, k)):
            acc = dot(x[...], w[n])
            for h in range(heads):
                part = acc[:, h * HD : (h + 1) * HD]
                turned = part * c + pltpu.roll(part, HD // 2, 1) * s
                ref[h, pl.ds(base, rows), :] = turned.astype(bf16)
        acc = dot(x[...], w[2]).astype(bf16)
        for h in range(heads):
            v[h, pl.ds(base, rows), :] = acc[:, h * HD : (h + 1) * HD]
    factor = HD**-0.5 * LOG2E
    for h in range(heads):
        vt = v[h].T
        for i in range(4):
            keys = (i + 1) * rows
            st = dot_nt(k[h, :keys, :], q[h, i * rows : keys, :]) * factor
            key_id = lax.broadcasted_iota(jnp.int32, st.shape, 0)
            row_id = lax.broadcasted_iota(jnp.int32, st.shape, 1) + i * rows
            st = jnp.where((key_id <= row_id) & (key_id < length), st, MASKED)
            top = jnp.max(st, axis=0, keepdims=True)
            weights = jnp.exp2(st - top)
            total = jnp.sum(weights, axis=0, keepdims=True)
            ot = dot(vt[:, :keys], weights.astype(bf16)) / total
            o[h, i * rows : keys, :] = ot.T.astype(bf16)
            lse[h : h + 1, i * rows : keys] = top + jnp.log2(total)
    for j in range(4):
        base = pl.multiple_of((mine ^ j) * rows, rows)
        both = jnp.concatenate([o[h, pl.ds(base, rows), :] for h in range(heads)], axis=1)
        att[j] = both
        parts[j][...] = dot(both, wo[...]).astype(bf16)


def attn_bwd_kernel(
    seq, scal, g0, g1, g2, g3, wo, q, k, v, o, lse, turn_rows, turn_blocks, w, st_out, p0, p1, p2, p3, dout, dq, dk, dv
):
    parts = (p0, p1, p2, p3)
    mine, length = scal[0], scal[1 + seq]
    rows = g0.shape[0]
    heads = q.shape[0]
    cols = heads * HD
    for j, g in enumerate((g0, g1, g2, g3)):
        mixed = dot_nt(g[...], wo[...]).astype(bf16)
        base = pl.multiple_of((mine ^ j) * rows, rows)
        for h in range(heads):
            dout[h, pl.ds(base, rows), :] = mixed[:, h * HD : (h + 1) * HD]
    scale = HD**-0.5
    factor = scale * LOG2E
    ones = jnp.ones((8, HD), f32)
    for h in range(heads):
        for i in (3, 2, 1, 0):
            keys = (i + 1) * rows
            here = slice(i * rows, keys)
            qi, di = q[h, here, :], dout[h, here, :]
            st = dot_nt(k[h, :keys, :], qi) * factor
            key_id = lax.broadcasted_iota(jnp.int32, st.shape, 0)
            row_id = lax.broadcasted_iota(jnp.int32, st.shape, 1) + i * rows
            st = jnp.where((key_id <= row_id) & (key_id < length), st, MASKED)
            probs = jnp.exp2(st - lse[h : h + 1, here])
            prob_grad = dot_nt(v[h, :keys, :], di)
            product = di.astype(f32) * o[h, here, :].astype(f32)
            inner = lax.dot_general(
                ones, product, (((1,), (1,)), ((), ())), precision=lax.Precision.HIGHEST, preferred_element_type=f32
            )[0:1, :]
            sg = (probs * (prob_grad - inner)).astype(bf16)
            new_v = dot(probs.astype(bf16), di)
            new_k = dot(sg, qi)
            if i == 3:
                dv[h] = new_v
                dk[h] = new_k
            else:
                dv[h, :keys, :] += new_v
                dk[h, :keys, :] += new_k
            dq[h, here, :] = dot_tn(sg, k[h, :keys, :])
    for j in range(4):
        base = pl.multiple_of((mine ^ j) * rows, rows)
        c, s = turn_tables(turn_rows, turn_blocks, j)
        c, s = c * scale, s * scale
        total = None
        for n, ref in enumerate((dq, dk, dv)):
            pieces = []
            for h in range(heads):
                part = ref[h, pl.ds(base, rows), :]
                if n < 2:
                    part = part * c - pltpu.roll(part, HD // 2, 1) * s
                pieces.append(part.astype(bf16))
            piece = jnp.concatenate(pieces, axis=1)
            st_out[j, :, n * cols : (n + 1) * cols] = piece
            add = dot_nt(piece, w[n])
            total = add if total is None else total + add
        parts[j][...] = total.astype(bf16)


def mlp_fwd_kernel(x0, x1, wgu, wd, hid, fa, fb, *parts):
    for j, x in enumerate((x0, x1)):
        gate = dot_nt(x[...], wgu[0])
        up = dot_nt(x[...], wgu[1])
        sig = jax.nn.sigmoid(gate)
        act = gate * sig
        hidden = (act * up).astype(bf16)
        hid[j] = hidden
        fa[j] = act.astype(bf16)
        fb[j] = (up * sig * (1.0 + gate * (1.0 - sig))).astype(bf16)
        parts[j][...] = dot(hidden, wd[...]).astype(bf16)


def mlp_bwd_kernel(g0, g1, wd, wgu, fa, fb, gg, gu, *parts):
    for j, g in enumerate((g0, g1)):
        hidden_grad = dot_nt(g[...], wd[...])
        gate_grad = (hidden_grad * fb[j].astype(f32)).astype(bf16)
        up_grad = (hidden_grad * fa[j].astype(f32)).astype(bf16)
        gg[j] = gate_grad
        gu[j] = up_grad
        parts[j][...] = (dot(gate_grad, wgu[0]) + dot(up_grad, wgu[1])).astype(bf16)


def factor_of(v):
    return lax.rsqrt(jnp.mean(v * v, axis=-1, keepdims=True) + EPS)


def norm_back(v, r, gain, e):
    scaled = e * gain
    inner = jnp.mean(scaled * v, axis=-1, keepdims=True)
    grad = r * (scaled - v * (r * r * inner))
    return grad, jnp.sum(e * v * r, axis=0, keepdims=True)


def summed(p0, near, far):
    return p0[...].astype(f32) + near[...].astype(f32) + far[...].astype(f32)


def mid_kernel(latent, p0, near, far, gains, proj_out, mid_out, normed_out):
    proj = summed(p0, near, far)
    mid = latent[...] + proj * factor_of(proj) * gains[1:2, :]
    proj_out[...] = proj
    mid_out[...] = mid
    normed_out[...] = (mid * factor_of(mid) * gains[2:3, :]).astype(bf16)


def live_grad(seq, scal, cot):
    rows = cot.shape[0]
    row_id = lax.broadcasted_iota(jnp.int32, (rows, 1), 0) + scal[0] * rows
    return jnp.where(row_id < scal[1 + seq], cot[...].astype(f32), 0.0)


def out_kernel(seq, scal, mid, p0, near, far, cot, gains, out, grad_out, gain_out):
    proj = summed(p0, near, far)
    r = factor_of(proj)
    gain = gains[3:4, :]
    out[...] = (mid[...] + proj * r * gain).astype(bf16)
    grad, gain_grad = norm_back(proj, r, gain, live_grad(seq, scal, cot))
    grad_out[...] = grad.astype(bf16)
    gain_out[...] = gain_grad


def back_kernel(seq, scal, mid, proj, p0, near, far, cot, gains, mid_grad_out, grad_out, gain_two, gain_three):
    three = summed(p0, near, far)
    m = mid[...]
    part, g3 = norm_back(m, factor_of(m), gains[2:3, :], three)
    mid_grad = live_grad(seq, scal, cot) + part
    pr = proj[...]
    grad, g2 = norm_back(pr, factor_of(pr), gains[1:2, :], mid_grad)
    mid_grad_out[...] = mid_grad
    grad_out[...] = grad.astype(bf16)
    gain_two[...] = g2
    gain_three[...] = g3


def last_kernel(latent, p0, near, far, mid_grad, gains, grad_out, gain_out):
    one = summed(p0, near, far)
    la = latent[...]
    part, g1 = norm_back(la, factor_of(la), gains[0:1, :], one)
    grad_out[...] = (mid_grad[...] + part).astype(bf16)
    gain_out[...] = g1


def first_kernel(x, w, gains, *refs):
    outs, acc = refs[:-1], refs[-1]
    seqs = len(outs) // 2
    whole = dot(x[...], w[...])
    rows, tiles = acc.shape[1] // seqs, acc.shape[0]
    for c in range(tiles):
        acc[c] = whole[:, c * 128 : (c + 1) * 128]
    for s in range(seqs):
        latent = jnp.concatenate([acc[c, pl.ds(s, rows, stride=seqs), :] for c in range(tiles)], axis=1)
        outs[s][...] = latent
        outs[seqs + s][...] = (latent * factor_of(latent) * gains[0:1, :]).astype(bf16)


def reversed_bits(index, bits):
    out = 0
    for b in range(bits):
        out = out + (((index >> b) & 1) << (bits - 1 - b))
    return out


def pair_block(g, me, pairs):
    return (me[0] >> 1) ^ reversed_bits(g, pairs.bit_length() - 1)


def grad_call(kernel, me, fixed, sliced, out, pairs, scratch=()):
    rows, d = sliced[0].shape
    wide = d // pairs
    shape = jax.ShapeDtypeStruct((pairs,) + out, bf16)
    spec = pl.BlockSpec((1,) + out, lambda g, m: (g,) + (0,) * len(out))

    def full_map(a):
        return lambda g, m: (0,) * a.ndim

    return pl.pallas_call(
        kernel,
        out_shape=(shape, shape),
        grid_spec=pltpu.PrefetchScalarGridSpec(
            num_scalar_prefetch=1,
            grid=(pairs,),
            in_specs=[pl.BlockSpec(a.shape, full_map(a)) for a in fixed]
            + [pl.BlockSpec((rows, wide), lambda g, m: (0, pair_block(g, m, pairs))) for _ in sliced],
            out_specs=(spec, spec),
            scratch_shapes=list(scratch),
        ),
        compiler_params=pltpu.CompilerParams(vmem_limit_bytes=24 * MIB),
        cost_estimate=LIGHT,
        name="weight_grad",
    )(me, *[in_hbm(a) for a in fixed], *[in_hbm(a) for a in sliced])


def grad_rows(me, xs, ys, dp, cols):
    pairs = dp // 2
    half = xs[0].shape[1] // dp
    count = ys[0].shape[-1] // cols

    def kernel(me_ref, *refs):
        yr, xr, (keep, send) = refs[: len(ys)], refs[len(ys) : len(ys) + len(xs)], refs[len(ys) + len(xs) :]
        lhs = jnp.concatenate([x[...] for x in xr], axis=0)
        rhs = jnp.concatenate([y[b] for y in yr for b in range(y.shape[0])], axis=0)
        acc = dot_tn(lhs, rhs)
        odd = (me_ref[0] & 1) == 1
        stay = jnp.where(odd, acc[half:], acc[:half]).astype(bf16)
        go = jnp.where(odd, acc[:half], acc[half:]).astype(bf16)
        for n in range(count):
            keep[0, n] = stay[:, n * cols : (n + 1) * cols]
            send[0, n] = go[:, n * cols : (n + 1) * cols]

    return grad_call(kernel, me, ys, xs, (count, half, cols), pairs)


def grad_cols(me, xs, ys, dp):
    pairs = dp // 2
    half = ys[0].shape[1] // dp
    m = xs[0].shape[-1]
    tokens = len(ys) * ys[0].shape[0]

    def kernel(me_ref, *refs):
        xr, yr, (keep, send, turned) = refs[: len(xs)], refs[len(xs) : len(xs) + len(ys)], refs[len(xs) + len(ys) :]

        @pl.when(pl.program_id(0) == 0)
        def _():
            turned[...] = jnp.concatenate([x[b] for x in xr for b in range(x.shape[0])], axis=0).T

        rhs = jnp.concatenate([y[...] for y in yr], axis=0)
        acc = dot(turned[...], rhs)
        odd = (me_ref[0] & 1) == 1
        keep[0] = jnp.where(odd, acc[:, half:], acc[:, :half]).astype(bf16)
        send[0] = jnp.where(odd, acc[:, :half], acc[:, half:]).astype(bf16)

    return grad_call(kernel, me, xs, ys, (m, half), pairs, [pltpu.VMEM((m, tokens), bf16)])


def grad_adapter(me, x, grads, dp):
    seqs, (rows, width) = len(grads), grads[0].shape
    tokens, joined = x.shape
    wide = joined // dp
    part = wide // 4

    def kernel(me_ref, x_ref, *refs):
        gs, (keep, send, wide_grad, grad, acc) = refs[:seqs], refs[seqs:]

        @pl.when(pl.program_id(0) == 0)
        def _():
            for c in range(width // 128):
                for s in range(seqs):
                    wide_grad[c, pl.ds(s, rows, stride=seqs), :] = gs[s][:, c * 128 : (c + 1) * 128].astype(f32)
            grad[...] = jnp.concatenate([wide_grad[c] for c in range(width // 128)], axis=1).astype(bf16)

        acc[...] = dot_tn(x_ref[...], grad[...])
        for far in (0, 1):
            for near, ref in ((0, keep), (1, send)):
                base = pl.multiple_of((me_ref[1] ^ (2 * far + near)) * part, part)
                ref[far, 0] = acc[pl.ds(base, part), :].astype(bf16)

    shape = jax.ShapeDtypeStruct((2, dp, part, width), bf16)
    spec = pl.BlockSpec((2, 1, part, width), lambda g, m: (0, g, 0, 0))
    return pl.pallas_call(
        kernel,
        out_shape=(shape, shape),
        grid_spec=pltpu.PrefetchScalarGridSpec(
            num_scalar_prefetch=1,
            grid=(dp,),
            in_specs=[pl.BlockSpec((tokens, wide), lambda g, m: (0, m[0] ^ g))]
            + [pl.BlockSpec((rows, width), lambda g, m: (0, 0)) for _ in grads],
            out_specs=(spec, spec),
            scratch_shapes=[
                pltpu.VMEM((width // 128, tokens, 128), f32),
                pltpu.VMEM((tokens, width), bf16),
                pltpu.VMEM((wide, width), f32),
            ],
        ),
        compiler_params=pltpu.CompilerParams(vmem_limit_bytes=32 * MIB),
        cost_estimate=LIGHT,
        name="grad_adapter",
    )(me, in_hbm(x), *grads)


def chip_sum(keep, send):
    return (keep.astype(f32) + swap(send, "tensor", 1).astype(f32)).astype(bf16)


def reduce_adapter(total, dp):
    _, _, part, width = total.shape
    bits = dp.bit_length() - 1
    total = total.reshape((2,) * (bits + 1) + (part, width))
    axes = [("tensor", 2)] + [("dp", 1 << b) for b in reversed(range(bits))]
    low = [("dp", 1 << b) for b in range(bits)]
    y = [("tensor", 2)]
    orders = [y + low, low[:1] + y + low[1:], low[1:2] + low[:1] + y + low[2:]]
    cut = [0, 384 * width // 1024, 768 * width // 1024, width]
    done = []
    for n, order in enumerate(orders):
        value, left = total[..., cut[n] : cut[n + 1]], list(axes)
        for step, (name, bit) in enumerate(order):
            at = left.index((name, bit))
            left.pop(at)
            got = swap(lax.index_in_dim(value, 1, at, keepdims=False), name, bit)
            value = lax.index_in_dim(value, 0, at, keepdims=False).astype(f32) + got.astype(f32)
            if step + 1 < len(order):
                value = value.astype(bf16)
        done.append(value)
    return jnp.concatenate(done, axis=-1)


class Halving:
    def __init__(self, keep, send):
        self.keep, self.send, self.bit = keep, send, 1
        self.launch()

    def launch(self):
        self.got = swap(self.send, "dp", self.bit)
        self.bit *= 2

    def step(self, order):
        total = after(self.keep, order).astype(f32) + self.got.astype(f32)
        if total.shape[0] == 1:
            self.result = total[0]
            return self.result
        total = total.astype(bf16)
        half = total.shape[0] // 2
        self.keep, self.send = total[:half], total[half:]
        self.launch()
        return self.keep


def body(adapter_in, lengths, cotangent, adapter_weight, gains, qkv_weight, out_weight, gate_up_weight, down_weight):
    rows, seqs = adapter_in.shape[0], adapter_in.shape[1]
    width = adapter_weight.shape[1]
    cols = qkv_weight.shape[2]
    heads = cols // HD
    units = down_weight.shape[0]
    members = lax.axis_size("tensor")
    dp = lax.axis_size("dp")
    seq_len = rows * members
    fast = (width // dp) % 128 == 0
    mine = lax.axis_index("tensor").astype(jnp.int32)
    me = lax.axis_index("dp").astype(jnp.int32).reshape(1)
    scal = jnp.concatenate([mine.reshape(1), lengths])

    lane = jnp.arange(HD, dtype=jnp.int32) % (HD // 2)
    freq = THETA ** (-(lane.astype(f32) * 2.0 / HD))
    inner = jnp.arange(rows, dtype=jnp.int32).astype(f32)[:, None] * freq[None, :]
    owner = (mine ^ jnp.arange(members, dtype=jnp.int32)) * rows
    outer = owner.astype(f32)[:, None] * freq[None, :]
    turn_rows = jnp.stack([jnp.cos(inner), jnp.sin(inner)])
    turn_blocks = jnp.stack([jnp.cos(outer), jnp.sin(outer)])

    every = range(seqs)
    x_in = adapter_in.reshape(rows * seqs, -1)
    tok = (rows, width)

    def parts(n):
        return [(tok, bf16)] * n

    gain = {}

    outs = whole_call(
        first_kernel,
        [(tok, f32)] * seqs + [(tok, bf16)] * seqs,
        [],
        [x_in, adapter_weight, gains],
        scratch=[pltpu.VMEM((width // 128, rows * seqs, 128), f32)],
        vmem=24,
        name="first",
    )
    latent, normed = outs[:seqs], outs[seqs:]
    w_qkv = qkv_weight.transpose(1, 0, 2)
    w_gu = gate_up_weight.transpose(1, 2, 0)
    early = after(cotangent, normed[0])
    cot = [early[:, s] for s in every]
    turn_rows, turn_blocks = after(turn_rows, normed[0]), after(turn_blocks, normed[0])

    def spread(block):
        return swap(block, "tensor", 2), swap(block, "tensor", 1)

    def relay(far, *order):
        far = after(far, *order)
        return far, swap(far, "tensor", 1)

    one = {s: [normed[s], *spread(normed[s])] for s in every}
    qkvo, att, across, addends = {}, {}, {}, {}
    head_shape = ((heads, seq_len, HD), bf16)
    tokn = normed[0]
    hop = (turn_rows, turn_blocks, *cot)
    for s in every:
        own, far, near = one[s]
        far, diag = relay(far, *hop)
        one[s] = [own, near, far, diag]
        *kept, at, p0, p1, p2, p3 = whole_call(
            functools.partial(attn_fwd_kernel, s),
            [head_shape] * 4 + [((8, seq_len), f32), ((members, rows, cols), bf16)] + parts(4),
            [scal],
            [after(own, tokn), near, far, diag, w_qkv, turn_rows, turn_blocks, out_weight],
            vmem=20,
            name="attn_fwd",
        )
        qkvo[s], att[s] = kept, at
        hop = (at,)
        across[s], addends[s] = scatter_blocks(p0, p1, p2, p3)
        tokn = across[s]

    hid_shape = ((2, rows, units), bf16)

    def ffn_fwd(x0, x1):
        return whole_call(
            mlp_fwd_kernel, [hid_shape] * 3 + parts(2), [], [x0, x1, w_gu, out_down], vmem=16, name="mlp_fwd"
        )

    out_down = down_weight
    mid, proj, three, first_half, ffn = {}, {}, {}, {}, {}
    for s in every:
        proj[s], mid[s], own = whole_call(
            mid_kernel,
            [(tok, f32), (tok, f32), (tok, bf16)],
            [],
            [after(latent[s], tokn), *addends[s], gains],
            vmem=8,
            name="mid",
        )
        far, near = spread(own)
        first_half[s] = ffn_fwd(own, near)
        tokn = first_half[s][0]
        three[s] = [own, near, far]
    for s in every:
        own, near, far = three[s]
        far, diag = relay(far, tokn if s == 0 else ffn[s - 1][1][0])
        three[s] = [own, near, far, diag]
        second = ffn_fwd(after(far, tokn), diag)
        ffn[s] = (first_half[s][:3], second[:3])
        across[s], addends[s] = scatter_blocks(*first_half[s][3:], *second[3:])
        tokn = across[s]

    def ffn_bwd(g0, g1, kept):
        return whole_call(
            mlp_bwd_kernel,
            [hid_shape] * 2 + parts(2),
            [],
            [g0, g1, down_weight, w_gu, kept[1], kept[2]],
            vmem=16,
            name="mlp_bwd",
        )

    block_out, mlp_g, gu_g = {}, {}, {}
    for s in every:
        block_out[s], own, gain[3, s] = whole_call(
            functools.partial(out_kernel, s),
            [(tok, bf16), (tok, bf16), ((1, width), f32)],
            [scal],
            [after(mid[s], tokn), *addends[s], cot[s], gains],
            vmem=10,
            name="out",
        )
        far, near = spread(own)
        first_half[s] = ffn_bwd(own, near, ffn[s][0])
        tokn = first_half[s][0]
        mlp_g[s] = [own, near, far]
    for s in every:
        own, near, far = mlp_g[s]
        far, diag = relay(far, tokn if s == 0 else gu_g[s - 1][1][0])
        mlp_g[s] = [own, near, far, diag]
        second = ffn_bwd(after(far, tokn), diag, ffn[s][1])
        gu_g[s] = (first_half[s][:2], second[:2])
        across[s], addends[s] = scatter_blocks(*first_half[s][2:], *second[2:])
        tokn = across[s]

    flat_three = [b for s in every for b in three[s]]
    flat_mlp = [b for s in every for b in mlp_g[s]]
    flat_one = [b for s in every for b in one[s]]
    gates = [gu_g[s][h][0] for s in every for h in (0, 1)]
    ups = [gu_g[s][h][1] for s in every for h in (0, 1)]
    hiddens = [ffn[s][h][0] for s in every for h in (0, 1)]
    sums = {}

    def reduced(name, keep, send):
        sums[name] = Halving(keep, send)
        return keep

    def slow(name, xs, ys, dim):
        xs, ys = [jnp.concatenate([a.reshape(-1, a.shape[-1]) for a in part], 0) for part in (xs, ys)]
        full = lax.dot_general(xs, ys, (((0,), (0,)), ((), ())), preferred_element_type=f32)
        sums[name] = lax.psum_scatter(full.astype(bf16), "dp", scatter_dimension=dim, tiled=True).astype(f32)
        return tokn

    def columns(name, xs, ys):
        if not fast:
            return slow(name, xs, ys, 1)
        return reduced(name, *grad_cols(me, xs, [after(ys[0], tokn), *ys[1:]], dp))

    def lines(name, xs, ys):
        if not fast:
            return slow(name, xs, ys, 0)
        return reduced(name, *grad_rows(me, [after(xs[0], tokn), *xs[1:]], ys, dp, cols))

    def step(name):
        return sums[name].step(tokn) if fast else tokn

    mid_grad, attn_g, stacked = {}, {}, {}
    for s in every:
        mid_grad[s], own, gain[1, s], gain[2, s] = whole_call(
            functools.partial(back_kernel, s),
            [(tok, f32), (tok, bf16), ((1, width), f32), ((1, width), f32)],
            [scal],
            [after(mid[s], tokn), proj[s], *addends[s], cot[s], gains],
            vmem=12,
            name="back",
        )
        attn_g[s] = [own, *spread(own)]
        tokn = mid_grad[s]
        if s == 0:
            tokn = columns("down", hiddens, flat_mlp)
        else:
            tokn = columns("gate", gates, flat_three)
    hop = tokn
    head_f32 = (heads, seq_len, HD)
    for s in every:
        own, far, near = attn_g[s]
        far, diag = relay(far, hop)
        attn_g[s] = [own, near, far, diag]
        stacked[s], p0, p1, p2, p3 = whole_call(
            functools.partial(attn_bwd_kernel, s),
            [((members, rows, 3 * cols), bf16)] + parts(4),
            [scal],
            [after(own, tokn), near, far, diag, out_weight, *qkvo[s], turn_rows, turn_blocks, w_qkv],
            scratch=[pltpu.VMEM(head_f32, bf16)] + [pltpu.VMEM(head_f32, f32)] * 3,
            vmem=24,
            name="attn_bwd",
        )
        hop = stacked[s]
        across[s], addends[s] = scatter_blocks(p0, p1, p2, p3)
        tokn = across[s]
        if s == 0:
            tokn = step("down")
    tokn = columns("up", ups, flat_three)
    tokn = step("gate")
    tokn = step("down")
    flat_attn = [b for s in every for b in attn_g[s]]
    latent_grad = {}
    for s in every:
        latent_grad[s], gain[0, s] = whole_call(
            last_kernel,
            [(tok, bf16), ((1, width), f32)],
            [],
            [after(latent[s], tokn), *addends[s], mid_grad[s], gains],
            vmem=10,
            name="last",
        )
        tokn = latent_grad[s]
        if s == 0:
            tokn = lines("qkv", flat_one, [stacked[i] for i in every])
            tokn = columns("out", [att[i] for i in every], flat_attn)
            tokn = step("up")
            tokn = step("gate")
            tokn = step("down")

    grads = [latent_grad[s] for s in every]
    if fast:
        keep, send = grad_adapter(jnp.concatenate([me, mine.reshape(1)]), x_in, grads, dp)
        tokn = late = chip_sum(keep, send)
        d_adapt = reduce_adapter(late, dp)
        for name in ("qkv", "out", "up", "gate", "qkv", "out", "up", "qkv", "out"):
            tokn = step(name)
        sums = {name: sums[name].result for name in sums}
    else:
        lhs = x_in.reshape(rows, seqs, -1).transpose(1, 0, 2).reshape(rows * seqs, -1)
        full = lax.dot_general(
            lhs, jnp.concatenate(grads, axis=0), (((0,), (0,)), ((), ())), preferred_element_type=f32
        )
        d_adapt = lax.psum_scatter(full, ("dp", "tensor"), scatter_dimension=0, tiled=True)
        late = grads[-1]
        sums["qkv"] = sums["qkv"].reshape(-1, 3, cols).transpose(1, 0, 2)
    d_gains = jnp.concatenate([sum(gain[g, s] for s in every) for g in range(4)], axis=0)
    d_gains = after(d_gains, late)
    for name, size in (("tensor", members), ("dp", dp)):
        bit = 1
        while bit < size:
            d_gains = d_gains + swap(d_gains, name, bit)
            bit *= 2
    share = width // (dp * members)
    d_gains = lax.dynamic_slice_in_dim(d_gains, (me[0] * members + mine) * share, share, 1)
    grad_in = jnp.stack(
        [
            lax.dot_general(after(g, late), adapter_weight, (((1,), (1,)), ((), ())), preferred_element_type=f32).astype(bf16)
            for g in grads
        ],
        axis=1,
    )
    out = jnp.stack([block_out[s] for s in every], axis=1)
    d_gate_up = jnp.stack([sums["gate"], sums["up"]]).transpose(2, 0, 1)
    d_qkv = sums["qkv"].transpose(1, 0, 2)
    return (out, grad_in, d_adapt, d_gains, d_qkv, sums["out"], d_gate_up, sums["down"])


def solution(mesh):
    return jax.shard_map(
        body,
        mesh=mesh,
        in_specs=(
            P("tensor", "dp", None),
            P("dp"),
            P("tensor", "dp", None),
            P(),
            P(),
            P(None, None, "tensor"),
            P("tensor", None),
            P(None, None, "tensor"),
            P("tensor", None),
        ),
        out_specs=(
            P("tensor", "dp", None),
            P("tensor", "dp", None),
            P(("dp", "tensor"), None),
            P(None, ("dp", "tensor")),
            P("dp", None, "tensor"),
            P("tensor", "dp"),
            P("dp", None, "tensor"),
            P("tensor", "dp"),
        ),
        check_vma=False,
    )
```

```python
import functools

import jax
import jax.numpy as jnp
import numpy as np
from jax import lax
from jax.experimental import pallas as pl
from jax.experimental.pallas import tpu as pltpu
from jax.sharding import PartitionSpec as P

HD = 128
LOG2E = 1.4426950408889634
EPS = 1e-06
THETA = 50000.0
MASKED = -1e30
f32 = jnp.float32
bf16 = jnp.bfloat16
MIB = 1024 * 1024
LIGHT = pl.CostEstimate(flops=1, bytes_accessed=1, transcendentals=0)


def dot(a, b):
    return jnp.dot(a, b, preferred_element_type=f32)


def dot_nt(a, b):
    return lax.dot_general(a, b, (((1,), (1,)), ((), ())), preferred_element_type=f32)


def dot_tn(a, b):
    return lax.dot_general(a, b, (((0,), (0,)), ((), ())), preferred_element_type=f32)


def full_map(rank):
    return lambda *_: (0,) * rank


def whole_call(kernel, outs, scalars, arrays, scratch=(), vmem=40, name=None):
    smem = pl.BlockSpec(memory_space=pltpu.SMEM)
    vm = pl.BlockSpec(memory_space=pltpu.VMEM)
    return pl.pallas_call(
        kernel,
        out_shape=tuple(pltpu.HBM(o[0], o[1]) if len(o) > 2 else jax.ShapeDtypeStruct(*o) for o in outs),
        in_specs=[smem] * len(scalars) + [vm] * len(arrays),
        out_specs=tuple(pl.BlockSpec(o[0], full_map(len(o[0]))) if len(o) > 2 else vm for o in outs),
        scratch_shapes=list(scratch),
        compiler_params=pltpu.CompilerParams(vmem_limit_bytes=vmem * MIB),
        cost_estimate=LIGHT,
        name=name,
    )(*scalars, *arrays)


def swap(x, axis, bit):
    n = lax.axis_size(axis)
    return lax.ppermute(x, axis, [(i, i ^ bit) for i in range(n)])


def gather_blocks(x):
    far = swap(x, "tensor", 2)
    near = swap(x, "tensor", 1)
    return [x, near, far, swap(far, "tensor", 1)]


def scatter_blocks(p0, p1, p2, p3):
    near = swap(p1, "tensor", 1)
    across = (p2.astype(f32) + swap(p3, "tensor", 1).astype(f32)).astype(bf16)
    return across, (p0, near, swap(across, "tensor", 2))


def in_hbm(x):
    return pltpu.with_memory_space_constraint(x, pltpu.HBM)


def after(x, *others):
    return lax.optimization_barrier((x,) + others)[0]


def turn_tables(turn_rows, turn_blocks, j):
    cr, sr = turn_rows[0], turn_rows[1]
    cb, sb = turn_blocks[0, j : j + 1, :], turn_blocks[1, j : j + 1, :]
    sign = jnp.where(lax.broadcasted_iota(jnp.int32, (1, HD), 1) < HD // 2, -1.0, 1.0)
    return cb * cr - sb * sr, (sb * cr + cb * sr) * sign


def attn_fwd_kernel(seq, scal, x0, x1, x2, x3, w, turn_rows, turn_blocks, wo, q, k, v, o, lse, att, *parts):
    mine, length = scal[0], scal[1 + seq]
    rows = x0.shape[0]
    heads = q.shape[0]
    for j, x in enumerate((x0, x1, x2, x3)):
        base = pl.multiple_of((mine ^ j) * rows, rows)
        c, s = turn_tables(turn_rows, turn_blocks, j)
        for n, ref in ((0, q), (1, k)):
            acc = dot(x[...], w[n])
            for h in range(heads):
                part = acc[:, h * HD : (h + 1) * HD]
                turned = part * c + pltpu.roll(part, HD // 2, 1) * s
                ref[h, pl.ds(base, rows), :] = turned.astype(bf16)
        acc = dot(x[...], w[2]).astype(bf16)
        for h in range(heads):
            v[h, pl.ds(base, rows), :] = acc[:, h * HD : (h + 1) * HD]
    factor = HD**-0.5 * LOG2E
    for h in range(heads):
        vt = v[h].T
        for i in range(4):
            keys = (i + 1) * rows
            st = dot_nt(k[h, :keys, :], q[h, i * rows : keys, :]) * factor
            key_id = lax.broadcasted_iota(jnp.int32, st.shape, 0)
            row_id = lax.broadcasted_iota(jnp.int32, st.shape, 1) + i * rows
            st = jnp.where((key_id <= row_id) & (key_id < length), st, MASKED)
            top = jnp.max(st, axis=0, keepdims=True)
            weights = jnp.exp2(st - top)
            total = jnp.sum(weights, axis=0, keepdims=True)
            ot = dot(vt[:, :keys], weights.astype(bf16)) / total
            o[h, i * rows : keys, :] = ot.T.astype(bf16)
            lse[h : h + 1, i * rows : keys] = top + jnp.log2(total)
    for j in range(4):
        base = pl.multiple_of((mine ^ j) * rows, rows)
        both = jnp.concatenate([o[h, pl.ds(base, rows), :] for h in range(heads)], axis=1)
        att[j] = both
        parts[j][...] = dot(both, wo[...]).astype(bf16)


def attn_bwd_kernel(
    seq, scal, g0, g1, g2, g3, wo, q, k, v, o, lse, turn_rows, turn_blocks, w, st_out, p0, p1, p2, p3, dout, dq, dk, dv
):
    parts = (p0, p1, p2, p3)
    mine, length = scal[0], scal[1 + seq]
    rows = g0.shape[0]
    heads = q.shape[0]
    cols = heads * HD
    for j, g in enumerate((g0, g1, g2, g3)):
        mixed = dot_nt(g[...], wo[...]).astype(bf16)
        base = pl.multiple_of((mine ^ j) * rows, rows)
        for h in range(heads):
            dout[h, pl.ds(base, rows), :] = mixed[:, h * HD : (h + 1) * HD]
    scale = HD**-0.5
    factor = scale * LOG2E
    ones = jnp.ones((8, HD), f32)
    for h in range(heads):
        for i in (3, 2, 1, 0):
            keys = (i + 1) * rows
            here = slice(i * rows, keys)
            qi, di = q[h, here, :], dout[h, here, :]
            st = dot_nt(k[h, :keys, :], qi) * factor
            key_id = lax.broadcasted_iota(jnp.int32, st.shape, 0)
            row_id = lax.broadcasted_iota(jnp.int32, st.shape, 1) + i * rows
            st = jnp.where((key_id <= row_id) & (key_id < length), st, MASKED)
            probs = jnp.exp2(st - lse[h : h + 1, here])
            prob_grad = dot_nt(v[h, :keys, :], di)
            product = di.astype(f32) * o[h, here, :].astype(f32)
            inner = lax.dot_general(
                ones, product, (((1,), (1,)), ((), ())), precision=lax.Precision.HIGHEST, preferred_element_type=f32
            )[0:1, :]
            sg = (probs * (prob_grad - inner)).astype(bf16)
            new_v = dot(probs.astype(bf16), di)
            new_k = dot(sg, qi)
            if i == 3:
                dv[h] = new_v
                dk[h] = new_k
            else:
                dv[h, :keys, :] += new_v
                dk[h, :keys, :] += new_k
            dq[h, here, :] = dot_tn(sg, k[h, :keys, :])
    for j in range(4):
        base = pl.multiple_of((mine ^ j) * rows, rows)
        c, s = turn_tables(turn_rows, turn_blocks, j)
        c, s = c * scale, s * scale
        total = None
        for n, ref in enumerate((dq, dk, dv)):
            pieces = []
            for h in range(heads):
                part = ref[h, pl.ds(base, rows), :]
                if n < 2:
                    part = part * c - pltpu.roll(part, HD // 2, 1) * s
                pieces.append(part.astype(bf16))
            piece = jnp.concatenate(pieces, axis=1)
            st_out[j, :, n * cols : (n + 1) * cols] = piece
            add = dot_nt(piece, w[n])
            total = add if total is None else total + add
        parts[j][...] = total.astype(bf16)


def mlp_fwd_kernel(x0, x1, wgu0, wgu1, wd0, wd1, *outs):
    kept, parts = outs[:6], outs[6:]
    rows = x0.shape[0]
    x = jnp.concatenate([x0[...], x1[...]], axis=0)
    total = None
    for n, (wgu, wd) in enumerate(((wgu0, wd0), (wgu1, wd1))):
        hid, fa, fb = kept[3 * n : 3 * n + 3]
        gate = dot_nt(x, wgu[0])
        up = dot_nt(x, wgu[1])
        sig = jax.nn.sigmoid(gate)
        act = gate * sig
        hidden = (act * up).astype(bf16)
        a = act.astype(bf16)
        b = (up * sig * (1.0 + gate * (1.0 - sig))).astype(bf16)
        for j in range(2):
            here = slice(j * rows, (j + 1) * rows)
            hid[j], fa[j], fb[j] = hidden[here], a[here], b[here]
        add = dot(hidden, wd[...])
        total = add if total is None else total + add
    for j in range(2):
        parts[j][...] = total[j * rows : (j + 1) * rows].astype(bf16)


def mlp_bwd_kernel(g0, g1, wgu0, wgu1, wd0, wd1, fa0, fb0, fa1, fb1, gg0, gu0, gg1, gu1, *parts):
    rows = g0.shape[0]
    g = jnp.concatenate([g0[...], g1[...]], axis=0)
    total = None
    for wgu, wd, fa, fb, gg, gu in ((wgu0, wd0, fa0, fb0, gg0, gu0), (wgu1, wd1, fa1, fb1, gg1, gu1)):
        hidden_grad = dot_nt(g, wd[...])
        a = jnp.concatenate([fa[0], fa[1]], axis=0).astype(f32)
        b = jnp.concatenate([fb[0], fb[1]], axis=0).astype(f32)
        gate_grad = (hidden_grad * b).astype(bf16)
        up_grad = (hidden_grad * a).astype(bf16)
        for j in range(2):
            here = slice(j * rows, (j + 1) * rows)
            gg[j], gu[j] = gate_grad[here], up_grad[here]
        add = dot(gate_grad, wgu[0]) + dot(up_grad, wgu[1])
        total = add if total is None else total + add
    for j in range(2):
        parts[j][...] = total[j * rows : (j + 1) * rows].astype(bf16)


def factor_of(v):
    return lax.rsqrt(jnp.mean(v * v, axis=-1, keepdims=True) + EPS)


def norm_back(v, r, gain, e):
    scaled = e * gain
    inner = jnp.mean(scaled * v, axis=-1, keepdims=True)
    grad = r * (scaled - v * (r * r * inner))
    return grad, jnp.sum(e * v * r, axis=0, keepdims=True)


def summed(*addends):
    total = addends[0][...].astype(f32)
    for a in addends[1:]:
        total = total + a[...].astype(f32)
    return total


def mid_kernel(latent, p0, near, far, gains, proj_out, mid_out, normed_out):
    proj = summed(p0, near, far)
    mid = latent[...] + proj * factor_of(proj) * gains[1:2, :]
    proj_out[...] = proj
    mid_out[...] = mid
    normed_out[...] = (mid * factor_of(mid) * gains[2:3, :]).astype(bf16)


def live_grad(seq, scal, cot):
    rows = cot.shape[0]
    row_id = lax.broadcasted_iota(jnp.int32, (rows, 1), 0) + scal[0] * rows
    return jnp.where(row_id < scal[1 + seq], cot[...].astype(f32), 0.0)


def out_kernel(seq, scal, mid, p0, near, cot, gains, out, grad_out, gain_out):
    proj = summed(p0, near)
    r = factor_of(proj)
    gain = gains[3:4, :]
    out[...] = (mid[...] + proj * r * gain).astype(bf16)
    grad, gain_grad = norm_back(proj, r, gain, live_grad(seq, scal, cot))
    grad_out[...] = grad.astype(bf16)
    gain_out[...] = gain_grad


def back_kernel(seq, scal, mid, proj, p0, near, cot, gains, mid_grad_out, grad_out, gain_two, gain_three):
    three = summed(p0, near)
    m = mid[...]
    part, g3 = norm_back(m, factor_of(m), gains[2:3, :], three)
    mid_grad = live_grad(seq, scal, cot) + part
    pr = proj[...]
    grad, g2 = norm_back(pr, factor_of(pr), gains[1:2, :], mid_grad)
    mid_grad_out[...] = mid_grad
    grad_out[...] = grad.astype(bf16)
    gain_two[...] = g2
    gain_three[...] = g3


def last_kernel(latent, p0, near, far, mid_grad, gains, grad_out, gain_out):
    one = summed(p0, near, far)
    la = latent[...]
    part, g1 = norm_back(la, factor_of(la), gains[0:1, :], one)
    grad_out[...] = (mid_grad[...] + part).astype(bf16)
    gain_out[...] = g1


def first_kernel(x, w, gains, *refs):
    outs, acc = refs[:-1], refs[-1]
    seqs = len(outs) // 2
    whole = dot(x[...], w[...])
    rows, tiles = acc.shape[1] // seqs, acc.shape[0]
    for c in range(tiles):
        acc[c] = whole[:, c * 128 : (c + 1) * 128]
    for s in range(seqs):
        latent = jnp.concatenate([acc[c, pl.ds(s, rows, stride=seqs), :] for c in range(tiles)], axis=1)
        outs[s][...] = latent
        outs[seqs + s][...] = (latent * factor_of(latent) * gains[0:1, :]).astype(bf16)


def reversed_bits(index, bits):
    out = 0
    for b in range(bits):
        out = out + (((index >> b) & 1) << (bits - 1 - b))
    return out


def pair_block(g, me, pairs):
    return (me[0] >> 1) ^ reversed_bits(g, pairs.bit_length() - 1)


def grad_call(kernel, me, fixed, sliced, out, pairs, scratch=()):
    rows, d = sliced[0].shape
    wide = d // pairs
    shape = jax.ShapeDtypeStruct((pairs,) + out, bf16)
    spec = pl.BlockSpec((1,) + out, lambda g, m: (g,) + (0,) * len(out))

    def full_map(a):
        return lambda g, m: (0,) * a.ndim

    return pl.pallas_call(
        kernel,
        out_shape=(shape, shape),
        grid_spec=pltpu.PrefetchScalarGridSpec(
            num_scalar_prefetch=1,
            grid=(pairs,),
            in_specs=[pl.BlockSpec(a.shape, full_map(a)) for a in fixed]
            + [pl.BlockSpec((rows, wide), lambda g, m: (0, pair_block(g, m, pairs))) for _ in sliced],
            out_specs=(spec, spec),
            scratch_shapes=list(scratch),
        ),
        compiler_params=pltpu.CompilerParams(vmem_limit_bytes=24 * MIB),
        cost_estimate=LIGHT,
        name="weight_grad",
    )(me, *[in_hbm(a) for a in fixed], *[in_hbm(a) for a in sliced])


def grad_rows(me, groups, dp, cols):
    pairs = dp // 2
    half = groups[0][0][0].shape[1] // dp
    fixed = [y for _, ys in groups for y in ys]
    sliced = [x for xs, _ in groups for x in xs]
    count = sum(ys[0].shape[-1] // cols for _, ys in groups)

    def kernel(me_ref, *refs):
        yr, xr, (keep, send) = refs[: len(fixed)], refs[len(fixed) : -2], refs[-2:]
        odd = (me_ref[0] & 1) == 1
        n = y0 = x0 = 0
        for xs, ys in groups:
            lhs = jnp.concatenate([x[...] for x in xr[x0 : x0 + len(xs)]], axis=0)
            rhs = jnp.concatenate([y[b] for y in yr[y0 : y0 + len(ys)] for b in range(y.shape[0])], axis=0)
            x0, y0 = x0 + len(xs), y0 + len(ys)
            acc = dot_tn(lhs, rhs)
            stay = jnp.where(odd, acc[half:], acc[:half]).astype(bf16)
            go = jnp.where(odd, acc[:half], acc[half:]).astype(bf16)
            for c in range(0, acc.shape[1], cols):
                keep[0, n] = stay[:, c : c + cols]
                send[0, n] = go[:, c : c + cols]
                n += 1

    return grad_call(kernel, me, fixed, sliced, (count, half, cols), pairs)


def grad_units(me, sets, ys, dp, first):
    rows, d = ys[0].shape
    pairs = dp // 2
    wide = d // pairs
    half = wide // 2
    units = sets[0][0].shape[-1]
    quarter = units // 4
    tokens = len(ys) * rows
    count = len(sets[0])
    inner = pairs // 2

    def kernel(me_ref, *refs):
        xr, yr = refs[: 2 * count], refs[2 * count : 2 * count + len(ys)]
        keep, send0, send1, turned = refs[2 * count + len(ys) :]
        sends = (send0, send1)
        step = pl.program_id(0)

        @pl.when(step == 0)
        def _():
            for n in range(2):
                block = jnp.concatenate([x[b] for x in xr[n * count : (n + 1) * count] for b in range(x.shape[0])], axis=0).T
                if n == 0:
                    turned[:units, :] = block
                else:
                    for r in range(4):
                        base = pl.multiple_of(units + ((me_ref[0] & 3) ^ r) * quarter, quarter)
                        turned[pl.ds(base, quarter), :] = block[r * quarter : (r + 1) * quarter]

        acc = dot(turned[...], jnp.concatenate([y[...] for y in yr], axis=0))
        odd = (me_ref[0] & 1) == 1
        same = jnp.where(odd, acc[:, half:], acc[:, :half]).astype(bf16)
        other = jnp.where(odd, acc[:, :half], acc[:, half:]).astype(bf16)
        if first == "y":
            for x, part in ((0, same), (1, other)):
                keep[x, 0] = part[:units]
                sends[x][0] = part[units:]
        elif first == "x":
            for n in range(2):
                keep[0, n, 0] = same[n * units : (n + 1) * units]
            for ref, when in ((send0, step < inner), (send1, step >= inner)):

                @pl.when(when)
                def _():
                    for n in range(2):
                        ref[n, 0] = other[n * units : (n + 1) * units]
        else:

            @pl.when(step < inner)
            def _():
                for n in range(2):
                    keep[n, 0, 0] = same[n * units : (n + 1) * units]
                    keep[n, 1, 0] = other[n * units : (n + 1) * units]

            @pl.when(step >= inner)
            def _():
                for n in range(2):
                    sends[n][0, 0] = same[n * units : (n + 1) * units]
                    sends[n][1, 0] = other[n * units : (n + 1) * units]

    def early(g):
        return jnp.minimum(g, inner - 1)

    def late(g):
        return jnp.maximum(g - inner, 0)

    if first == "y":
        outs = [((2, pairs), (2, 1), lambda g, m: (0, g, 0, 0))] + [((pairs,), (1,), lambda g, m: (g, 0, 0))] * 2
    elif first == "x":
        outs = [
            ((2, 2, inner), (1, 2, 1), lambda g, m: (g // inner, 0, g % inner, 0, 0)),
            ((2, inner), (2, 1), lambda g, m: (0, early(g), 0, 0)),
            ((2, inner), (2, 1), lambda g, m: (0, late(g), 0, 0)),
        ]
    else:
        outs = [((2, 2, inner), (2, 2, 1), lambda g, m: (0, 0, early(g), 0, 0))] + [
            ((2, inner), (2, 1), lambda g, m: (0, late(g), 0, 0))
        ] * 2
    fixed = [a for one_set in sets for a in one_set]
    return pl.pallas_call(
        kernel,
        out_shape=tuple(jax.ShapeDtypeStruct(shape + (units, half), bf16) for shape, _, _ in outs),
        grid_spec=pltpu.PrefetchScalarGridSpec(
            num_scalar_prefetch=1,
            grid=(pairs,),
            in_specs=[pl.BlockSpec(a.shape, lambda g, m: (0, 0, 0)) for a in fixed]
            + [pl.BlockSpec((rows, wide), lambda g, m: (0, pair_block(g, m, pairs))) for _ in ys],
            out_specs=tuple(pl.BlockSpec(block + (units, half), f) for _, block, f in outs),
            scratch_shapes=[pltpu.VMEM((2 * units, tokens), bf16)],
        ),
        compiler_params=pltpu.CompilerParams(vmem_limit_bytes=28 * MIB),
        cost_estimate=LIGHT,
        name="grad_units",
    )(me, *[in_hbm(a) for a in fixed], *[in_hbm(a) for a in ys])


def grad_adapter(me, x, grad, dp):
    tokens, joined = x.shape
    width = grad.shape[1]
    wide = joined // dp
    part = wide // 4

    def kernel(me_ref, x_ref, g_ref, keep, send0, send1, acc):
        acc[...] = dot_tn(x_ref[...], g_ref[...])
        for far in (0, 1):
            for near in (0, 1):
                base = pl.multiple_of((me_ref[1] ^ (2 * far + near)) * part, part)
                piece = acc[pl.ds(base, part), :].astype(bf16)
                if near == 0:
                    keep[far, 0] = piece
                else:
                    (send0, send1)[far][0] = piece

    def shape(*lead):
        return jax.ShapeDtypeStruct(lead + (part, width), bf16)

    one = pl.BlockSpec((1, part, width), lambda g, m: (g, 0, 0))
    return pl.pallas_call(
        kernel,
        out_shape=(shape(2, dp), shape(dp), shape(dp)),
        grid_spec=pltpu.PrefetchScalarGridSpec(
            num_scalar_prefetch=1,
            grid=(dp,),
            in_specs=[
                pl.BlockSpec((tokens, wide), lambda g, m: (0, m[0] ^ g)),
                pl.BlockSpec((tokens, width), lambda g, m: (0, 0)),
            ],
            out_specs=(pl.BlockSpec((2, 1, part, width), lambda g, m: (0, g, 0, 0)), one, one),
            scratch_shapes=[pltpu.VMEM((wide, width), f32)],
        ),
        compiler_params=pltpu.CompilerParams(vmem_limit_bytes=20 * MIB),
        cost_estimate=LIGHT,
        name="grad_adapter",
    )(me, in_hbm(x), grad)


def plus(a, *others):
    total = a.astype(f32)
    for o in others:
        total = total + o.astype(f32)
    return total


def low(a, *others):
    return plus(a, *others).astype(bf16)


def body(adapter_in, lengths, cotangent, adapter_weight, gains, qkv_weight, out_weight, gate_up_weight, down_weight):
    rows, seqs = adapter_in.shape[0], adapter_in.shape[1]
    width = adapter_weight.shape[1]
    cols = qkv_weight.shape[2]
    heads = cols // HD
    units = down_weight.shape[0]
    members = lax.axis_size("tensor")
    dp = lax.axis_size("dp")
    seq_len = rows * members
    fast = dp == 8 and (width // dp) % 128 == 0
    mine = lax.axis_index("tensor").astype(jnp.int32)
    me = lax.axis_index("dp").astype(jnp.int32).reshape(1)
    scal = jnp.concatenate([mine.reshape(1), lengths])

    lane = jnp.arange(HD, dtype=jnp.int32) % (HD // 2)
    freq = THETA ** (-(lane.astype(f32) * 2.0 / HD))
    inner = jnp.arange(rows, dtype=jnp.int32).astype(f32)[:, None] * freq[None, :]
    owner = (mine ^ jnp.arange(members, dtype=jnp.int32)) * rows
    outer = owner.astype(f32)[:, None] * freq[None, :]
    turn_rows = jnp.stack([jnp.cos(inner), jnp.sin(inner)])
    turn_blocks = jnp.stack([jnp.cos(outer), jnp.sin(outer)])

    every = range(seqs)
    x_in = adapter_in.reshape(rows * seqs, -1)
    x_first = x_in
    tok = (rows, width)

    def parts(n):
        return [(tok, bf16)] * n

    gain = {}

    clock = [None]

    def gate(x):
        return x if clock[0] is None else after(x, clock[0])

    def close(*values):
        values = lax.optimization_barrier(tuple(values))
        clock[0] = values[0]
        return values

    moves = {"c": ("tensor", 1), "y": ("tensor", 2), "x": ("dp", 1), "z": ("dp", 2), "w": ("dp", 4)}

    def go(x, m):
        return swap(gate(x), *moves[m])

    def hop(x):
        return swap(x, "tensor", 1)

    place = me[0] & 3
    w_gu = gate_up_weight.transpose(1, 2, 0)
    w_qkv = qkv_weight.transpose(1, 0, 2)
    quarter = units // 4
    gu0 = swap(lax.dynamic_slice_in_dim(w_gu, place * quarter, quarter, 1), "tensor", 2)
    latent_a, latent_b, normed_a, normed_b = whole_call(
        first_kernel,
        [(tok, f32, True)] * seqs + [(tok, bf16)] * seqs,
        [],
        [in_hbm(x_in), in_hbm(adapter_weight), gains],
        scratch=[pltpu.VMEM((width // 128, rows * seqs, 128), f32)],
        vmem=24,
        name="first",
    )
    latent = [latent_a, latent_b]
    normed_a, normed_b, gu0, turn_rows, turn_blocks = close(normed_a, normed_b, gu0, turn_rows, turn_blocks)

    far_a, near_a = go(normed_a, "y"), go(normed_a, "c")
    d0 = go(lax.dynamic_slice_in_dim(down_weight, place * quarter, quarter, 0), "y")
    gu1, gu2 = go(gu0, "x"), go(gu0, "z")
    early = gate(cotangent)
    cot = [early[:, s] for s in every]
    far_a, near_a, d0, gu1, gu2, cot_a, cot_b = close(far_a, near_a, d0, gu1, gu2, *cot)
    cot = [cot_a, cot_b]

    head_shape = ((heads, seq_len, HD), bf16, True)

    def attn_fwd(s, blocks):
        *kept, at, p0, p1, p2, p3 = whole_call(
            functools.partial(attn_fwd_kernel, s),
            [head_shape] * 4 + [((8, seq_len), f32, True), ((members, rows, cols), bf16, True)] + parts(4),
            [scal],
            [*blocks, w_qkv, turn_rows, turn_blocks, out_weight],
            vmem=20,
            name="attn_fwd",
        )
        return kept, at, p0, p1, p2, p3

    far_b, near_b = go(normed_b, "y"), go(normed_b, "c")
    gu3, d2 = go(gu2, "x"), go(d0, "z")
    one = {0: [normed_a, near_a, far_a, hop(far_a)]}
    qkvo, att = {}, {}
    qkvo[0], att[0], *sums = attn_fwd(0, one[0])
    p0, p1, p2, p3, far_b, near_b, gu3, d2 = close(*sums, far_b, near_b, gu3, d2)
    across_a, near_a = low(p2, hop(p3)), hop(p1)
    across_a, near_a, own_a = close(across_a, near_a, p0)

    far_a, d1 = go(across_a, "y"), go(d0, "x")
    one[1] = [gate(normed_b), near_b, far_b, hop(far_b)]
    qkvo[1], att[1], *sums = attn_fwd(1, one[1])
    p0, p1, p2, p3, far_a, d1 = close(*sums, far_a, d1)
    across_b, near_b = low(p2, hop(p3)), hop(p1)
    across_b, near_b, own_b = close(across_b, near_b, p0)

    far_b, d3 = go(across_b, "y"), go(d1, "z")
    far_gu = jnp.concatenate([gate(gu0), gu1, gu2, gu3], axis=1)

    def mid_of(s, *addends):
        return whole_call(
            mid_kernel,
            [(tok, f32, True), (tok, f32, True), (tok, bf16)],
            [],
            [gate(latent[s]), *addends, gains],
            vmem=8,
            name="mid",
        )

    proj, mid, three, ffn, block_out, mlp_g, gu_g = {}, {}, {}, {}, {}, {}, {}
    proj[0], mid[0], own = mid_of(0, own_a, near_a, far_a)
    three[0] = [own, hop(own)]
    far_b, d3, far_gu, t0, t1 = close(far_b, d3, far_gu, *three[0])
    three[0] = [t0, t1]

    far_d = jnp.concatenate([gate(d0), d1, d2, d3], axis=0)
    mlp_weights = [w_gu, far_gu, down_weight, far_d]
    hid_shape = ((2, rows, units), bf16, True)

    def ffn_fwd(s):
        *ffn[s], p0, p1 = whole_call(
            mlp_fwd_kernel, [hid_shape] * 6 + parts(2), [], [*three[s], *mlp_weights], vmem=36, name="mlp_fwd"
        )
        return p0, hop(p1)

    def out_of(s, *addends):
        block_out[s], own, gain[3, s] = whole_call(
            functools.partial(out_kernel, s),
            [(tok, bf16, True), (tok, bf16), ((1, width), f32)],
            [scal],
            [mid[s], *addends, cot[s], gains],
            vmem=10,
            name="out",
        )
        mlp_g[s] = [own, hop(own)]

    def ffn_bwd(s):
        *gu_g[s], p0, p1 = whole_call(
            mlp_bwd_kernel,
            [hid_shape] * 4 + parts(2),
            [],
            [*mlp_g[s], *mlp_weights, *ffn[s][1:3], *ffn[s][4:6]],
            vmem=36,
            name="mlp_bwd",
        )
        return p0, p1

    mid_grad, attn_g, stacked = {}, {}, {}

    def back_of(s, *addends):
        mid_grad[s], own, gain[1, s], gain[2, s] = whole_call(
            functools.partial(back_kernel, s),
            [(tok, f32, True), (tok, bf16), ((1, width), f32), ((1, width), f32)],
            [scal],
            [mid[s], proj[s], *addends, cot[s], gains],
            vmem=12,
            name="back",
        )
        return own

    sum_a = ffn_fwd(0)
    proj[1], mid[1], own = mid_of(1, own_b, near_b, far_b)
    three[1] = [own, hop(own)]
    out_of(0, *sum_a)
    sum_b = ffn_fwd(1)
    p0, p1 = ffn_bwd(0)
    sum_a = p0, hop(p1)
    out_of(1, *sum_b)
    grad_a = back_of(0, *sum_a)
    grad_a, b0, b1 = close(grad_a, *mlp_g[1])
    mlp_g[1] = [b0, b1]

    def full_grad(xs, ys):
        xs, ys = [jnp.concatenate([a.reshape(-1, a.shape[-1]) for a in part], 0) for part in (xs, ys)]
        return lax.dot_general(xs, ys, (((0,), (0,)), ((), ())), preferred_element_type=f32).astype(bf16)

    def unit_grad(sets, ys, first):
        ys = [gate(ys[0]), *ys[1:]]
        if fast:
            keep, send0, send1 = grad_units(me, sets, ys, dp, first)
            split = (2, 2) + keep.shape[-2:]
            return keep.reshape((2,) + split), send0.reshape(split), send1.reshape(split)
        own, far = [full_grad(xs, ys) for xs in sets]
        far = jnp.concatenate([lax.dynamic_slice_in_dim(far, (place ^ a) * quarter, quarter, 0) for a in range(4)], axis=0)
        total = low(own, swap(far, "tensor", 2))
        return lax.psum_scatter(total, "dp", scatter_dimension=1, tiled=True).astype(f32)

    far_a, near_a = go(grad_a, "y"), go(grad_a, "c")
    sum_b = ffn_bwd(1)
    flat_three = [b for s in every for b in three[s]]
    flat_mlp = [b for s in every for b in mlp_g[s]]
    flat_one = [b for s in every for b in one[s]]
    hiddens = [[ffn[s][3 * n] for s in every] for n in (0, 1)]
    gates = [[gu_g[s][2 * n] for s in every] for n in (0, 1)]
    ups = [[gu_g[s][2 * n + 1] for s in every] for n in (0, 1)]

    if fast:
        down_keep, down0, down1 = unit_grad(hiddens, flat_mlp, "z")
        p0, p1, far_a, near_a, down0, down1 = close(*sum_b, far_a, near_a, down0, down1)
    else:
        p0, p1, far_a, near_a = close(*sum_b, far_a, near_a)
    grad_b = close(back_of(1, p0, hop(p1)))[0]


    head_f32 = (heads, seq_len, HD)

    def attn_bwd(s, blocks):
        stacked[s], p0, p1, p2, p3 = whole_call(
            functools.partial(attn_bwd_kernel, s),
            [((members, rows, 3 * cols), bf16, True)] + parts(4),
            [scal],
            [*blocks, out_weight, *qkvo[s], turn_rows, turn_blocks, w_qkv],
            scratch=[pltpu.VMEM(head_f32, bf16)] + [pltpu.VMEM(head_f32, f32)] * 3,
            vmem=24,
            name="attn_bwd",
        )
        return p0, p1, p2, p3

    far_b, near_b = go(grad_b, "y"), go(grad_b, "c")
    attn_g[0] = [gate(grad_a), near_a, far_a, hop(far_a)]
    sums = attn_bwd(0, attn_g[0])
    if fast:
        down_got1 = go(down1, "z")
        gate_keep, gate0, gate1 = unit_grad(gates, flat_three, "x")
        p0, p1, p2, p3, far_b, near_b, gate0, gate1, down_got1 = close(*sums, far_b, near_b, gate0, gate1, down_got1)
    else:
        p0, p1, p2, p3, far_b, near_b = close(*sums, far_b, near_b)
    across_a, near_a = low(p2, hop(p3)), hop(p1)
    across_a, near_a, own_a = close(across_a, near_a, p0)

    far_a = go(across_a, "y")
    attn_g[1] = [gate(grad_b), near_b, far_b, hop(far_b)]
    sums = attn_bwd(1, attn_g[1])
    if fast:
        down_got0, gate_got1 = go(down0, "z"), go(gate1, "x")
        up_keep, up0, up1 = unit_grad(ups, flat_three, "y")
        p0, p1, p2, p3, far_a, down_got0, gate_got1, up0, up1 = close(*sums, far_a, down_got0, gate_got1, up0, up1)
    else:
        p0, p1, p2, p3, far_a = close(*sums, far_a)
    across_b, near_b = low(p2, hop(p3)), hop(p1)
    across_b, near_b, own_b = close(across_b, near_b, p0)

    latent_grad = {}

    def last_of(s, *addends):
        latent_grad[s], gain[0, s] = whole_call(
            last_kernel,
            [(tok, bf16), ((1, width), f32)],
            [],
            [gate(latent[s]), *addends, mid_grad[s], gains],
            vmem=10,
            name="last",
        )

    both_me = jnp.concatenate([me, mine.reshape(1)])
    tokens_of = adapter_in.transpose(1, 0, 2)

    far_b = go(across_b, "y")
    last_of(0, own_a, near_a, far_a)
    flat_attn = [b for s in every for b in attn_g[s]]
    if fast:
        gate_got0 = go(gate0, "x")
        gate_got2 = swap(low(gate(gate_keep[1]), gate_got1), *moves["z"])
        keep_a, send_a0, send_a1 = grad_adapter(both_me, tokens_of[0], latent_grad[0], dp)
        first = [gate(flat_one[0]), *flat_one[1:]]
        attn_keep, attn_send = grad_rows(
            me, [(first, [stacked[s] for s in every]), (flat_attn, [att[s] for s in every])], dp, cols
        )
        lead = (2, 2) + attn_keep.shape[1:]
        attn_keep, attn_send = attn_keep.reshape(lead), attn_send.reshape(lead)
        far_b, send_a0, send_a1, attn_send, gate_got0, gate_got2 = close(
            far_b, send_a0, send_a1, attn_send, gate_got0, gate_got2
        )
    else:
        far_b = close(far_b)[0]

    last_of(1, own_b, near_b, far_b)
    grads = [latent_grad[s] for s in every]
    d_gains = sum(jnp.concatenate([gain[g, s] for g in range(4)], axis=0) for s in every)
    if fast:
        up_got1, attn_got = go(up1, "y"), go(attn_send, "x")
        got_a0, got_a1 = go(send_a0, "c"), go(send_a1, "c")
        gate2 = low(low(gate(gate_keep[0]), gate_got0), gate_got2)
        gate_got3 = swap(gate2[1], *moves["y"])
        down_next = low(gate(down_keep[1]), down_got1)
        down_stay = low(gate(down_keep[0]), down_got0)
        keep_b, send_b0, send_b1 = grad_adapter(both_me, tokens_of[1], latent_grad[1], dp)
        send_b0, send_b1, up_got1, attn_got, got_a0, got_a1, gate_got3, d_gains, down_next = close(
            send_b0, send_b1, up_got1, attn_got, got_a0, got_a1, gate_got3, d_gains, down_next
        )
        got_b = jnp.stack([hop(send_b0), hop(send_b1)])
        total = low(keep_a, jnp.stack([got_a0, got_a1]), keep_b, got_b)
        total = close(total)[0]

        part = total.shape[-2]
        ranges = total.reshape(2, 2, 2, 2, part, width)
        cut = [0, 384 * width // 1024, 768 * width // 1024, width]
        orders = ["yxzw", "xyzw", "zxyw"]
        axes = ["ywzx"] * 3
        state = [ranges[..., cut[n] : cut[n + 1]] for n in range(3)]

        def adapter_round(r, state):
            kept, got = [], []
            for n in range(3):
                m = orders[n][r]
                at = axes[n].index(m)
                axes[n] = axes[n].replace(m, "")
                kept.append(lax.index_in_dim(state[n], 0, at, keepdims=False))
                got.append(swap(lax.index_in_dim(state[n], 1, at, keepdims=False), *moves[m]))
            return kept, got

        up_got0 = go(up0, "y")
        up_got2 = swap(low(gate(up_keep[1]), up_got1), *moves["x"])
        kept, got = adapter_round(0, state)
        attn = low(gate(attn_keep), attn_got)
        attn_got = swap(attn[1], *moves["z"])
        gate3 = low(gate(gate2[0]), gate_got3)
        gate_got4 = swap(gate3[1], *moves["w"])
        gains_got = go(d_gains, "c")
        grad_in = [
            lax.dot_general(gate(g), adapter_weight, (((1,), (1,)), ((), ())), preferred_element_type=f32).astype(bf16)
            for g in grads
        ]
        got0, got1, got2, up_got0, up_got2, attn_got, gate_got4, gains_got = close(
            *got, up_got0, up_got2, attn_got, gate_got4, gains_got
        )

        down_got2 = go(down_next, "y")
        state = [low(k, g) for k, g in zip(kept, (got0, got1, got2))]
        kept, got = adapter_round(1, state)
        up2 = low(low(gate(up_keep[0]), up_got0), up_got2)
        up_got3 = swap(up2[1], *moves["z"])
        attn = low(gate(attn[0]), attn_got)
        attn_got = swap(attn[1], *moves["w"])
        d_gate = plus(gate(gate3[0]), gate_got4)
        d_gains = d_gains + gains_got
        gains_got = swap(d_gains, *moves["y"])
        got0, got1, got2, up_got3, attn_got, down_got2, gains_got = close(
            *got, up_got3, attn_got, down_got2, gains_got
        )

        down2 = low(gate(down_stay), down_got2)
        down_got3 = swap(down2[1], *moves["x"])
        state = [low(k, g) for k, g in zip(kept, (got0, got1, got2))]
        kept, got = adapter_round(2, state)
        up3 = low(gate(up2[0]), up_got3)
        up_got4 = swap(up3[1], *moves["w"])
        attn = plus(gate(attn[0]), attn_got)
        d_gains = d_gains + gains_got
        gains_got = swap(d_gains, *moves["x"])
        got0, got1, got2, up_got4, down_got3, gains_got = close(*got, up_got4, down_got3, gains_got)

        down3 = low(gate(down2[0]), down_got3)
        down_got4 = swap(down3[1], *moves["w"])
        state = [low(k, g) for k, g in zip(kept, (got0, got1, got2))]
        kept, got = adapter_round(3, state)
        d_gains = d_gains + gains_got
        gains_got = [swap(d_gains, "dp", bits) for bits in (2, 4, 6)]
        d_up = plus(gate(up3[0]), up_got4)
        d_down = plus(down3[0], down_got4)
        d_adapt = jnp.concatenate([plus(k, g) for k, g in zip(kept, got)], axis=-1)
        d_gains = plus(d_gains, *gains_got)
        d_qkv = attn[:3].transpose(1, 0, 2)
        d_out = attn[3].T
    else:
        for name, size in (("tensor", members), ("dp", dp)):
            bit = 1
            while bit < size:
                d_gains = d_gains + swap(d_gains, name, bit)
                bit *= 2
        d_down = unit_grad(hiddens, flat_mlp, "z")
        d_gate = unit_grad(gates, flat_three, "x")
        d_up = unit_grad(ups, flat_three, "y")

        def reduced(xs, ys, dim):
            return lax.psum_scatter(full_grad(xs, ys), "dp", scatter_dimension=dim, tiled=True).astype(f32)

        d_qkv = reduced(flat_one, [stacked[s] for s in every], 0).reshape(-1, 3, cols)
        d_out = reduced([att[s] for s in every], flat_attn, 1)
        full = full_grad([tokens_of[s] for s in every], grads).astype(f32)
        d_adapt = lax.psum_scatter(full, ("dp", "tensor"), scatter_dimension=0, tiled=True)
        grad_in = [
            lax.dot_general(g, adapter_weight, (((1,), (1,)), ((), ())), preferred_element_type=f32).astype(bf16)
            for g in grads
        ]
    share = width // (dp * members)
    d_gains = lax.dynamic_slice_in_dim(d_gains, (me[0] * members + mine) * share, share, 1)
    grad_in = jnp.stack(grad_in, axis=1)
    out = jnp.stack([block_out[s] for s in every], axis=1)
    d_gate_up = jnp.stack([d_gate, d_up]).transpose(2, 0, 1)
    return (out, grad_in, d_adapt, d_gains, d_qkv, d_out, d_gate_up, d_down)


def solution(mesh):
    return jax.shard_map(
        body,
        mesh=mesh,
        in_specs=(
            P("tensor", "dp", None),
            P("dp"),
            P("tensor", "dp", None),
            P(),
            P(),
            P(None, None, "tensor"),
            P("tensor", None),
            P(None, None, "tensor"),
            P("tensor", None),
        ),
        out_specs=(
            P("tensor", "dp", None),
            P("tensor", "dp", None),
            P(("dp", "tensor"), None),
            P(None, ("dp", "tensor")),
            P("dp", None, "tensor"),
            P("tensor", "dp"),
            P("dp", None, "tensor"),
            P("tensor", "dp"),
        ),
        check_vma=False,
    )
```

```python
import functools

import jax
import jax.numpy as jnp
import numpy as np
from jax import lax
from jax.experimental import pallas as pl
from jax.experimental.pallas import tpu as pltpu
from jax.sharding import PartitionSpec as P

HD = 128
LOG2E = 1.4426950408889634
EPS = 1e-06
THETA = 50000.0
MASKED = -1e30
f32 = jnp.float32
bf16 = jnp.bfloat16
MIB = 1024 * 1024
LIGHT = pl.CostEstimate(flops=1, bytes_accessed=1, transcendentals=0)


def dot(a, b):
    return jnp.dot(a, b, preferred_element_type=f32)


def dot_nt(a, b):
    return lax.dot_general(a, b, (((1,), (1,)), ((), ())), preferred_element_type=f32)


def dot_tn(a, b):
    return lax.dot_general(a, b, (((0,), (0,)), ((), ())), preferred_element_type=f32)


def full_map(rank):
    return lambda *_: (0,) * rank


def whole_call(kernel, outs, scalars, arrays, scratch=(), vmem=40, name=None):
    smem = pl.BlockSpec(memory_space=pltpu.SMEM)
    vm = pl.BlockSpec(memory_space=pltpu.VMEM)
    return pl.pallas_call(
        kernel,
        out_shape=tuple(pltpu.HBM(o[0], o[1]) if len(o) > 2 else jax.ShapeDtypeStruct(*o) for o in outs),
        in_specs=[smem] * len(scalars) + [vm] * len(arrays),
        out_specs=tuple(pl.BlockSpec(o[0], full_map(len(o[0]))) if len(o) > 2 else vm for o in outs),
        scratch_shapes=list(scratch),
        compiler_params=pltpu.CompilerParams(vmem_limit_bytes=vmem * MIB),
        cost_estimate=LIGHT,
        name=name,
    )(*scalars, *arrays)


def swap(x, axis, bit):
    n = lax.axis_size(axis)
    return lax.ppermute(x, axis, [(i, i ^ bit) for i in range(n)])


def gather_blocks(x):
    far = swap(x, "tensor", 2)
    near = swap(x, "tensor", 1)
    return [x, near, far, swap(far, "tensor", 1)]


def scatter_blocks(p0, p1, p2, p3):
    near = swap(p1, "tensor", 1)
    across = (p2.astype(f32) + swap(p3, "tensor", 1).astype(f32)).astype(bf16)
    return across, (p0, near, swap(across, "tensor", 2))


def in_hbm(x):
    return pltpu.with_memory_space_constraint(x, pltpu.HBM)


def after(x, *others):
    return lax.optimization_barrier((x,) + others)[0]


def turn_tables(turn_rows, turn_blocks, j):
    cr, sr = turn_rows[0], turn_rows[1]
    cb, sb = turn_blocks[0, j : j + 1, :], turn_blocks[1, j : j + 1, :]
    sign = jnp.where(lax.broadcasted_iota(jnp.int32, (1, HD), 1) < HD // 2, -1.0, 1.0)
    return cb * cr - sb * sr, (sb * cr + cb * sr) * sign


def attn_fwd_kernel(seq, scal, x0, x1, x2, x3, w, turn_rows, turn_blocks, wo, q, k, v, o, lse, att, *parts):
    mine, length = scal[0], scal[1 + seq]
    rows = x0.shape[0]
    heads = q.shape[0]
    for j, x in enumerate((x0, x1, x2, x3)):
        base = pl.multiple_of((mine ^ j) * rows, rows)
        c, s = turn_tables(turn_rows, turn_blocks, j)
        for n, ref in ((0, q), (1, k)):
            acc = dot(x[...], w[n])
            for h in range(heads):
                part = acc[:, h * HD : (h + 1) * HD]
                turned = part * c + pltpu.roll(part, HD // 2, 1) * s
                ref[h, pl.ds(base, rows), :] = turned.astype(bf16)
        acc = dot(x[...], w[2]).astype(bf16)
        for h in range(heads):
            v[h, pl.ds(base, rows), :] = acc[:, h * HD : (h + 1) * HD]
    factor = HD**-0.5 * LOG2E
    for h in range(heads):
        vt = v[h].T
        for i in range(4):
            keys = (i + 1) * rows
            st = dot_nt(k[h, :keys, :], q[h, i * rows : keys, :]) * factor
            key_id = lax.broadcasted_iota(jnp.int32, st.shape, 0)
            row_id = lax.broadcasted_iota(jnp.int32, st.shape, 1) + i * rows
            st = jnp.where((key_id <= row_id) & (key_id < length), st, MASKED)
            top = jnp.max(st, axis=0, keepdims=True)
            weights = jnp.exp2(st - top)
            total = jnp.sum(weights, axis=0, keepdims=True)
            ot = dot(vt[:, :keys], weights.astype(bf16)) / total
            o[h, i * rows : keys, :] = ot.T.astype(bf16)
            lse[h : h + 1, i * rows : keys] = top + jnp.log2(total)
    for j in range(4):
        base = pl.multiple_of((mine ^ j) * rows, rows)
        both = jnp.concatenate([o[h, pl.ds(base, rows), :] for h in range(heads)], axis=1)
        att[j] = both
        parts[j][...] = dot(both, wo[...]).astype(bf16)


def attn_bwd_kernel(
    seq, scal, g0, g1, g2, g3, wo, q, k, v, o, lse, turn_rows, turn_blocks, w, st_out, p0, p1, p2, p3, dout, dq, dk, dv
):
    parts = (p0, p1, p2, p3)
    mine, length = scal[0], scal[1 + seq]
    rows = g0.shape[0]
    heads = q.shape[0]
    cols = heads * HD
    for j, g in enumerate((g0, g1, g2, g3)):
        mixed = dot_nt(g[...], wo[...]).astype(bf16)
        base = pl.multiple_of((mine ^ j) * rows, rows)
        for h in range(heads):
            dout[h, pl.ds(base, rows), :] = mixed[:, h * HD : (h + 1) * HD]
    scale = HD**-0.5
    factor = scale * LOG2E
    ones = jnp.ones((8, HD), f32)
    for h in range(heads):
        for i in (3, 2, 1, 0):
            keys = (i + 1) * rows
            here = slice(i * rows, keys)
            qi, di = q[h, here, :], dout[h, here, :]
            st = dot_nt(k[h, :keys, :], qi) * factor
            key_id = lax.broadcasted_iota(jnp.int32, st.shape, 0)
            row_id = lax.broadcasted_iota(jnp.int32, st.shape, 1) + i * rows
            st = jnp.where((key_id <= row_id) & (key_id < length), st, MASKED)
            probs = jnp.exp2(st - lse[h : h + 1, here])
            prob_grad = dot_nt(v[h, :keys, :], di)
            product = di.astype(f32) * o[h, here, :].astype(f32)
            inner = lax.dot_general(
                ones, product, (((1,), (1,)), ((), ())), precision=lax.Precision.HIGHEST, preferred_element_type=f32
            )[0:1, :]
            sg = (probs * (prob_grad - inner)).astype(bf16)
            new_v = dot(probs.astype(bf16), di)
            new_k = dot(sg, qi)
            if i == 3:
                dv[h] = new_v
                dk[h] = new_k
            else:
                dv[h, :keys, :] += new_v
                dk[h, :keys, :] += new_k
            dq[h, here, :] = dot_tn(sg, k[h, :keys, :])
    for j in range(4):
        base = pl.multiple_of((mine ^ j) * rows, rows)
        c, s = turn_tables(turn_rows, turn_blocks, j)
        c, s = c * scale, s * scale
        total = None
        for n, ref in enumerate((dq, dk, dv)):
            pieces = []
            for h in range(heads):
                part = ref[h, pl.ds(base, rows), :]
                if n < 2:
                    part = part * c - pltpu.roll(part, HD // 2, 1) * s
                pieces.append(part.astype(bf16))
            piece = jnp.concatenate(pieces, axis=1)
            st_out[j, :, n * cols : (n + 1) * cols] = piece
            add = dot_nt(piece, w[n])
            total = add if total is None else total + add
        parts[j][...] = total.astype(bf16)


def mlp_fwd_kernel(x0, x1, wgu0, wgu1, wd0, wd1, *outs):
    kept, parts = outs[:6], outs[6:]
    rows = x0.shape[0]
    x = jnp.concatenate([x0[...], x1[...]], axis=0)
    total = None
    for n, (wgu, wd) in enumerate(((wgu0, wd0), (wgu1, wd1))):
        hid, fa, fb = kept[3 * n : 3 * n + 3]
        gate = dot_nt(x, wgu[0])
        up = dot_nt(x, wgu[1])
        sig = jax.nn.sigmoid(gate)
        act = gate * sig
        hidden = (act * up).astype(bf16)
        a = act.astype(bf16)
        b = (up * sig * (1.0 + gate * (1.0 - sig))).astype(bf16)
        for j in range(2):
            here = slice(j * rows, (j + 1) * rows)
            hid[j], fa[j], fb[j] = hidden[here], a[here], b[here]
        add = dot(hidden, wd[...])
        total = add if total is None else total + add
    for j in range(2):
        parts[j][...] = total[j * rows : (j + 1) * rows].astype(bf16)


def mlp_bwd_kernel(g0, g1, wgu0, wgu1, wd0, wd1, fa0, fb0, fa1, fb1, gg0, gu0, gg1, gu1, *parts):
    rows = g0.shape[0]
    g = jnp.concatenate([g0[...], g1[...]], axis=0)
    total = None
    for wgu, wd, fa, fb, gg, gu in ((wgu0, wd0, fa0, fb0, gg0, gu0), (wgu1, wd1, fa1, fb1, gg1, gu1)):
        hidden_grad = dot_nt(g, wd[...])
        a = jnp.concatenate([fa[0], fa[1]], axis=0).astype(f32)
        b = jnp.concatenate([fb[0], fb[1]], axis=0).astype(f32)
        gate_grad = (hidden_grad * b).astype(bf16)
        up_grad = (hidden_grad * a).astype(bf16)
        for j in range(2):
            here = slice(j * rows, (j + 1) * rows)
            gg[j], gu[j] = gate_grad[here], up_grad[here]
        add = dot(gate_grad, wgu[0]) + dot(up_grad, wgu[1])
        total = add if total is None else total + add
    for j in range(2):
        parts[j][...] = total[j * rows : (j + 1) * rows].astype(bf16)


def factor_of(v):
    return lax.rsqrt(jnp.mean(v * v, axis=-1, keepdims=True) + EPS)


def norm_back(v, r, gain, e):
    scaled = e * gain
    inner = jnp.mean(scaled * v, axis=-1, keepdims=True)
    grad = r * (scaled - v * (r * r * inner))
    return grad, jnp.sum(e * v * r, axis=0, keepdims=True)


def summed(*addends):
    total = addends[0][...].astype(f32)
    for a in addends[1:]:
        total = total + a[...].astype(f32)
    return total


def mid_kernel(latent, p0, near, far, gains, proj_out, mid_out, normed_out):
    proj = summed(p0, near, far)
    mid = latent[...] + proj * factor_of(proj) * gains[1:2, :]
    proj_out[...] = proj
    mid_out[...] = mid
    normed_out[...] = (mid * factor_of(mid) * gains[2:3, :]).astype(bf16)


def live_grad(seq, scal, cot):
    rows = cot.shape[0]
    row_id = lax.broadcasted_iota(jnp.int32, (rows, 1), 0) + scal[0] * rows
    return jnp.where(row_id < scal[1 + seq], cot[...].astype(f32), 0.0)


def out_kernel(seq, scal, mid, p0, near, cot, gains, out, grad_out, gain_out):
    proj = summed(p0, near)
    r = factor_of(proj)
    gain = gains[3:4, :]
    out[...] = (mid[...] + proj * r * gain).astype(bf16)
    grad, gain_grad = norm_back(proj, r, gain, live_grad(seq, scal, cot))
    grad_out[...] = grad.astype(bf16)
    gain_out[...] = gain_grad


def back_kernel(seq, scal, mid, proj, p0, near, cot, gains, mid_grad_out, grad_out, gain_two, gain_three):
    three = summed(p0, near)
    m = mid[...]
    part, g3 = norm_back(m, factor_of(m), gains[2:3, :], three)
    mid_grad = live_grad(seq, scal, cot) + part
    pr = proj[...]
    grad, g2 = norm_back(pr, factor_of(pr), gains[1:2, :], mid_grad)
    mid_grad_out[...] = mid_grad
    grad_out[...] = grad.astype(bf16)
    gain_two[...] = g2
    gain_three[...] = g3


def last_kernel(latent, p0, near, far, mid_grad, gains, grad_out, gain_out):
    one = summed(p0, near, far)
    la = latent[...]
    part, g1 = norm_back(la, factor_of(la), gains[0:1, :], one)
    grad_out[...] = (mid_grad[...] + part).astype(bf16)
    gain_out[...] = g1


def first_kernel(x, w, gains, *refs):
    outs, acc = refs[:-1], refs[-1]
    seqs = len(outs) // 2
    whole = dot(x[...], w[...])
    rows, tiles = acc.shape[1] // seqs, acc.shape[0]
    for c in range(tiles):
        acc[c] = whole[:, c * 128 : (c + 1) * 128]
    for s in range(seqs):
        latent = jnp.concatenate([acc[c, pl.ds(s, rows, stride=seqs), :] for c in range(tiles)], axis=1)
        outs[s][...] = latent
        outs[seqs + s][...] = (latent * factor_of(latent) * gains[0:1, :]).astype(bf16)


def reversed_bits(index, bits):
    out = 0
    for b in range(bits):
        out = out + (((index >> b) & 1) << (bits - 1 - b))
    return out


def pair_block(g, me, pairs):
    return (me[0] >> 1) ^ reversed_bits(g, pairs.bit_length() - 1)


def grad_call(kernel, me, fixed, sliced, out, pairs, scratch=()):
    rows, d = sliced[0].shape
    wide = d // pairs
    shape = pltpu.HBM((pairs,) + out, bf16)
    spec = pl.BlockSpec((1,) + out, lambda g, m: (g,) + (0,) * len(out))

    def full_map(a):
        return lambda g, m: (0,) * a.ndim

    return pl.pallas_call(
        kernel,
        out_shape=(shape, shape),
        grid_spec=pltpu.PrefetchScalarGridSpec(
            num_scalar_prefetch=1,
            grid=(pairs,),
            in_specs=[pl.BlockSpec(a.shape, full_map(a)) for a in fixed]
            + [pl.BlockSpec((rows, wide), lambda g, m: (0, pair_block(g, m, pairs))) for _ in sliced],
            out_specs=(spec, spec),
            scratch_shapes=list(scratch),
        ),
        compiler_params=pltpu.CompilerParams(vmem_limit_bytes=20 * MIB),
        cost_estimate=LIGHT,
        name="weight_grad",
    )(me, *[in_hbm(a) for a in fixed], *[in_hbm(a) for a in sliced])


def grad_rows(me, groups, dp, cols):
    pairs = dp // 2
    half = groups[0][0][0].shape[1] // dp
    fixed = [y for _, ys in groups for y in ys]
    sliced = [x for xs, _ in groups for x in xs]
    count = sum(ys[0].shape[-1] // cols for _, ys in groups)

    def kernel(me_ref, *refs):
        yr, xr, (keep, send) = refs[: len(fixed)], refs[len(fixed) : -2], refs[-2:]
        odd = (me_ref[0] & 1) == 1
        n = y0 = x0 = 0
        for group, (xs, ys) in enumerate(groups):
            lhs = jnp.concatenate([x[...] for x in xr[x0 : x0 + len(xs)]], axis=0)
            rhs = jnp.concatenate([y[b] for y in yr[y0 : y0 + len(ys)] for b in range(y.shape[0])], axis=0)
            x0, y0 = x0 + len(xs), y0 + len(ys)
            acc = dot_tn(lhs, rhs)
            stay = jnp.where(odd, acc[half:], acc[:half]).astype(bf16)
            go = jnp.where(odd, acc[:half], acc[half:]).astype(bf16)
            if group == len(groups) - 1:
                for ref, value in ((keep, stay), (send, go)):
                    value = value.T
                    for c in range(0, cols, half):
                        ref[0, n, :, c : c + half] = value[c : c + half]
                continue
            for c in range(0, acc.shape[1], cols):
                keep[0, n] = stay[:, c : c + cols]
                send[0, n] = go[:, c : c + cols]
                n += 1

    return grad_call(kernel, me, fixed, sliced, (count, half, cols), pairs)


def grad_units(me, sets, ys, dp, first):
    rows, d = ys[0].shape
    pairs = dp // 2
    wide = d // pairs
    half = wide // 2
    units = sets[0][0].shape[-1]
    quarter = units // 4
    tokens = len(ys) * rows
    count = len(sets[0])
    inner = pairs // 2

    def kernel(me_ref, *refs):
        xr, yr = refs[: 2 * count], refs[2 * count : 2 * count + len(ys)]
        keep, send0, send1, turned = refs[2 * count + len(ys) :]
        sends = (send0, send1)
        step = pl.program_id(0)

        @pl.when(step == 0)
        def _():
            for n in range(2):
                block = jnp.concatenate([x[b] for x in xr[n * count : (n + 1) * count] for b in range(x.shape[0])], axis=0).T
                if n == 0:
                    turned[:units, :] = block
                else:
                    for r in range(4):
                        base = pl.multiple_of(units + ((me_ref[0] & 3) ^ r) * quarter, quarter)
                        turned[pl.ds(base, quarter), :] = block[r * quarter : (r + 1) * quarter]

        acc = dot(turned[...], jnp.concatenate([y[...] for y in yr], axis=0))
        odd = (me_ref[0] & 1) == 1
        same = jnp.where(odd, acc[:, half:], acc[:, :half]).astype(bf16)
        other = jnp.where(odd, acc[:, :half], acc[:, half:]).astype(bf16)
        if first == "y":
            for x, part in ((0, same), (1, other)):
                keep[x, 0] = part[:units]
                sends[x][0] = part[units:]
        elif first == "x":
            for n in range(2):
                keep[0, n, 0] = same[n * units : (n + 1) * units]
            for ref, when in ((send0, step < inner), (send1, step >= inner)):

                @pl.when(when)
                def _():
                    for n in range(2):
                        ref[n, 0] = other[n * units : (n + 1) * units]
        else:

            @pl.when(step < inner)
            def _():
                for n in range(2):
                    keep[n, 0, 0] = same[n * units : (n + 1) * units]
                    keep[n, 1, 0] = other[n * units : (n + 1) * units]

            @pl.when(step >= inner)
            def _():
                for n in range(2):
                    sends[n][0, 0] = same[n * units : (n + 1) * units]
                    sends[n][1, 0] = other[n * units : (n + 1) * units]

    def early(g):
        return jnp.minimum(g, inner - 1)

    def late(g):
        return jnp.maximum(g - inner, 0)

    if first == "y":
        outs = [((2, pairs), (2, 1), lambda g, m: (0, g, 0, 0))] + [((pairs,), (1,), lambda g, m: (g, 0, 0))] * 2
    elif first == "x":
        outs = [
            ((2, 2, inner), (1, 2, 1), lambda g, m: (g // inner, 0, g % inner, 0, 0)),
            ((2, inner), (2, 1), lambda g, m: (0, early(g), 0, 0)),
            ((2, inner), (2, 1), lambda g, m: (0, late(g), 0, 0)),
        ]
    else:
        outs = [((2, 2, inner), (2, 2, 1), lambda g, m: (0, 0, early(g), 0, 0))] + [
            ((2, inner), (2, 1), lambda g, m: (0, late(g), 0, 0))
        ] * 2
    fixed = [a for one_set in sets for a in one_set]
    return pl.pallas_call(
        kernel,
        out_shape=tuple(pltpu.HBM(shape + (units, half), bf16) for shape, _, _ in outs),
        grid_spec=pltpu.PrefetchScalarGridSpec(
            num_scalar_prefetch=1,
            grid=(pairs,),
            in_specs=[pl.BlockSpec(a.shape, lambda g, m: (0, 0, 0)) for a in fixed]
            + [pl.BlockSpec((rows, wide), lambda g, m: (0, pair_block(g, m, pairs))) for _ in ys],
            out_specs=tuple(pl.BlockSpec(block + (units, half), f) for _, block, f in outs),
            scratch_shapes=[pltpu.VMEM((2 * units, tokens), bf16)],
        ),
        compiler_params=pltpu.CompilerParams(vmem_limit_bytes=20 * MIB),
        cost_estimate=LIGHT,
        name="grad_units",
    )(me, *[in_hbm(a) for a in fixed], *[in_hbm(a) for a in ys])


def grad_adapter(me, xs, grads, dp):
    rows, joined = xs[0].shape
    width = grads[0].shape[1]
    wide = joined // dp
    part = wide // 4
    count = len(xs)

    def kernel(me_ref, *refs):
        xr, gr, (keep, send, grad, acc) = refs[:count], refs[count : 2 * count], refs[2 * count :]

        @pl.when(pl.program_id(0) == 0)
        def _():
            for n in range(count):
                grad[n * rows : (n + 1) * rows, :] = gr[n][...]

        acc[...] = dot_tn(jnp.concatenate([x[...] for x in xr], axis=0), grad[...])
        for far in (0, 1):
            for near, ref in ((0, keep), (1, send)):
                base = pl.multiple_of((me_ref[1] ^ (2 * far + near)) * part, part)
                ref[far, 0] = acc[pl.ds(base, part), :].astype(bf16)

    shape = jax.ShapeDtypeStruct((2, dp, part, width), bf16)
    spec = pl.BlockSpec((2, 1, part, width), lambda g, m: (0, g, 0, 0))
    return pl.pallas_call(
        kernel,
        out_shape=(shape, shape),
        grid_spec=pltpu.PrefetchScalarGridSpec(
            num_scalar_prefetch=1,
            grid=(dp,),
            in_specs=[pl.BlockSpec((rows, wide), lambda g, m: (0, m[0] ^ g)) for _ in xs]
            + [pl.BlockSpec((rows, width), lambda g, m: (0, 0)) for _ in grads],
            out_specs=(spec, spec),
            scratch_shapes=[pltpu.VMEM((count * rows, width), bf16), pltpu.VMEM((wide, width), f32)],
        ),
        compiler_params=pltpu.CompilerParams(vmem_limit_bytes=20 * MIB),
        cost_estimate=LIGHT,
        name="grad_adapter",
    )(me, *[in_hbm(x) for x in xs], *grads)


def plus(a, *others):
    total = a.astype(f32)
    for o in others:
        total = total + o.astype(f32)
    return total


def low(a, *others):
    return plus(a, *others).astype(bf16)


def body(adapter_in, lengths, cotangent, adapter_weight, gains, qkv_weight, out_weight, gate_up_weight, down_weight):
    rows, seqs = adapter_in.shape[0], adapter_in.shape[1]
    width = adapter_weight.shape[1]
    cols = qkv_weight.shape[2]
    heads = cols // HD
    units = down_weight.shape[0]
    members = lax.axis_size("tensor")
    dp = lax.axis_size("dp")
    seq_len = rows * members
    fast = dp == 8 and (width // dp) % 128 == 0
    mine = lax.axis_index("tensor").astype(jnp.int32)
    me = lax.axis_index("dp").astype(jnp.int32).reshape(1)
    scal = jnp.concatenate([mine.reshape(1), lengths])

    lane = jnp.arange(HD, dtype=jnp.int32) % (HD // 2)
    freq = THETA ** (-(lane.astype(f32) * 2.0 / HD))
    inner = jnp.arange(rows, dtype=jnp.int32).astype(f32)[:, None] * freq[None, :]
    owner = (mine ^ jnp.arange(members, dtype=jnp.int32)) * rows
    outer = owner.astype(f32)[:, None] * freq[None, :]
    turn_rows = jnp.stack([jnp.cos(inner), jnp.sin(inner)])
    turn_blocks = jnp.stack([jnp.cos(outer), jnp.sin(outer)])

    every = range(seqs)
    x_in = adapter_in.reshape(rows * seqs, -1)
    x_first = x_in
    tok = (rows, width)

    def parts(n):
        return [(tok, bf16)] * n

    gain = {}

    clock = [None]

    def gate(x):
        return x if clock[0] is None else after(x, clock[0])

    def close(*values):
        values = lax.optimization_barrier(tuple(values))
        clock[0] = values[0]
        return values

    moves = {"c": ("tensor", 1), "y": ("tensor", 2), "x": ("dp", 1), "z": ("dp", 2), "w": ("dp", 4)}

    def go(x, m):
        return swap(gate(x), *moves[m])

    def hop(x):
        return swap(x, "tensor", 1)

    place = me[0] & 3
    w_gu = gate_up_weight.transpose(1, 2, 0)
    w_qkv = qkv_weight.transpose(1, 0, 2)
    quarter = units // 4
    gu0 = swap(lax.dynamic_slice_in_dim(w_gu, place * quarter, quarter, 1), "tensor", 2)
    latent_a, latent_b, normed_a, normed_b = whole_call(
        first_kernel,
        [(tok, f32, True)] * seqs + [(tok, bf16)] * seqs,
        [],
        [in_hbm(x_in), in_hbm(adapter_weight), gains],
        scratch=[pltpu.VMEM((width // 128, rows * seqs, 128), f32)],
        vmem=24,
        name="first",
    )
    latent = [latent_a, latent_b]
    normed_a, normed_b, gu0, turn_rows, turn_blocks = close(normed_a, normed_b, gu0, turn_rows, turn_blocks)

    far_a, near_a = go(normed_a, "y"), go(normed_a, "c")
    d0 = go(lax.dynamic_slice_in_dim(down_weight, place * quarter, quarter, 0), "y")
    gu1, gu2 = go(gu0, "x"), go(gu0, "z")
    early = gate(cotangent)
    cot = [early[:, s] for s in every]
    tokens_of = gate(adapter_in)
    tokens_of = [tokens_of[:, s] for s in every]
    far_a, near_a, d0, gu1, gu2, *both = close(far_a, near_a, d0, gu1, gu2, *cot, *tokens_of)
    cot, tokens_of = both[:seqs], both[seqs:]

    head_shape = ((heads, seq_len, HD), bf16, True)

    def attn_fwd(s, blocks):
        *kept, at, p0, p1, p2, p3 = whole_call(
            functools.partial(attn_fwd_kernel, s),
            [head_shape] * 4 + [((8, seq_len), f32, True), ((members, rows, cols), bf16, True)] + parts(4),
            [scal],
            [*blocks, w_qkv, turn_rows, turn_blocks, out_weight],
            vmem=20,
            name="attn_fwd",
        )
        return kept, at, p0, p1, p2, p3

    far_b, near_b = go(normed_b, "y"), go(normed_b, "c")
    gu3, d2 = go(gu2, "x"), go(d0, "z")
    one = {0: [normed_a, near_a, far_a, hop(far_a)]}
    qkvo, att = {}, {}
    qkvo[0], att[0], *sums = attn_fwd(0, one[0])
    p0, p1, p2, p3, far_b, near_b, gu3, d2 = close(*sums, far_b, near_b, gu3, d2)
    across_a, near_a = low(p2, hop(p3)), hop(p1)
    across_a, near_a, own_a = close(across_a, near_a, p0)

    far_a, d1 = go(across_a, "y"), go(d0, "x")
    one[1] = [gate(normed_b), near_b, far_b, hop(far_b)]
    qkvo[1], att[1], *sums = attn_fwd(1, one[1])
    p0, p1, p2, p3, far_a, d1 = close(*sums, far_a, d1)
    across_b, near_b = low(p2, hop(p3)), hop(p1)
    across_b, near_b, own_b = close(across_b, near_b, p0)

    far_b, d3 = go(across_b, "y"), go(d1, "z")
    far_gu = jnp.concatenate([gate(gu0), gu1, gu2, gu3], axis=1)

    def mid_of(s, *addends):
        return whole_call(
            mid_kernel,
            [(tok, f32, True), (tok, f32, True), (tok, bf16)],
            [],
            [gate(latent[s]), *addends, gains],
            vmem=8,
            name="mid",
        )

    proj, mid, three, ffn, block_out, mlp_g, gu_g = {}, {}, {}, {}, {}, {}, {}
    proj[0], mid[0], own = mid_of(0, own_a, near_a, far_a)
    three[0] = [own, hop(own)]
    far_b, d3, far_gu, t0, t1 = close(far_b, d3, far_gu, *three[0])
    three[0] = [t0, t1]

    far_d = jnp.concatenate([gate(d0), d1, d2, d3], axis=0)
    mlp_weights = [w_gu, far_gu, down_weight, far_d]
    hid_shape = ((2, rows, units), bf16, True)

    def ffn_fwd(s):
        *ffn[s], p0, p1 = whole_call(
            mlp_fwd_kernel, [hid_shape] * 6 + parts(2), [], [*three[s], *mlp_weights], vmem=36, name="mlp_fwd"
        )
        return p0, hop(p1)

    def out_of(s, *addends):
        block_out[s], own, gain[3, s] = whole_call(
            functools.partial(out_kernel, s),
            [(tok, bf16, True), (tok, bf16), ((1, width), f32)],
            [scal],
            [mid[s], *addends, cot[s], gains],
            vmem=10,
            name="out",
        )
        mlp_g[s] = [own, hop(own)]

    def ffn_bwd(s):
        *gu_g[s], p0, p1 = whole_call(
            mlp_bwd_kernel,
            [hid_shape] * 4 + parts(2),
            [],
            [*mlp_g[s], *mlp_weights, *ffn[s][1:3], *ffn[s][4:6]],
            vmem=36,
            name="mlp_bwd",
        )
        return p0, p1

    mid_grad, attn_g, stacked = {}, {}, {}

    def back_of(s, *addends):
        mid_grad[s], own, gain[1, s], gain[2, s] = whole_call(
            functools.partial(back_kernel, s),
            [(tok, f32, True), (tok, bf16), ((1, width), f32), ((1, width), f32)],
            [scal],
            [mid[s], proj[s], *addends, cot[s], gains],
            vmem=12,
            name="back",
        )
        return own

    sum_a = ffn_fwd(0)
    proj[1], mid[1], own = mid_of(1, own_b, near_b, far_b)
    three[1] = [own, hop(own)]
    out_of(0, *sum_a)
    sum_b = ffn_fwd(1)
    p0, p1 = ffn_bwd(0)
    sum_a = p0, hop(p1)
    out_of(1, *sum_b)
    grad_a = back_of(0, *sum_a)
    grad_a, b0, b1 = close(grad_a, *mlp_g[1])
    mlp_g[1] = [b0, b1]

    def full_grad(xs, ys):
        xs, ys = [jnp.concatenate([a.reshape(-1, a.shape[-1]) for a in part], 0) for part in (xs, ys)]
        return lax.dot_general(xs, ys, (((0,), (0,)), ((), ())), preferred_element_type=f32).astype(bf16)

    def unit_grad(sets, ys, first):
        ys = [gate(ys[0]), *ys[1:]]
        if fast:
            keep, send0, send1 = grad_units(me, sets, ys, dp, first)
            split = (2, 2) + keep.shape[-2:]
            return keep.reshape((2,) + split), send0.reshape(split), send1.reshape(split)
        own, far = [full_grad(xs, ys) for xs in sets]
        far = jnp.concatenate([lax.dynamic_slice_in_dim(far, (place ^ a) * quarter, quarter, 0) for a in range(4)], axis=0)
        total = low(own, swap(far, "tensor", 2))
        return lax.psum_scatter(total, "dp", scatter_dimension=1, tiled=True).astype(f32)

    far_a, near_a = go(grad_a, "y"), go(grad_a, "c")
    sum_b = ffn_bwd(1)
    flat_three = [b for s in every for b in three[s]]
    flat_mlp = [b for s in every for b in mlp_g[s]]
    flat_one = [b for s in every for b in one[s]]
    hiddens = [[ffn[s][3 * n] for s in every] for n in (0, 1)]
    gates = [[gu_g[s][2 * n] for s in every] for n in (0, 1)]
    ups = [[gu_g[s][2 * n + 1] for s in every] for n in (0, 1)]

    if fast:
        down_keep, down0, down1 = unit_grad(hiddens, flat_mlp, "z")
        p0, p1, far_a, near_a, down0, down1 = close(*sum_b, far_a, near_a, down0, down1)
    else:
        p0, p1, far_a, near_a = close(*sum_b, far_a, near_a)
    grad_b = close(back_of(1, p0, hop(p1)))[0]


    head_f32 = (heads, seq_len, HD)

    def attn_bwd(s, blocks):
        stacked[s], p0, p1, p2, p3 = whole_call(
            functools.partial(attn_bwd_kernel, s),
            [((members, rows, 3 * cols), bf16, True)] + parts(4),
            [scal],
            [*blocks, out_weight, *qkvo[s], turn_rows, turn_blocks, w_qkv],
            scratch=[pltpu.VMEM(head_f32, bf16)] + [pltpu.VMEM(head_f32, f32)] * 3,
            vmem=24,
            name="attn_bwd",
        )
        return p0, p1, p2, p3

    far_b, near_b = go(grad_b, "y"), go(grad_b, "c")
    attn_g[0] = [gate(grad_a), near_a, far_a, hop(far_a)]
    sums = attn_bwd(0, attn_g[0])
    if fast:
        down_got1 = go(down1, "z")
        gate_keep, gate0, gate1 = unit_grad(gates, flat_three, "x")
        p0, p1, p2, p3, far_b, near_b, gate0, gate1, down_got1 = close(*sums, far_b, near_b, gate0, gate1, down_got1)
    else:
        p0, p1, p2, p3, far_b, near_b = close(*sums, far_b, near_b)
    across_a, near_a = low(p2, hop(p3)), hop(p1)
    across_a, near_a, own_a = close(across_a, near_a, p0)

    far_a = go(across_a, "y")
    attn_g[1] = [gate(grad_b), near_b, far_b, hop(far_b)]
    sums = attn_bwd(1, attn_g[1])
    if fast:
        down_got0, gate_got1 = go(down0, "z"), go(gate1, "x")
        up_keep, up0, up1 = unit_grad(ups, flat_three, "y")
        p0, p1, p2, p3, far_a, down_got0, gate_got1, up0, up1 = close(*sums, far_a, down_got0, gate_got1, up0, up1)
    else:
        p0, p1, p2, p3, far_a = close(*sums, far_a)
    across_b, near_b = low(p2, hop(p3)), hop(p1)
    across_b, near_b, own_b = close(across_b, near_b, p0)

    latent_grad = {}

    def last_of(s, *addends):
        latent_grad[s], gain[0, s] = whole_call(
            last_kernel,
            [(tok, bf16), ((1, width), f32)],
            [],
            [gate(latent[s]), *addends, mid_grad[s], gains],
            vmem=10,
            name="last",
        )

    both_me = jnp.concatenate([me, mine.reshape(1)])

    far_b = go(across_b, "y")
    last_of(0, own_a, near_a, far_a)
    flat_attn = [b for s in every for b in attn_g[s]]
    if fast:
        gate_got0 = go(gate0, "x")
        down_next = low(gate(down_keep[1]), down_got1)
        gate_got2 = swap(low(gate(gate_keep[1]), gate_got1), *moves["z"])
        down_stay = low(gate(down_keep[0]), down_got0)
        first = [gate(flat_one[0]), *flat_one[1:]]
        attn_keep, attn_send = grad_rows(
            me, [(first, [stacked[s] for s in every]), (flat_attn, [att[s] for s in every])], dp, cols
        )
        lead = (2, 2) + attn_keep.shape[1:]
        half = width // dp
        attn_keep, attn_send = attn_keep.reshape(lead), attn_send.reshape(lead)
        far_b, attn_send, gate_got0, gate_got2, down_next, down_stay = close(
            far_b, attn_send, gate_got0, gate_got2, down_next, down_stay
        )
    else:
        far_b = close(far_b)[0]

    last_of(1, own_b, near_b, far_b)
    grads = [latent_grad[s] for s in every]
    d_gains = sum(jnp.concatenate([gain[g, s] for g in range(4)], axis=0) for s in every)
    if fast:
        up_got1, attn_got = go(up1, "y"), go(attn_send, "x")
        gate2 = low(low(gate(gate_keep[0]), gate_got0), gate_got2)
        gate_got3 = swap(gate2[1], *moves["y"])
        keep, send = grad_adapter(both_me, tokens_of, grads, dp)
        send, up_got1, attn_got, gate_got3, d_gains = close(send, up_got1, attn_got, gate_got3, d_gains)
        d_gains = d_gains + hop(d_gains)
        total, d_gains = close(low(keep, hop(send)), d_gains + swap(d_gains, *moves["y"]))

        part = total.shape[-2]
        ranges = total.reshape(2, 2, 2, 2, part, width)
        orders = ["zxyw", "yxzw"]
        cut = width * 5 // 8
        axes = ["ywzx"] * 2
        state = [ranges[..., :cut], ranges[..., cut:]]

        def adapter_round(r, state):
            kept, got = [], []
            for n in range(2):
                m = orders[n][r]
                at = axes[n].index(m)
                axes[n] = axes[n].replace(m, "")
                kept.append(lax.index_in_dim(state[n], 0, at, keepdims=False))
                got.append(swap(lax.index_in_dim(state[n], 1, at, keepdims=False), *moves[m]))
            return kept, got

        up_got0 = go(up0, "y")
        up_got2 = swap(low(gate(up_keep[1]), up_got1), *moves["x"])
        kept, got = adapter_round(0, state)
        attn = low(gate(attn_keep), attn_got)
        attn_got = swap(attn[1], *moves["z"])
        gate3 = low(gate(gate2[0]), gate_got3)
        grad_in = [
            lax.dot_general(gate(g), adapter_weight, (((1,), (1,)), ((), ())), preferred_element_type=f32).astype(bf16)
            for g in grads
        ]
        got0, got1, up_got0, up_got2, attn_got = close(*got, up_got0, up_got2, attn_got)

        down_got2 = go(down_next, "y")
        state = [low(k, g) for k, g in zip(kept, (got0, got1))]
        kept, got = adapter_round(1, state)
        up2 = low(low(gate(up_keep[0]), up_got0), up_got2)
        up_got3 = swap(up2[1], *moves["z"])
        attn = low(gate(attn[0]), attn_got)
        attn_got = swap(attn[1], *moves["w"])
        got0, got1, up_got3, attn_got, down_got2 = close(*got, up_got3, attn_got, down_got2)

        down2 = low(gate(down_stay), down_got2)
        down_got3 = swap(down2[1], *moves["x"])
        gate_got4 = go(gate3[1], "w")
        state = [low(k, g) for k, g in zip(kept, (got0, got1))]
        kept, got = adapter_round(2, state)
        up3 = low(gate(up2[0]), up_got3)
        up_got4 = swap(up3[1], *moves["w"])
        attn = plus(gate(attn[0]), attn_got)
        got0, got1, up_got4, gate_got4, down_got3, attn = close(*got, up_got4, gate_got4, down_got3, attn)

        state = [low(k, g) for k, g in zip(kept, (got0, got1))]
        kept, got = adapter_round(3, state)
        down3 = low(gate(down2[0]), down_got3)
        down_got4 = swap(down3[1], *moves["w"])
        d_gains = gate(d_gains)
        d_gains = d_gains + swap(d_gains, *moves["x"])
        d_gains = plus(d_gains, *[swap(d_gains, "dp", bits) for bits in (2, 4, 6)])
        d_up = plus(gate(up3[0]), up_got4)
        d_gate = plus(gate(gate3[0]), gate_got4)
        d_down = plus(down3[0], down_got4)
        d_adapt = jnp.concatenate([plus(k, g) for k, g in zip(kept, got)], axis=-1)
        d_qkv = attn[:3].transpose(1, 0, 2)
        d_out = jnp.concatenate([attn[3, :, :half], attn[3, :, half:]], axis=0)
    else:
        d_gains = lax.psum(d_gains, ("dp", "tensor"))
        d_down = unit_grad(hiddens, flat_mlp, "z")
        d_gate = unit_grad(gates, flat_three, "x")
        d_up = unit_grad(ups, flat_three, "y")

        def reduced(xs, ys, dim):
            return lax.psum_scatter(full_grad(xs, ys), "dp", scatter_dimension=dim, tiled=True).astype(f32)

        d_qkv = reduced(flat_one, [stacked[s] for s in every], 0).reshape(-1, 3, cols)
        d_out = reduced([att[s] for s in every], flat_attn, 1)
        full = full_grad([tokens_of[s] for s in every], grads).astype(f32)
        d_adapt = lax.psum_scatter(full, ("dp", "tensor"), scatter_dimension=0, tiled=True)
        grad_in = [
            lax.dot_general(g, adapter_weight, (((1,), (1,)), ((), ())), preferred_element_type=f32).astype(bf16)
            for g in grads
        ]
    share = width // (dp * members)
    d_gains = lax.dynamic_slice_in_dim(d_gains, (me[0] * members + mine) * share, share, 1)
    grad_in = jnp.stack(grad_in, axis=1)
    out = jnp.stack([block_out[s] for s in every], axis=1)
    d_gate_up = jnp.stack([d_gate, d_up]).transpose(2, 0, 1)
    return (out, grad_in, d_adapt, d_gains, d_qkv, d_out, d_gate_up, d_down)


def solution(mesh):
    return jax.shard_map(
        body,
        mesh=mesh,
        in_specs=(
            P("tensor", "dp", None),
            P("dp"),
            P("tensor", "dp", None),
            P(),
            P(),
            P(None, None, "tensor"),
            P("tensor", None),
            P(None, None, "tensor"),
            P("tensor", None),
        ),
        out_specs=(
            P("tensor", "dp", None),
            P("tensor", "dp", None),
            P(("dp", "tensor"), None),
            P(None, ("dp", "tensor")),
            P("dp", None, "tensor"),
            P("tensor", "dp"),
            P("dp", None, "tensor"),
            P("tensor", "dp"),
        ),
        check_vma=False,
    )
```

```python
import functools

import jax
import jax.numpy as jnp
import numpy as np
from jax import lax
from jax.experimental import pallas as pl
from jax.experimental.pallas import tpu as pltpu
from jax.sharding import PartitionSpec as P

HD = 128
LOG2E = 1.4426950408889634
EPS = 1e-06
THETA = 50000.0
MASKED = -1e30
f32 = jnp.float32
bf16 = jnp.bfloat16
MIB = 1024 * 1024
LIGHT = pl.CostEstimate(flops=1, bytes_accessed=1, transcendentals=0)


def dot(a, b):
    return jnp.dot(a, b, preferred_element_type=f32)


def dot_nt(a, b):
    return lax.dot_general(a, b, (((1,), (1,)), ((), ())), preferred_element_type=f32)


def dot_tn(a, b):
    return lax.dot_general(a, b, (((0,), (0,)), ((), ())), preferred_element_type=f32)


def full_map(rank):
    return lambda *_: (0,) * rank


def whole_call(kernel, outs, scalars, arrays, scratch=(), vmem=40, name=None):
    smem = pl.BlockSpec(memory_space=pltpu.SMEM)
    vm = pl.BlockSpec(memory_space=pltpu.VMEM)
    return pl.pallas_call(
        kernel,
        out_shape=tuple(pltpu.HBM(o[0], o[1]) if len(o) > 2 else jax.ShapeDtypeStruct(*o) for o in outs),
        in_specs=[smem] * len(scalars) + [vm] * len(arrays),
        out_specs=tuple(pl.BlockSpec(o[0], full_map(len(o[0]))) if len(o) > 2 else vm for o in outs),
        scratch_shapes=list(scratch),
        compiler_params=pltpu.CompilerParams(vmem_limit_bytes=vmem * MIB),
        cost_estimate=LIGHT,
        name=name,
    )(*scalars, *arrays)


def swap(x, axis, bit):
    n = lax.axis_size(axis)
    return lax.ppermute(x, axis, [(i, i ^ bit) for i in range(n)])


def gather_blocks(x):
    far = swap(x, "tensor", 2)
    near = swap(x, "tensor", 1)
    return [x, near, far, swap(far, "tensor", 1)]


def scatter_blocks(p0, p1, p2, p3):
    near = swap(p1, "tensor", 1)
    across = (p2.astype(f32) + swap(p3, "tensor", 1).astype(f32)).astype(bf16)
    return across, (p0, near, swap(across, "tensor", 2))


def in_hbm(x):
    return pltpu.with_memory_space_constraint(x, pltpu.HBM)


def after(x, *others):
    return lax.optimization_barrier((x,) + others)[0]


def turn_tables(turn_rows, turn_blocks, j):
    cr, sr = turn_rows[0], turn_rows[1]
    cb, sb = turn_blocks[0, j : j + 1, :], turn_blocks[1, j : j + 1, :]
    sign = jnp.where(lax.broadcasted_iota(jnp.int32, (1, HD), 1) < HD // 2, -1.0, 1.0)
    return cb * cr - sb * sr, (sb * cr + cb * sr) * sign


def attn_fwd_kernel(seq, scal, x0, x1, x2, x3, w, turn_rows, turn_blocks, wo, q, k, v, o, lse, att, *parts):
    mine, length = scal[0], scal[1 + seq]
    rows = x0.shape[0]
    heads = q.shape[0]
    for j, x in enumerate((x0, x1, x2, x3)):
        base = pl.multiple_of((mine ^ j) * rows, rows)
        c, s = turn_tables(turn_rows, turn_blocks, j)
        for n, ref in ((0, q), (1, k)):
            acc = dot(x[...], w[n])
            for h in range(heads):
                part = acc[:, h * HD : (h + 1) * HD]
                turned = part * c + pltpu.roll(part, HD // 2, 1) * s
                ref[h, pl.ds(base, rows), :] = turned.astype(bf16)
        acc = dot(x[...], w[2]).astype(bf16)
        for h in range(heads):
            v[h, pl.ds(base, rows), :] = acc[:, h * HD : (h + 1) * HD]
    factor = HD**-0.5 * LOG2E
    for h in range(heads):
        vt = v[h].T
        for i in range(4):
            keys = (i + 1) * rows
            st = dot_nt(k[h, :keys, :], q[h, i * rows : keys, :]) * factor
            key_id = lax.broadcasted_iota(jnp.int32, st.shape, 0)
            row_id = lax.broadcasted_iota(jnp.int32, st.shape, 1) + i * rows
            st = jnp.where((key_id <= row_id) & (key_id < length), st, MASKED)
            top = jnp.max(st, axis=0, keepdims=True)
            weights = jnp.exp2(st - top)
            total = jnp.sum(weights, axis=0, keepdims=True)
            ot = dot(vt[:, :keys], weights.astype(bf16)) / total
            o[h, i * rows : keys, :] = ot.T.astype(bf16)
            lse[h : h + 1, i * rows : keys] = top + jnp.log2(total)
    for j in range(4):
        base = pl.multiple_of((mine ^ j) * rows, rows)
        both = jnp.concatenate([o[h, pl.ds(base, rows), :] for h in range(heads)], axis=1)
        att[j] = both
        parts[j][...] = dot(both, wo[...]).astype(bf16)


def attn_bwd_kernel(
    seq, scal, g0, g1, g2, g3, wo, q, k, v, o, lse, turn_rows, turn_blocks, w, st_out, p0, p1, p2, p3, dout, dq, dk, dv
):
    parts = (p0, p1, p2, p3)
    mine, length = scal[0], scal[1 + seq]
    rows = g0.shape[0]
    heads = q.shape[0]
    cols = heads * HD
    for j, g in enumerate((g0, g1, g2, g3)):
        mixed = dot_nt(g[...], wo[...]).astype(bf16)
        base = pl.multiple_of((mine ^ j) * rows, rows)
        for h in range(heads):
            dout[h, pl.ds(base, rows), :] = mixed[:, h * HD : (h + 1) * HD]
    scale = HD**-0.5
    factor = scale * LOG2E
    ones = jnp.ones((8, HD), f32)
    for h in range(heads):
        for i in (3, 2, 1, 0):
            keys = (i + 1) * rows
            here = slice(i * rows, keys)
            qi, di = q[h, here, :], dout[h, here, :]
            st = dot_nt(k[h, :keys, :], qi) * factor
            key_id = lax.broadcasted_iota(jnp.int32, st.shape, 0)
            row_id = lax.broadcasted_iota(jnp.int32, st.shape, 1) + i * rows
            st = jnp.where((key_id <= row_id) & (key_id < length), st, MASKED)
            probs = jnp.exp2(st - lse[h : h + 1, here])
            prob_grad = dot_nt(v[h, :keys, :], di)
            product = di.astype(f32) * o[h, here, :].astype(f32)
            inner = lax.dot_general(
                ones, product, (((1,), (1,)), ((), ())), precision=lax.Precision.HIGHEST, preferred_element_type=f32
            )[0:1, :]
            sg = (probs * (prob_grad - inner)).astype(bf16)
            new_v = dot(probs.astype(bf16), di)
            new_k = dot(sg, qi)
            if i == 3:
                dv[h] = new_v
                dk[h] = new_k
            else:
                dv[h, :keys, :] += new_v
                dk[h, :keys, :] += new_k
            dq[h, here, :] = dot_tn(sg, k[h, :keys, :])
    for j in range(4):
        base = pl.multiple_of((mine ^ j) * rows, rows)
        c, s = turn_tables(turn_rows, turn_blocks, j)
        c, s = c * scale, s * scale
        total = None
        for n, ref in enumerate((dq, dk, dv)):
            pieces = []
            for h in range(heads):
                part = ref[h, pl.ds(base, rows), :]
                if n < 2:
                    part = part * c - pltpu.roll(part, HD // 2, 1) * s
                pieces.append(part.astype(bf16))
            piece = jnp.concatenate(pieces, axis=1)
            st_out[j, :, n * cols : (n + 1) * cols] = piece
            add = dot_nt(piece, w[n])
            total = add if total is None else total + add
        parts[j][...] = total.astype(bf16)


def mlp_fwd_kernel(x0, x1, wgu0, wgu1, wd0, wd1, *outs):
    kept, parts = outs[:6], outs[6:]
    rows = x0.shape[0]
    x = jnp.concatenate([x0[...], x1[...]], axis=0)
    total = None
    for n, (wgu, wd) in enumerate(((wgu0, wd0), (wgu1, wd1))):
        hid, fa, fb = kept[3 * n : 3 * n + 3]
        gate = dot_nt(x, wgu[0])
        up = dot_nt(x, wgu[1])
        sig = jax.nn.sigmoid(gate)
        act = gate * sig
        hidden = (act * up).astype(bf16)
        a = act.astype(bf16)
        b = (up * sig * (1.0 + gate * (1.0 - sig))).astype(bf16)
        for j in range(2):
            here = slice(j * rows, (j + 1) * rows)
            hid[j], fa[j], fb[j] = hidden[here], a[here], b[here]
        add = dot(hidden, wd[...])
        total = add if total is None else total + add
    for j in range(2):
        parts[j][...] = total[j * rows : (j + 1) * rows].astype(bf16)


def mlp_bwd_kernel(g0, g1, wgu0, wgu1, wd0, wd1, fa0, fb0, fa1, fb1, gg0, gu0, gg1, gu1, *parts):
    rows = g0.shape[0]
    g = jnp.concatenate([g0[...], g1[...]], axis=0)
    total = None
    for wgu, wd, fa, fb, gg, gu in ((wgu0, wd0, fa0, fb0, gg0, gu0), (wgu1, wd1, fa1, fb1, gg1, gu1)):
        hidden_grad = dot_nt(g, wd[...])
        a = jnp.concatenate([fa[0], fa[1]], axis=0).astype(f32)
        b = jnp.concatenate([fb[0], fb[1]], axis=0).astype(f32)
        gate_grad = (hidden_grad * b).astype(bf16)
        up_grad = (hidden_grad * a).astype(bf16)
        for j in range(2):
            here = slice(j * rows, (j + 1) * rows)
            gg[j], gu[j] = gate_grad[here], up_grad[here]
        add = dot(gate_grad, wgu[0]) + dot(up_grad, wgu[1])
        total = add if total is None else total + add
    for j in range(2):
        parts[j][...] = total[j * rows : (j + 1) * rows].astype(bf16)


def factor_of(v):
    return lax.rsqrt(jnp.mean(v * v, axis=-1, keepdims=True) + EPS)


def norm_back(v, r, gain, e):
    scaled = e * gain
    inner = jnp.mean(scaled * v, axis=-1, keepdims=True)
    grad = r * (scaled - v * (r * r * inner))
    return grad, jnp.sum(e * v * r, axis=0, keepdims=True)


def summed(*addends):
    total = addends[0][...].astype(f32)
    for a in addends[1:]:
        total = total + a[...].astype(f32)
    return total


def mid_kernel(latent, p0, near, far, gains, proj_out, mid_out, normed_out):
    proj = summed(p0, near, far)
    mid = latent[...] + proj * factor_of(proj) * gains[1:2, :]
    proj_out[...] = proj
    mid_out[...] = mid
    normed_out[...] = (mid * factor_of(mid) * gains[2:3, :]).astype(bf16)


def live_grad(seq, scal, cot):
    rows = cot.shape[0]
    row_id = lax.broadcasted_iota(jnp.int32, (rows, 1), 0) + scal[0] * rows
    return jnp.where(row_id < scal[1 + seq], cot[...].astype(f32), 0.0)


def out_kernel(seq, scal, mid, p0, near, cot, gains, out, grad_out, gain_out):
    proj = summed(p0, near)
    r = factor_of(proj)
    gain = gains[3:4, :]
    out[...] = (mid[...] + proj * r * gain).astype(bf16)
    grad, gain_grad = norm_back(proj, r, gain, live_grad(seq, scal, cot))
    grad_out[...] = grad.astype(bf16)
    gain_out[...] = gain_grad


def back_kernel(seq, scal, mid, proj, p0, near, cot, gains, mid_grad_out, grad_out, gain_two, gain_three):
    three = summed(p0, near)
    m = mid[...]
    part, g3 = norm_back(m, factor_of(m), gains[2:3, :], three)
    mid_grad = live_grad(seq, scal, cot) + part
    pr = proj[...]
    grad, g2 = norm_back(pr, factor_of(pr), gains[1:2, :], mid_grad)
    mid_grad_out[...] = mid_grad
    grad_out[...] = grad.astype(bf16)
    gain_two[...] = g2
    gain_three[...] = g3


def last_kernel(latent, p0, near, far, mid_grad, gains, grad_out, gain_out):
    one = summed(p0, near, far)
    la = latent[...]
    part, g1 = norm_back(la, factor_of(la), gains[0:1, :], one)
    grad_out[...] = (mid_grad[...] + part).astype(bf16)
    gain_out[...] = g1


def first_kernel(x, w, gains, *refs):
    outs, acc = refs[:-1], refs[-1]
    seqs = len(outs) // 2
    whole = dot(x[...], w[...])
    rows, tiles = acc.shape[1] // seqs, acc.shape[0]
    for c in range(tiles):
        acc[c] = whole[:, c * 128 : (c + 1) * 128]
    for s in range(seqs):
        latent = jnp.concatenate([acc[c, pl.ds(s, rows, stride=seqs), :] for c in range(tiles)], axis=1)
        outs[s][...] = latent
        outs[seqs + s][...] = (latent * factor_of(latent) * gains[0:1, :]).astype(bf16)


def reversed_bits(index, bits):
    out = 0
    for b in range(bits):
        out = out + (((index >> b) & 1) << (bits - 1 - b))
    return out


def pair_block(g, me, pairs):
    return (me[0] >> 1) ^ reversed_bits(g, pairs.bit_length() - 1)


def grad_call(kernel, me, fixed, sliced, out, pairs, scratch=()):
    rows, d = sliced[0].shape
    wide = d // pairs
    shape = pltpu.HBM((pairs,) + out, bf16)
    spec = pl.BlockSpec((1,) + out, lambda g, m: (g,) + (0,) * len(out))

    def full_map(a):
        return lambda g, m: (0,) * a.ndim

    return pl.pallas_call(
        kernel,
        out_shape=(shape, shape),
        grid_spec=pltpu.PrefetchScalarGridSpec(
            num_scalar_prefetch=1,
            grid=(pairs,),
            in_specs=[pl.BlockSpec(a.shape, full_map(a)) for a in fixed]
            + [pl.BlockSpec((rows, wide), lambda g, m: (0, pair_block(g, m, pairs))) for _ in sliced],
            out_specs=(spec, spec),
            scratch_shapes=list(scratch),
        ),
        compiler_params=pltpu.CompilerParams(vmem_limit_bytes=20 * MIB),
        cost_estimate=LIGHT,
        name="weight_grad",
    )(me, *[in_hbm(a) for a in fixed], *[in_hbm(a) for a in sliced])


def grad_rows(me, groups, dp, cols):
    pairs = dp // 2
    half = groups[0][0][0].shape[1] // dp
    fixed = [y for _, ys in groups for y in ys]
    sliced = [x for xs, _ in groups for x in xs]
    count = sum(ys[0].shape[-1] // cols for _, ys in groups)

    def kernel(me_ref, *refs):
        yr, xr, (keep, send) = refs[: len(fixed)], refs[len(fixed) : -2], refs[-2:]
        odd = (me_ref[0] & 1) == 1
        n = y0 = x0 = 0
        for group, (xs, ys) in enumerate(groups):
            lhs = jnp.concatenate([x[...] for x in xr[x0 : x0 + len(xs)]], axis=0)
            rhs = jnp.concatenate([y[b] for y in yr[y0 : y0 + len(ys)] for b in range(y.shape[0])], axis=0)
            x0, y0 = x0 + len(xs), y0 + len(ys)
            acc = dot_tn(lhs, rhs)
            stay = jnp.where(odd, acc[half:], acc[:half]).astype(bf16)
            go = jnp.where(odd, acc[:half], acc[half:]).astype(bf16)
            if group == len(groups) - 1:
                for ref, value in ((keep, stay), (send, go)):
                    value = value.T
                    for c in range(0, cols, half):
                        ref[0, n, :, c : c + half] = value[c : c + half]
                continue
            for c in range(0, acc.shape[1], cols):
                keep[0, n] = stay[:, c : c + cols]
                send[0, n] = go[:, c : c + cols]
                n += 1

    return grad_call(kernel, me, fixed, sliced, (count, half, cols), pairs)


def grad_units(me, sets, ys, dp, first):
    rows, d = ys[0].shape
    pairs = dp // 2
    wide = d // pairs
    half = wide // 2
    units = sets[0][0].shape[-1]
    quarter = units // 4
    tokens = len(ys) * rows
    count = len(sets[0])
    inner = pairs // 2

    def kernel(me_ref, *refs):
        xr, yr = refs[: 2 * count], refs[2 * count : 2 * count + len(ys)]
        keep, send0, send1, turned = refs[2 * count + len(ys) :]
        sends = (send0, send1)
        step = pl.program_id(0)

        @pl.when(step == 0)
        def _():
            for n in range(2):
                block = jnp.concatenate([x[b] for x in xr[n * count : (n + 1) * count] for b in range(x.shape[0])], axis=0).T
                if n == 0:
                    turned[:units, :] = block
                else:
                    for r in range(4):
                        base = pl.multiple_of(units + ((me_ref[0] & 3) ^ r) * quarter, quarter)
                        turned[pl.ds(base, quarter), :] = block[r * quarter : (r + 1) * quarter]

        acc = dot(turned[...], jnp.concatenate([y[...] for y in yr], axis=0))
        odd = (me_ref[0] & 1) == 1
        same = jnp.where(odd, acc[:, half:], acc[:, :half]).astype(bf16)
        other = jnp.where(odd, acc[:, :half], acc[:, half:]).astype(bf16)
        if first == "y":
            for x, part in ((0, same), (1, other)):
                keep[x, 0] = part[:units]
                sends[x][0] = part[units:]
        elif first == "x":
            for n in range(2):
                keep[0, n, 0] = same[n * units : (n + 1) * units]
            for ref, when in ((send0, step < inner), (send1, step >= inner)):

                @pl.when(when)
                def _():
                    for n in range(2):
                        ref[n, 0] = other[n * units : (n + 1) * units]
        else:

            @pl.when(step < inner)
            def _():
                for n in range(2):
                    keep[0, n, 0] = same[n * units : (n + 1) * units]
                    keep[1, n, 0] = other[n * units : (n + 1) * units]

            @pl.when(step >= inner)
            def _():
                for n in range(2):
                    sends[0][n, 0] = same[n * units : (n + 1) * units]
                    sends[1][n, 0] = other[n * units : (n + 1) * units]

    def early(g):
        return jnp.minimum(g, inner - 1)

    def late(g):
        return jnp.maximum(g - inner, 0)

    if first == "y":
        outs = [((2, pairs), (2, 1), lambda g, m: (0, g, 0, 0))] + [((pairs,), (1,), lambda g, m: (g, 0, 0))] * 2
    elif first == "x":
        outs = [
            ((2, 2, inner), (1, 2, 1), lambda g, m: (g // inner, 0, g % inner, 0, 0)),
            ((2, inner), (2, 1), lambda g, m: (0, early(g), 0, 0)),
            ((2, inner), (2, 1), lambda g, m: (0, late(g), 0, 0)),
        ]
    else:
        outs = [((2, 2, inner), (2, 2, 1), lambda g, m: (0, 0, early(g), 0, 0))] + [
            ((2, inner), (2, 1), lambda g, m: (0, late(g), 0, 0))
        ] * 2
    fixed = [a for one_set in sets for a in one_set]
    return pl.pallas_call(
        kernel,
        out_shape=tuple(pltpu.HBM(shape + (units, half), bf16) for shape, _, _ in outs),
        grid_spec=pltpu.PrefetchScalarGridSpec(
            num_scalar_prefetch=1,
            grid=(pairs,),
            in_specs=[pl.BlockSpec(a.shape, lambda g, m: (0, 0, 0)) for a in fixed]
            + [pl.BlockSpec((rows, wide), lambda g, m: (0, pair_block(g, m, pairs))) for _ in ys],
            out_specs=tuple(pl.BlockSpec(block + (units, half), f) for _, block, f in outs),
            scratch_shapes=[pltpu.VMEM((2 * units, tokens), bf16)],
        ),
        compiler_params=pltpu.CompilerParams(vmem_limit_bytes=20 * MIB),
        cost_estimate=LIGHT,
        name="grad_units",
    )(me, *[in_hbm(a) for a in fixed], *[in_hbm(a) for a in ys])


def grad_adapter(me, xs, grads, gains, dp):
    rows, joined = xs[0].shape
    width = grads[0].shape[1]
    wide = joined // dp
    part = wide // 4
    count = len(xs)

    def kernel(me_ref, *refs):
        xr, gr, (gain, keep, send, grad, acc) = refs[:count], refs[count : 2 * count], refs[2 * count :]

        @pl.when(pl.program_id(0) == 0)
        def _():
            for n in range(count):
                grad[n * rows : (n + 1) * rows, :] = gr[n][...]

        acc[...] = dot_tn(jnp.concatenate([x[...] for x in xr], axis=0), grad[...])
        rest = jnp.zeros((8, width - 128), bf16)
        extra = jnp.concatenate([gain[...].astype(bf16), rest], axis=1)
        for far in (0, 1):
            for near, ref in ((0, keep), (1, send)):
                base = pl.multiple_of((me_ref[1] ^ (2 * far + near)) * part, part)
                ref[far, 0, :part, :] = acc[pl.ds(base, part), :].astype(bf16)
                ref[far, 0, part:, :] = extra

    shape = jax.ShapeDtypeStruct((2, dp, part + 8, width), bf16)
    spec = pl.BlockSpec((2, 1, part + 8, width), lambda g, m: (0, g, 0, 0))
    return pl.pallas_call(
        kernel,
        out_shape=(shape, shape),
        grid_spec=pltpu.PrefetchScalarGridSpec(
            num_scalar_prefetch=1,
            grid=(dp,),
            in_specs=[pl.BlockSpec((rows, wide), lambda g, m: (0, m[0] ^ g)) for _ in xs]
            + [pl.BlockSpec((rows, width), lambda g, m: (0, 0)) for _ in grads]
            + [pl.BlockSpec((8, 128), lambda g, m: (0, m[0] ^ g))],
            out_specs=(spec, spec),
            scratch_shapes=[pltpu.VMEM((count * rows, width), bf16), pltpu.VMEM((wide, width), f32)],
        ),
        compiler_params=pltpu.CompilerParams(vmem_limit_bytes=20 * MIB),
        cost_estimate=LIGHT,
        name="grad_adapter",
    )(me, *[in_hbm(x) for x in xs], *grads, gains)


def plus(a, *others):
    total = a.astype(f32)
    for o in others:
        total = total + o.astype(f32)
    return total


def low(a, *others):
    return plus(a, *others).astype(bf16)


def body(adapter_in, lengths, cotangent, adapter_weight, gains, qkv_weight, out_weight, gate_up_weight, down_weight):
    rows, seqs = adapter_in.shape[0], adapter_in.shape[1]
    width = adapter_weight.shape[1]
    cols = qkv_weight.shape[2]
    heads = cols // HD
    units = down_weight.shape[0]
    members = lax.axis_size("tensor")
    dp = lax.axis_size("dp")
    seq_len = rows * members
    fast = dp == 8 and (width // dp) % 128 == 0
    mine = lax.axis_index("tensor").astype(jnp.int32)
    me = lax.axis_index("dp").astype(jnp.int32).reshape(1)
    scal = jnp.concatenate([mine.reshape(1), lengths])

    lane = jnp.arange(HD, dtype=jnp.int32) % (HD // 2)
    freq = THETA ** (-(lane.astype(f32) * 2.0 / HD))
    inner = jnp.arange(rows, dtype=jnp.int32).astype(f32)[:, None] * freq[None, :]
    owner = (mine ^ jnp.arange(members, dtype=jnp.int32)) * rows
    outer = owner.astype(f32)[:, None] * freq[None, :]
    turn_rows = jnp.stack([jnp.cos(inner), jnp.sin(inner)])
    turn_blocks = jnp.stack([jnp.cos(outer), jnp.sin(outer)])

    every = range(seqs)
    x_in = adapter_in.reshape(rows * seqs, -1)
    x_first = x_in
    tok = (rows, width)

    def parts(n):
        return [(tok, bf16)] * n

    gain = {}

    clock = [None]

    def gate(x):
        return x if clock[0] is None else after(x, clock[0])

    def close(*values):
        values = lax.optimization_barrier(tuple(values))
        clock[0] = values[0]
        return values

    moves = {"c": ("tensor", 1), "y": ("tensor", 2), "x": ("dp", 1), "z": ("dp", 2), "w": ("dp", 4)}

    def go(x, m):
        return swap(gate(x), *moves[m])

    def hop(x):
        return swap(x, "tensor", 1)

    place = me[0] & 3
    w_gu = gate_up_weight.transpose(1, 2, 0)
    w_qkv = qkv_weight.transpose(1, 0, 2)
    quarter = units // 4
    gu0 = swap(lax.dynamic_slice_in_dim(w_gu, place * quarter, quarter, 1), "tensor", 2)
    latent_a, latent_b, normed_a, normed_b = whole_call(
        first_kernel,
        [(tok, f32, True)] * seqs + [(tok, bf16)] * seqs,
        [],
        [in_hbm(x_in), in_hbm(adapter_weight), gains],
        scratch=[pltpu.VMEM((width // 128, rows * seqs, 128), f32)],
        vmem=24,
        name="first",
    )
    latent = [latent_a, latent_b]
    normed_a, normed_b, gu0, turn_rows, turn_blocks = close(normed_a, normed_b, gu0, turn_rows, turn_blocks)

    far_a, near_a = go(normed_a, "y"), go(normed_a, "c")
    d0 = go(lax.dynamic_slice_in_dim(down_weight, place * quarter, quarter, 0), "y")
    gu1, gu2 = go(gu0, "x"), go(gu0, "z")
    early = gate(cotangent)
    cot = [early[:, s] for s in every]
    tokens_of = gate(adapter_in)
    tokens_of = [tokens_of[:, s] for s in every]
    far_a, near_a, d0, gu1, gu2, *both = close(far_a, near_a, d0, gu1, gu2, *cot, *tokens_of)
    cot, tokens_of = both[:seqs], both[seqs:]

    head_shape = ((heads, seq_len, HD), bf16, True)

    def attn_fwd(s, blocks):
        *kept, at, p0, p1, p2, p3 = whole_call(
            functools.partial(attn_fwd_kernel, s),
            [head_shape] * 4 + [((8, seq_len), f32, True), ((members, rows, cols), bf16, True)] + parts(4),
            [scal],
            [*blocks, w_qkv, turn_rows, turn_blocks, out_weight],
            vmem=20,
            name="attn_fwd",
        )
        return kept, at, p0, p1, p2, p3

    far_b, near_b = go(normed_b, "y"), go(normed_b, "c")
    gu3, d2 = go(gu2, "x"), go(d0, "z")
    one = {0: [normed_a, near_a, far_a, hop(far_a)]}
    qkvo, att = {}, {}
    qkvo[0], att[0], *sums = attn_fwd(0, one[0])
    p0, p1, p2, p3, far_b, near_b, gu3, d2 = close(*sums, far_b, near_b, gu3, d2)
    across_a, own_a, p1 = close(low(p2, hop(p3)), p0, p1)

    far_a, d1, near_a = go(across_a, "y"), go(d0, "x"), go(p1, "c")
    one[1] = [gate(normed_b), near_b, far_b, hop(far_b)]
    qkvo[1], att[1], *sums = attn_fwd(1, one[1])
    p0, p1, p2, p3, far_a, d1, near_a = close(*sums, far_a, d1, near_a)
    across_b, own_b, p1 = close(low(p2, hop(p3)), p0, p1)

    far_b, d3, near_b = go(across_b, "y"), go(d1, "z"), go(p1, "c")
    far_gu = jnp.concatenate([gate(gu0), gu1, gu2, gu3], axis=1)

    def mid_of(s, *addends):
        return whole_call(
            mid_kernel,
            [(tok, f32, True), (tok, f32, True), (tok, bf16)],
            [],
            [gate(latent[s]), *addends, gains],
            vmem=8,
            name="mid",
        )

    proj, mid, three, ffn, block_out, mlp_g, gu_g = {}, {}, {}, {}, {}, {}, {}
    proj[0], mid[0], own = mid_of(0, own_a, near_a, far_a)
    three[0] = [own, hop(own)]
    far_b, near_b, d3, far_gu, t0, t1 = close(far_b, near_b, d3, far_gu, *three[0])
    three[0] = [t0, t1]

    far_d = jnp.concatenate([gate(d0), d1, d2, d3], axis=0)
    mlp_weights = [w_gu, far_gu, down_weight, far_d]
    hid_shape = ((2, rows, units), bf16, True)

    def ffn_fwd(s):
        *ffn[s], p0, p1 = whole_call(
            mlp_fwd_kernel, [hid_shape] * 6 + parts(2), [], [*three[s], *mlp_weights], vmem=36, name="mlp_fwd"
        )
        return p0, hop(p1)

    def out_of(s, *addends):
        block_out[s], own, gain[3, s] = whole_call(
            functools.partial(out_kernel, s),
            [(tok, bf16, True), (tok, bf16), ((1, width), f32)],
            [scal],
            [mid[s], *addends, cot[s], gains],
            vmem=10,
            name="out",
        )
        mlp_g[s] = [own, hop(own)]

    def ffn_bwd(s):
        *gu_g[s], p0, p1 = whole_call(
            mlp_bwd_kernel,
            [hid_shape] * 4 + parts(2),
            [],
            [*mlp_g[s], *mlp_weights, *ffn[s][1:3], *ffn[s][4:6]],
            vmem=36,
            name="mlp_bwd",
        )
        return p0, p1

    mid_grad, attn_g, stacked = {}, {}, {}

    def back_of(s, *addends):
        mid_grad[s], own, gain[1, s], gain[2, s] = whole_call(
            functools.partial(back_kernel, s),
            [(tok, f32, True), (tok, bf16), ((1, width), f32), ((1, width), f32)],
            [scal],
            [mid[s], proj[s], *addends, cot[s], gains],
            vmem=12,
            name="back",
        )
        return own

    sum_a = ffn_fwd(0)
    proj[1], mid[1], own = mid_of(1, own_b, near_b, far_b)
    three[1] = [own, hop(own)]
    out_of(0, *sum_a)
    sum_b = ffn_fwd(1)
    p0, p1 = ffn_bwd(0)
    sum_a = p0, hop(p1)
    out_of(1, *sum_b)
    grad_a = back_of(0, *sum_a)
    grad_a, b0, b1 = close(grad_a, *mlp_g[1])
    mlp_g[1] = [b0, b1]

    def full_grad(xs, ys):
        xs, ys = [jnp.concatenate([a.reshape(-1, a.shape[-1]) for a in part], 0) for part in (xs, ys)]
        return lax.dot_general(xs, ys, (((0,), (0,)), ((), ())), preferred_element_type=f32).astype(bf16)

    def unit_grad(sets, ys, first):
        ys = [gate(ys[0]), *ys[1:]]
        if fast:
            keep, send0, send1 = grad_units(me, sets, ys, dp, first)
            split = (2, 2) + keep.shape[-2:]
            return keep.reshape((2,) + split), send0.reshape(split), send1.reshape(split)
        own, far = [full_grad(xs, ys) for xs in sets]
        far = jnp.concatenate([lax.dynamic_slice_in_dim(far, (place ^ a) * quarter, quarter, 0) for a in range(4)], axis=0)
        total = low(own, swap(far, "tensor", 2))
        return lax.psum_scatter(total, "dp", scatter_dimension=1, tiled=True).astype(f32)

    far_a, near_a = go(grad_a, "y"), go(grad_a, "c")
    sum_b = ffn_bwd(1)
    flat_three = [b for s in every for b in three[s]]
    flat_mlp = [b for s in every for b in mlp_g[s]]
    flat_one = [b for s in every for b in one[s]]
    hiddens = [[ffn[s][3 * n] for s in every] for n in (0, 1)]
    gates = [[gu_g[s][2 * n] for s in every] for n in (0, 1)]
    ups = [[gu_g[s][2 * n + 1] for s in every] for n in (0, 1)]

    if fast:
        down_keep, down0, down1 = unit_grad(hiddens, flat_mlp, "x")
        p0, p1, far_a, near_a, down0, down1 = close(*sum_b, far_a, near_a, down0, down1)
    else:
        p0, p1, far_a, near_a = close(*sum_b, far_a, near_a)
    grad_b = close(back_of(1, p0, hop(p1)))[0]


    head_f32 = (heads, seq_len, HD)

    def attn_bwd(s, blocks):
        stacked[s], p0, p1, p2, p3 = whole_call(
            functools.partial(attn_bwd_kernel, s),
            [((members, rows, 3 * cols), bf16, True)] + parts(4),
            [scal],
            [*blocks, out_weight, *qkvo[s], turn_rows, turn_blocks, w_qkv],
            scratch=[pltpu.VMEM(head_f32, bf16)] + [pltpu.VMEM(head_f32, f32)] * 3,
            vmem=24,
            name="attn_bwd",
        )
        return p0, p1, p2, p3

    far_b, near_b = go(grad_b, "y"), go(grad_b, "c")
    attn_g[0] = [gate(grad_a), near_a, far_a, hop(far_a)]
    sums = attn_bwd(0, attn_g[0])
    if fast:
        down_got1 = go(down1, "x")
        gate_keep, gate0, gate1 = unit_grad(gates, flat_three, "z")
        p0, p1, p2, p3, far_b, near_b, gate0, gate1, down_got1 = close(*sums, far_b, near_b, gate0, gate1, down_got1)
    else:
        p0, p1, p2, p3, far_b, near_b = close(*sums, far_b, near_b)
    across_a, own_a, p1 = close(low(p2, hop(p3)), p0, p1)

    far_a, near_a = go(across_a, "y"), go(p1, "c")
    attn_g[1] = [gate(grad_b), near_b, far_b, hop(far_b)]
    sums = attn_bwd(1, attn_g[1])
    if fast:
        down_got0, gate_got1 = go(down0, "x"), go(gate1, "z")
        up_keep, up0, up1 = unit_grad(ups, flat_three, "y")
        p0, p1, p2, p3, far_a, near_a, down_got0, gate_got1, up0, up1 = close(
            *sums, far_a, near_a, down_got0, gate_got1, up0, up1
        )
    else:
        p0, p1, p2, p3, far_a, near_a = close(*sums, far_a, near_a)
    across_b, own_b, p1 = close(low(p2, hop(p3)), p0, p1)

    latent_grad = {}

    def last_of(s, *addends):
        latent_grad[s], gain[0, s] = whole_call(
            last_kernel,
            [(tok, bf16), ((1, width), f32)],
            [],
            [gate(latent[s]), *addends, mid_grad[s], gains],
            vmem=10,
            name="last",
        )

    both_me = jnp.concatenate([me, mine.reshape(1)])

    far_b, near_b = go(across_b, "y"), go(p1, "c")
    last_of(0, own_a, near_a, far_a)
    flat_attn = [b for s in every for b in attn_g[s]]
    if fast:
        gate_got0 = go(gate0, "z")
        down_next = low(gate(down_keep)[1], down_got1)
        gate_got2 = swap(low(gate(gate_keep)[1], gate_got1), *moves["x"])
        down_stay = low(gate(down_keep)[0], down_got0)
        first = [gate(flat_one[0]), *flat_one[1:]]
        attn_keep, attn_send = grad_rows(
            me, [(first, [stacked[s] for s in every]), (flat_attn, [att[s] for s in every])], dp, cols
        )
        lead = (2, 2) + attn_keep.shape[1:]
        half = width // dp
        attn_keep, attn_send = attn_keep.reshape(lead), attn_send.reshape(lead)
        far_b, near_b, attn_send, gate_got0, gate_got2, down_next, down_stay = close(
            far_b, near_b, attn_send, gate_got0, gate_got2, down_next, down_stay
        )
    else:
        far_b, near_b = close(far_b, near_b)

    last_of(1, own_b, near_b, far_b)
    grads = [latent_grad[s] for s in every]
    d_gains = jnp.concatenate([sum(gain[g, s] for s in every) for g in range(4)], axis=0)
    if fast:
        up_got1, attn_got, down_got2 = go(up1, "y"), go(attn_send, "x"), go(down_next, "z")
        gate2 = low(low(gate(gate_keep)[0], gate_got0), gate_got2)
        gate_got3 = swap(gate2[1], *moves["y"])
        d_gains = jnp.concatenate([d_gains, jnp.zeros_like(d_gains)], axis=0)
        keep, send = grad_adapter(both_me, tokens_of, grads, d_gains, dp)
        send, up_got1, attn_got, gate_got3, down_got2 = close(send, up_got1, attn_got, gate_got3, down_got2)
        total = close(low(keep, hop(send)))[0]

        part = total.shape[-2]
        ranges = total.reshape(2, 2, 2, 2, part, width)
        orders = ["zxyw", "yxzw"]
        cut = width * 5 // 8
        axes = ["ywzx"] * 2
        state = [ranges[..., :cut], ranges[..., cut:]]

        def adapter_round(r, state):
            kept, got = [], []
            for n in range(2):
                m = orders[n][r]
                at = axes[n].index(m)
                axes[n] = axes[n].replace(m, "")
                kept.append(lax.index_in_dim(state[n], 0, at, keepdims=False))
                got.append(swap(lax.index_in_dim(state[n], 1, at, keepdims=False), *moves[m]))
            return kept, got

        up_got0 = go(up0, "y")
        up_got2 = swap(low(gate(up_keep)[1], up_got1), *moves["x"])
        kept, got = adapter_round(0, state)
        attn = low(gate(attn_keep), attn_got)
        attn_got = swap(attn[:, 1], *moves["w"])
        gate3 = low(gate(gate2[0]), gate_got3)
        grad_in = [
            lax.dot_general(gate(g), adapter_weight, (((1,), (1,)), ((), ())), preferred_element_type=f32).astype(bf16)
            for g in grads
        ]
        out = jnp.stack([gate(block_out[s]) for s in every], axis=1)
        down2 = low(gate(down_stay), down_got2)
        got0, got1, up_got0, up_got2, attn_got, out, down2 = close(*got, up_got0, up_got2, attn_got, out, down2)

        down_got3, gate_got4 = go(down2[1], "y"), go(gate3[1], "w")
        state = [low(k, g) for k, g in zip(kept, (got0, got1))]
        both_x = [[lax.index_in_dim(state[n], i, 2, keepdims=False) for n in range(2)] for i in (0, 1)]
        kept = both_x[0]
        got = [swap(jnp.concatenate(both_x[1], axis=-1), *moves["x"])]
        axes = ["yw", "wz"]
        up2 = low(low(gate(up_keep)[0], up_got0), up_got2)
        up_got3 = swap(up2[1], *moves["z"])
        attn = low(gate(attn)[:, 0], attn_got)
        attn_got = swap(attn[1], *moves["z"])
        got0, up_got3, attn_got, down_got3, gate_got4 = close(*got, up_got3, attn_got, down_got3, gate_got4)
        got0, got1 = got0[..., :cut], got0[..., cut:]

        down3 = low(gate(down2[0]), down_got3)
        down_got4 = swap(down3[1], *moves["w"])
        d_gate = plus(gate(gate3[0]), gate_got4)
        state = [low(k, g) for k, g in zip(kept, (got0, got1))]
        kept, got = adapter_round(2, state)
        up3 = low(gate(up2[0]), up_got3)
        up_got4 = swap(up3[1], *moves["w"])
        attn = plus(gate(attn[0]), attn_got)
        got0, got1, up_got4, down_got4, attn, d_gate = close(*got, up_got4, down_got4, attn, d_gate)

        state = [low(k, g) for k, g in zip(kept, (got0, got1))]
        kept, got = adapter_round(3, state)
        d_up = plus(gate(up3[0]), up_got4)
        d_down = plus(gate(down3[0]), down_got4)
        rows_out = part - 8
        d_adapt = jnp.concatenate([plus(k[:rows_out], g[:rows_out]) for k, g in zip(kept, got)], axis=-1)
        d_gains = plus(kept[0][rows_out : rows_out + 4, :128], got[0][rows_out : rows_out + 4, :128])
        share = 128 // members
        d_gains = lax.dynamic_slice_in_dim(d_gains, mine * share, share, 1)
        d_qkv = attn[:3].transpose(1, 0, 2)
        d_out = jnp.concatenate([attn[3, :, :half], attn[3, :, half:]], axis=0)
    else:
        out = jnp.stack([block_out[s] for s in every], axis=1)
        share = width // (dp * members)
        d_gains = lax.psum(d_gains, ("dp", "tensor"))
        d_gains = lax.dynamic_slice_in_dim(d_gains, (me[0] * members + mine) * share, share, 1)
        d_down = unit_grad(hiddens, flat_mlp, "z")
        d_gate = unit_grad(gates, flat_three, "x")
        d_up = unit_grad(ups, flat_three, "y")

        def reduced(xs, ys, dim):
            return lax.psum_scatter(full_grad(xs, ys), "dp", scatter_dimension=dim, tiled=True).astype(f32)

        d_qkv = reduced(flat_one, [stacked[s] for s in every], 0).reshape(-1, 3, cols)
        d_out = reduced([att[s] for s in every], flat_attn, 1)
        full = full_grad([tokens_of[s] for s in every], grads).astype(f32)
        d_adapt = lax.psum_scatter(full, ("dp", "tensor"), scatter_dimension=0, tiled=True)
        grad_in = [
            lax.dot_general(g, adapter_weight, (((1,), (1,)), ((), ())), preferred_element_type=f32).astype(bf16)
            for g in grads
        ]
    grad_in = jnp.stack(grad_in, axis=1)
    d_gate_up = jnp.stack([d_gate, d_up]).transpose(2, 0, 1)
    return (out, grad_in, d_adapt, d_gains, d_qkv, d_out, d_gate_up, d_down)


def solution(mesh):
    return jax.shard_map(
        body,
        mesh=mesh,
        in_specs=(
            P("tensor", "dp", None),
            P("dp"),
            P("tensor", "dp", None),
            P(),
            P(),
            P(None, None, "tensor"),
            P("tensor", None),
            P(None, None, "tensor"),
            P("tensor", None),
        ),
        out_specs=(
            P("tensor", "dp", None),
            P("tensor", "dp", None),
            P(("dp", "tensor"), None),
            P(None, ("dp", "tensor")),
            P("dp", None, "tensor"),
            P("tensor", "dp"),
            P("dp", None, "tensor"),
            P("tensor", "dp"),
        ),
        check_vma=False,
    )
```

```python
import functools

import jax
import jax.numpy as jnp
import numpy as np
from jax import lax
from jax.experimental import pallas as pl
from jax.experimental.pallas import tpu as pltpu
from jax.sharding import PartitionSpec as P

HD = 128
LOG2E = 1.4426950408889634
EPS = 1e-06
THETA = 50000.0
MASKED = -1e30
f32 = jnp.float32
bf16 = jnp.bfloat16
MIB = 1024 * 1024
LIGHT = pl.CostEstimate(flops=1, bytes_accessed=1, transcendentals=0)


def dot(a, b):
    return jnp.dot(a, b, preferred_element_type=f32)


def dot_nt(a, b):
    return lax.dot_general(a, b, (((1,), (1,)), ((), ())), preferred_element_type=f32)


def dot_tn(a, b):
    return lax.dot_general(a, b, (((0,), (0,)), ((), ())), preferred_element_type=f32)


def full_map(rank):
    return lambda *_: (0,) * rank


def whole_call(kernel, outs, scalars, arrays, scratch=(), vmem=40, name=None):
    smem = pl.BlockSpec(memory_space=pltpu.SMEM)
    vm = pl.BlockSpec(memory_space=pltpu.VMEM)
    return pl.pallas_call(
        kernel,
        out_shape=tuple(pltpu.HBM(o[0], o[1]) if len(o) > 2 else jax.ShapeDtypeStruct(*o) for o in outs),
        in_specs=[smem] * len(scalars) + [vm] * len(arrays),
        out_specs=tuple(pl.BlockSpec(o[0], full_map(len(o[0]))) if len(o) > 2 else vm for o in outs),
        scratch_shapes=list(scratch),
        compiler_params=pltpu.CompilerParams(vmem_limit_bytes=vmem * MIB),
        cost_estimate=LIGHT,
        name=name,
    )(*scalars, *arrays)


def swap(x, axis, bit):
    n = lax.axis_size(axis)
    return lax.ppermute(x, axis, [(i, i ^ bit) for i in range(n)])


def gather_blocks(x):
    far = swap(x, "tensor", 2)
    near = swap(x, "tensor", 1)
    return [x, near, far, swap(far, "tensor", 1)]


def scatter_blocks(p0, p1, p2, p3):
    near = swap(p1, "tensor", 1)
    across = (p2.astype(f32) + swap(p3, "tensor", 1).astype(f32)).astype(bf16)
    return across, (p0, near, swap(across, "tensor", 2))


def in_hbm(x):
    return pltpu.with_memory_space_constraint(x, pltpu.HBM)


def after(x, *others):
    return lax.optimization_barrier((x,) + others)[0]


def turn_tables(turn_rows, turn_blocks, j):
    cr, sr = turn_rows[0], turn_rows[1]
    cb, sb = turn_blocks[0, j : j + 1, :], turn_blocks[1, j : j + 1, :]
    sign = jnp.where(lax.broadcasted_iota(jnp.int32, (1, HD), 1) < HD // 2, -1.0, 1.0)
    return cb * cr - sb * sr, (sb * cr + cb * sr) * sign


def attn_fwd_kernel(seq, scal, x0, x1, x2, x3, w, turn_rows, turn_blocks, wo, q, k, v, o, lse, att, *parts):
    mine, length = scal[0], scal[1 + seq]
    rows = x0.shape[0]
    heads = q.shape[0]
    for j, x in enumerate((x0, x1, x2, x3)):
        base = pl.multiple_of((mine ^ j) * rows, rows)
        c, s = turn_tables(turn_rows, turn_blocks, j)
        for n, ref in ((0, q), (1, k)):
            acc = dot(x[...], w[n])
            for h in range(heads):
                part = acc[:, h * HD : (h + 1) * HD]
                turned = part * c + pltpu.roll(part, HD // 2, 1) * s
                ref[h, pl.ds(base, rows), :] = turned.astype(bf16)
        acc = dot(x[...], w[2]).astype(bf16)
        for h in range(heads):
            v[h, pl.ds(base, rows), :] = acc[:, h * HD : (h + 1) * HD]
    factor = HD**-0.5 * LOG2E

    @pl.loop(0, heads)
    def _(h):
        vt = v[h].T
        for i in range(4):
            keys = (i + 1) * rows
            st = dot_nt(k[h, :keys, :], q[h, i * rows : keys, :]) * factor
            key_id = lax.broadcasted_iota(jnp.int32, st.shape, 0)
            row_id = lax.broadcasted_iota(jnp.int32, st.shape, 1) + i * rows
            st = jnp.where((key_id <= row_id) & (key_id < length), st, MASKED)
            top = jnp.max(st, axis=0, keepdims=True)
            weights = jnp.exp2(st - top)
            total = jnp.sum(weights, axis=0, keepdims=True)
            ot = dot(vt[:, :keys], weights.astype(bf16)) / total
            o[h, i * rows : keys, :] = ot.T.astype(bf16)
            lse[pl.ds(h, 1), i * rows : keys] = top + jnp.log2(total)

    for j in range(4):
        base = pl.multiple_of((mine ^ j) * rows, rows)
        both = jnp.concatenate([o[h, pl.ds(base, rows), :] for h in range(heads)], axis=1)
        att[j] = both
        parts[j][...] = dot(both, wo[...]).astype(bf16)


def attn_bwd_kernel(
    seq, scal, g0, g1, g2, g3, wo, q, k, v, o, lse, turn_rows, turn_blocks, w, st_out, p0, p1, p2, p3, dout, dq, dk, dv
):
    parts = (p0, p1, p2, p3)
    mine, length = scal[0], scal[1 + seq]
    rows = g0.shape[0]
    heads = q.shape[0]
    cols = heads * HD
    for j, g in enumerate((g0, g1, g2, g3)):
        mixed = dot_nt(g[...], wo[...]).astype(bf16)
        base = pl.multiple_of((mine ^ j) * rows, rows)
        for h in range(heads):
            dout[h, pl.ds(base, rows), :] = mixed[:, h * HD : (h + 1) * HD]
    scale = HD**-0.5
    factor = scale * LOG2E
    ones = jnp.ones((8, HD), f32)
    for h in range(heads):
        for i in (3, 2, 1, 0):
            keys = (i + 1) * rows
            here = slice(i * rows, keys)
            qi, di = q[h, here, :], dout[h, here, :]
            st = dot_nt(k[h, :keys, :], qi) * factor
            key_id = lax.broadcasted_iota(jnp.int32, st.shape, 0)
            row_id = lax.broadcasted_iota(jnp.int32, st.shape, 1) + i * rows
            st = jnp.where((key_id <= row_id) & (key_id < length), st, MASKED)
            probs = jnp.exp2(st - lse[h : h + 1, here])
            prob_grad = dot_nt(v[h, :keys, :], di)
            product = di.astype(f32) * o[h, here, :].astype(f32)
            inner = lax.dot_general(
                ones, product, (((1,), (1,)), ((), ())), precision=lax.Precision.HIGHEST, preferred_element_type=f32
            )[0:1, :]
            sg = (probs * (prob_grad - inner)).astype(bf16)
            new_v = dot(probs.astype(bf16), di)
            new_k = dot(sg, qi)
            if i == 3:
                dv[h] = new_v
                dk[h] = new_k
            else:
                dv[h, :keys, :] += new_v
                dk[h, :keys, :] += new_k
            dq[h, here, :] = dot_tn(sg, k[h, :keys, :])
    for j in range(4):
        base = pl.multiple_of((mine ^ j) * rows, rows)
        c, s = turn_tables(turn_rows, turn_blocks, j)
        c, s = c * scale, s * scale
        total = None
        for n, ref in enumerate((dq, dk, dv)):
            pieces = []
            for h in range(heads):
                part = ref[h, pl.ds(base, rows), :]
                if n < 2:
                    part = part * c - pltpu.roll(part, HD // 2, 1) * s
                pieces.append(part.astype(bf16))
            piece = jnp.concatenate(pieces, axis=1)
            st_out[j, :, n * cols : (n + 1) * cols] = piece
            add = dot_nt(piece, w[n])
            total = add if total is None else total + add
        parts[j][...] = total.astype(bf16)


def mlp_fwd_kernel(x0, x1, wgu0, wgu1, wd0, wd1, *outs):
    kept, parts = outs[:6], outs[6:]
    rows = x0.shape[0]
    x = jnp.concatenate([x0[...], x1[...]], axis=0)
    total = None
    for n, (wgu, wd) in enumerate(((wgu0, wd0), (wgu1, wd1))):
        hid, fa, fb = kept[3 * n : 3 * n + 3]
        gate = dot_nt(x, wgu[0])
        up = dot_nt(x, wgu[1])
        sig = jax.nn.sigmoid(gate)
        act = gate * sig
        hidden = (act * up).astype(bf16)
        a = act.astype(bf16)
        b = (up * sig * (1.0 + gate * (1.0 - sig))).astype(bf16)
        for j in range(2):
            here = slice(j * rows, (j + 1) * rows)
            hid[j], fa[j], fb[j] = hidden[here], a[here], b[here]
        add = dot(hidden, wd[...])
        total = add if total is None else total + add
    for j in range(2):
        parts[j][...] = total[j * rows : (j + 1) * rows].astype(bf16)


def mlp_bwd_kernel(g0, g1, wgu0, wgu1, wd0, wd1, fa0, fb0, fa1, fb1, gg0, gu0, gg1, gu1, *parts):
    rows = g0.shape[0]
    g = jnp.concatenate([g0[...], g1[...]], axis=0)
    total = None
    for wgu, wd, fa, fb, gg, gu in ((wgu0, wd0, fa0, fb0, gg0, gu0), (wgu1, wd1, fa1, fb1, gg1, gu1)):
        hidden_grad = dot_nt(g, wd[...])
        a = jnp.concatenate([fa[0], fa[1]], axis=0).astype(f32)
        b = jnp.concatenate([fb[0], fb[1]], axis=0).astype(f32)
        gate_grad = (hidden_grad * b).astype(bf16)
        up_grad = (hidden_grad * a).astype(bf16)
        for j in range(2):
            here = slice(j * rows, (j + 1) * rows)
            gg[j], gu[j] = gate_grad[here], up_grad[here]
        add = dot(gate_grad, wgu[0]) + dot(up_grad, wgu[1])
        total = add if total is None else total + add
    for j in range(2):
        parts[j][...] = total[j * rows : (j + 1) * rows].astype(bf16)


def factor_of(v):
    return lax.rsqrt(jnp.mean(v * v, axis=-1, keepdims=True) + EPS)


def norm_back(v, r, gain, e):
    scaled = e * gain
    inner = jnp.mean(scaled * v, axis=-1, keepdims=True)
    grad = r * (scaled - v * (r * r * inner))
    return grad, jnp.sum(e * v * r, axis=0, keepdims=True)


def summed(*addends):
    total = addends[0][...].astype(f32)
    for a in addends[1:]:
        total = total + a[...].astype(f32)
    return total


def mid_kernel(latent, p0, near, far, gains, proj_out, mid_out, normed_out):
    proj = summed(p0, near, far)
    mid = latent[...] + proj * factor_of(proj) * gains[1:2, :]
    proj_out[...] = proj
    mid_out[...] = mid
    normed_out[...] = (mid * factor_of(mid) * gains[2:3, :]).astype(bf16)


def live_grad(seq, scal, cot):
    rows = cot.shape[0]
    row_id = lax.broadcasted_iota(jnp.int32, (rows, 1), 0) + scal[0] * rows
    return jnp.where(row_id < scal[1 + seq], cot[...].astype(f32), 0.0)


def out_kernel(seq, scal, mid, p0, near, cot, gains, out, grad_out, gain_out):
    proj = summed(p0, near)
    r = factor_of(proj)
    gain = gains[3:4, :]
    out[...] = (mid[...] + proj * r * gain).astype(bf16)
    grad, gain_grad = norm_back(proj, r, gain, live_grad(seq, scal, cot))
    grad_out[...] = grad.astype(bf16)
    gain_out[...] = gain_grad


def back_kernel(seq, scal, mid, proj, p0, near, cot, gains, mid_grad_out, grad_out, gain_two, gain_three):
    three = summed(p0, near)
    m = mid[...]
    part, g3 = norm_back(m, factor_of(m), gains[2:3, :], three)
    mid_grad = live_grad(seq, scal, cot) + part
    pr = proj[...]
    grad, g2 = norm_back(pr, factor_of(pr), gains[1:2, :], mid_grad)
    mid_grad_out[...] = mid_grad
    grad_out[...] = grad.astype(bf16)
    gain_two[...] = g2
    gain_three[...] = g3


def last_kernel(latent, p0, near, far, mid_grad, gains, grad_out, gain_out):
    one = summed(p0, near, far)
    la = latent[...]
    part, g1 = norm_back(la, factor_of(la), gains[0:1, :], one)
    grad_out[...] = (mid_grad[...] + part).astype(bf16)
    gain_out[...] = g1


def first_kernel(x, w, gains, *refs):
    outs, acc = refs[:-1], refs[-1]
    seqs = len(outs) // 2
    whole = dot(x[...], w[...])
    rows, tiles = acc.shape[1] // seqs, acc.shape[0]
    for c in range(tiles):
        acc[c] = whole[:, c * 128 : (c + 1) * 128]
    for s in range(seqs):
        latent = jnp.concatenate([acc[c, pl.ds(s, rows, stride=seqs), :] for c in range(tiles)], axis=1)
        outs[s][...] = latent
        outs[seqs + s][...] = (latent * factor_of(latent) * gains[0:1, :]).astype(bf16)


def reversed_bits(index, bits):
    out = 0
    for b in range(bits):
        out = out + (((index >> b) & 1) << (bits - 1 - b))
    return out


def pair_block(g, me, pairs):
    return (me[0] >> 1) ^ reversed_bits(g, pairs.bit_length() - 1)


def grad_call(kernel, me, fixed, sliced, out, pairs, scratch=()):
    rows, d = sliced[0].shape
    wide = d // pairs
    shape = pltpu.HBM((pairs,) + out, bf16)
    spec = pl.BlockSpec((1,) + out, lambda g, m: (g,) + (0,) * len(out))

    def full_map(a):
        return lambda g, m: (0,) * a.ndim

    return pl.pallas_call(
        kernel,
        out_shape=(shape, shape),
        grid_spec=pltpu.PrefetchScalarGridSpec(
            num_scalar_prefetch=1,
            grid=(pairs,),
            in_specs=[pl.BlockSpec(a.shape, full_map(a)) for a in fixed]
            + [pl.BlockSpec((rows, wide), lambda g, m: (0, pair_block(g, m, pairs))) for _ in sliced],
            out_specs=(spec, spec),
            scratch_shapes=list(scratch),
        ),
        compiler_params=pltpu.CompilerParams(vmem_limit_bytes=20 * MIB),
        cost_estimate=LIGHT,
        name="weight_grad",
    )(me, *[in_hbm(a) for a in fixed], *[in_hbm(a) for a in sliced])


def grad_rows(me, groups, dp, cols):
    pairs = dp // 2
    half = groups[0][0][0].shape[1] // dp
    fixed = [y for _, ys in groups for y in ys]
    sliced = [x for xs, _ in groups for x in xs]
    count = sum(ys[0].shape[-1] // cols for _, ys in groups)

    def kernel(me_ref, *refs):
        yr, xr, (keep, send) = refs[: len(fixed)], refs[len(fixed) : -2], refs[-2:]
        odd = (me_ref[0] & 1) == 1
        n = y0 = x0 = 0
        for group, (xs, ys) in enumerate(groups):
            lhs = jnp.concatenate([x[...] for x in xr[x0 : x0 + len(xs)]], axis=0)
            rhs = jnp.concatenate([y[b] for y in yr[y0 : y0 + len(ys)] for b in range(y.shape[0])], axis=0)
            x0, y0 = x0 + len(xs), y0 + len(ys)
            acc = dot_tn(lhs, rhs)
            stay = jnp.where(odd, acc[half:], acc[:half]).astype(bf16)
            go = jnp.where(odd, acc[:half], acc[half:]).astype(bf16)
            if group == len(groups) - 1:
                for ref, value in ((keep, stay), (send, go)):
                    value = value.T
                    for c in range(0, cols, half):
                        ref[0, n, :, c : c + half] = value[c : c + half]
                continue
            for c in range(0, acc.shape[1], cols):
                keep[0, n] = stay[:, c : c + cols]
                send[0, n] = go[:, c : c + cols]
                n += 1

    return grad_call(kernel, me, fixed, sliced, (count, half, cols), pairs)


def grad_units(me, sets, ys, dp, first):
    rows, d = ys[0].shape
    pairs = dp // 2
    wide = d // pairs
    half = wide // 2
    units = sets[0][0].shape[-1]
    quarter = units // 4
    tokens = len(ys) * rows
    count = len(sets[0])
    inner = pairs // 2

    def kernel(me_ref, *refs):
        xr, yr = refs[: 2 * count], refs[2 * count : 2 * count + len(ys)]
        keep, send0, send1, turned = refs[2 * count + len(ys) :]
        sends = (send0, send1)
        step = pl.program_id(0)

        @pl.when(step == 0)
        def _():
            for n in range(2):
                block = jnp.concatenate([x[b] for x in xr[n * count : (n + 1) * count] for b in range(x.shape[0])], axis=0).T
                if n == 0:
                    turned[:units, :] = block
                else:
                    for r in range(4):
                        base = pl.multiple_of(units + ((me_ref[0] & 3) ^ r) * quarter, quarter)
                        turned[pl.ds(base, quarter), :] = block[r * quarter : (r + 1) * quarter]

        acc = dot(turned[...], jnp.concatenate([y[...] for y in yr], axis=0))
        odd = (me_ref[0] & 1) == 1
        same = jnp.where(odd, acc[:, half:], acc[:, :half]).astype(bf16)
        other = jnp.where(odd, acc[:, :half], acc[:, half:]).astype(bf16)
        if first == "y":
            for x, part in ((0, same), (1, other)):
                keep[x, 0] = part[:units]
                sends[x][0] = part[units:]
        elif first == "x":
            for n in range(2):
                keep[0, n, 0] = same[n * units : (n + 1) * units]
            for ref, when in ((send0, step < inner), (send1, step >= inner)):

                @pl.when(when)
                def _():
                    for n in range(2):
                        ref[n, 0] = other[n * units : (n + 1) * units]
        else:

            @pl.when(step < inner)
            def _():
                for n in range(2):
                    keep[0, n, 0] = same[n * units : (n + 1) * units]
                    keep[1, n, 0] = other[n * units : (n + 1) * units]

            @pl.when(step >= inner)
            def _():
                for n in range(2):
                    sends[0][n, 0] = same[n * units : (n + 1) * units]
                    sends[1][n, 0] = other[n * units : (n + 1) * units]

    def early(g):
        return jnp.minimum(g, inner - 1)

    def late(g):
        return jnp.maximum(g - inner, 0)

    if first == "y":
        outs = [((2, pairs), (2, 1), lambda g, m: (0, g, 0, 0))] + [((pairs,), (1,), lambda g, m: (g, 0, 0))] * 2
    elif first == "x":
        outs = [
            ((2, 2, inner), (1, 2, 1), lambda g, m: (g // inner, 0, g % inner, 0, 0)),
            ((2, inner), (2, 1), lambda g, m: (0, early(g), 0, 0)),
            ((2, inner), (2, 1), lambda g, m: (0, late(g), 0, 0)),
        ]
    else:
        outs = [((2, 2, inner), (2, 2, 1), lambda g, m: (0, 0, early(g), 0, 0))] + [
            ((2, inner), (2, 1), lambda g, m: (0, late(g), 0, 0))
        ] * 2
    fixed = [a for one_set in sets for a in one_set]
    return pl.pallas_call(
        kernel,
        out_shape=tuple(pltpu.HBM(shape + (units, half), bf16) for shape, _, _ in outs),
        grid_spec=pltpu.PrefetchScalarGridSpec(
            num_scalar_prefetch=1,
            grid=(pairs,),
            in_specs=[pl.BlockSpec(a.shape, lambda g, m: (0, 0, 0)) for a in fixed]
            + [pl.BlockSpec((rows, wide), lambda g, m: (0, pair_block(g, m, pairs))) for _ in ys],
            out_specs=tuple(pl.BlockSpec(block + (units, half), f) for _, block, f in outs),
            scratch_shapes=[pltpu.VMEM((2 * units, tokens), bf16)],
        ),
        compiler_params=pltpu.CompilerParams(vmem_limit_bytes=20 * MIB),
        cost_estimate=LIGHT,
        name="grad_units",
    )(me, *[in_hbm(a) for a in fixed], *[in_hbm(a) for a in ys])


def grad_adapter(me, xs, grads, gains, dp):
    rows, joined = xs[0].shape
    width = grads[0].shape[1]
    wide = joined // dp
    part = wide // 4
    count = len(xs)

    def kernel(me_ref, *refs):
        xr, gr, (gain, keep, send, grad, acc) = refs[:count], refs[count : 2 * count], refs[2 * count :]

        @pl.when(pl.program_id(0) == 0)
        def _():
            for n in range(count):
                grad[n * rows : (n + 1) * rows, :] = gr[n][...]

        acc[...] = dot_tn(jnp.concatenate([x[...] for x in xr], axis=0), grad[...])
        rest = jnp.zeros((8, width - 128), bf16)
        extra = jnp.concatenate([gain[...].astype(bf16), rest], axis=1)
        for far in (0, 1):
            for near, ref in ((0, keep), (1, send)):
                base = pl.multiple_of((me_ref[1] ^ (2 * far + near)) * part, part)
                ref[far, 0, :part, :] = acc[pl.ds(base, part), :].astype(bf16)
                ref[far, 0, part:, :] = extra

    shape = jax.ShapeDtypeStruct((2, dp, part + 8, width), bf16)
    spec = pl.BlockSpec((2, 1, part + 8, width), lambda g, m: (0, g, 0, 0))
    return pl.pallas_call(
        kernel,
        out_shape=(shape, shape),
        grid_spec=pltpu.PrefetchScalarGridSpec(
            num_scalar_prefetch=1,
            grid=(dp,),
            in_specs=[pl.BlockSpec((rows, wide), lambda g, m: (0, m[0] ^ g)) for _ in xs]
            + [pl.BlockSpec((rows, width), lambda g, m: (0, 0)) for _ in grads]
            + [pl.BlockSpec((8, 128), lambda g, m: (0, m[0] ^ g))],
            out_specs=(spec, spec),
            scratch_shapes=[pltpu.VMEM((count * rows, width), bf16), pltpu.VMEM((wide, width), f32)],
        ),
        compiler_params=pltpu.CompilerParams(vmem_limit_bytes=20 * MIB),
        cost_estimate=LIGHT,
        name="grad_adapter",
    )(me, *[in_hbm(x) for x in xs], *grads, gains)


def plus(a, *others):
    total = a.astype(f32)
    for o in others:
        total = total + o.astype(f32)
    return total


def low(a, *others):
    return plus(a, *others).astype(bf16)


def body(adapter_in, lengths, cotangent, adapter_weight, gains, qkv_weight, out_weight, gate_up_weight, down_weight):
    rows, seqs = adapter_in.shape[0], adapter_in.shape[1]
    width = adapter_weight.shape[1]
    cols = qkv_weight.shape[2]
    heads = cols // HD
    units = down_weight.shape[0]
    members = lax.axis_size("tensor")
    dp = lax.axis_size("dp")
    seq_len = rows * members
    fast = dp == 8 and (width // dp) % 128 == 0
    mine = lax.axis_index("tensor").astype(jnp.int32)
    me = lax.axis_index("dp").astype(jnp.int32).reshape(1)
    scal = jnp.concatenate([mine.reshape(1), lengths])

    lane = jnp.arange(HD, dtype=jnp.int32) % (HD // 2)
    freq = THETA ** (-(lane.astype(f32) * 2.0 / HD))
    inner = jnp.arange(rows, dtype=jnp.int32).astype(f32)[:, None] * freq[None, :]
    owner = (mine ^ jnp.arange(members, dtype=jnp.int32)) * rows
    outer = owner.astype(f32)[:, None] * freq[None, :]
    turn_rows = jnp.stack([jnp.cos(inner), jnp.sin(inner)])
    turn_blocks = jnp.stack([jnp.cos(outer), jnp.sin(outer)])

    every = range(seqs)
    x_in = adapter_in.reshape(rows * seqs, -1)
    x_first = x_in
    tok = (rows, width)

    def parts(n):
        return [(tok, bf16)] * n

    gain = {}

    clock = [None]

    def gate(x):
        return x if clock[0] is None else after(x, clock[0])

    def close(*values):
        values = lax.optimization_barrier(tuple(values))
        clock[0] = values[0]
        return values

    moves = {"c": ("tensor", 1), "y": ("tensor", 2), "x": ("dp", 1), "z": ("dp", 2), "w": ("dp", 4)}

    def go(x, m):
        return swap(gate(x), *moves[m])

    def hop(x):
        return swap(x, "tensor", 1)

    place = me[0] & 3
    w_gu = gate_up_weight.transpose(1, 2, 0)
    w_qkv = qkv_weight.transpose(1, 0, 2)
    quarter = units // 4
    gu0 = swap(lax.dynamic_slice_in_dim(w_gu, place * quarter, quarter, 1), "tensor", 2)
    latent_a, latent_b, normed_a, normed_b = whole_call(
        first_kernel,
        [(tok, f32, True)] * seqs + [(tok, bf16)] * seqs,
        [],
        [in_hbm(x_in), in_hbm(adapter_weight), gains],
        scratch=[pltpu.VMEM((width // 128, rows * seqs, 128), f32)],
        vmem=24,
        name="first",
    )
    latent = [latent_a, latent_b]
    normed_a, normed_b, gu0, turn_rows, turn_blocks = close(normed_a, normed_b, gu0, turn_rows, turn_blocks)

    far_a, near_a = go(normed_a, "y"), go(normed_a, "c")
    d0 = go(lax.dynamic_slice_in_dim(down_weight, place * quarter, quarter, 0), "y")
    gu1, gu2 = go(gu0, "x"), go(gu0, "z")
    early = gate(cotangent)
    cot = [early[:, s] for s in every]
    tokens_of = gate(adapter_in)
    tokens_of = [tokens_of[:, s] for s in every]
    far_a, near_a, d0, gu1, gu2, *both = close(far_a, near_a, d0, gu1, gu2, *cot, *tokens_of)
    cot, tokens_of = both[:seqs], both[seqs:]

    head_shape = ((heads, seq_len, HD), bf16, True)

    def attn_fwd(s, blocks):
        *kept, at, p0, p1, p2, p3 = whole_call(
            functools.partial(attn_fwd_kernel, s),
            [head_shape] * 4 + [((8, seq_len), f32, True), ((members, rows, cols), bf16, True)] + parts(4),
            [scal],
            [*blocks, w_qkv, turn_rows, turn_blocks, out_weight],
            vmem=20,
            name="attn_fwd",
        )
        return kept, at, p0, p1, p2, p3

    far_b, near_b = go(normed_b, "y"), go(normed_b, "c")
    gu3, d2 = go(gu2, "x"), go(d0, "z")
    one = {0: [normed_a, near_a, far_a, hop(far_a)]}
    qkvo, att = {}, {}
    qkvo[0], att[0], *sums = attn_fwd(0, one[0])
    p0, p1, p2, p3, far_b, near_b, gu3, d2 = close(*sums, far_b, near_b, gu3, d2)
    across_a, own_a, p1 = close(low(p2, hop(p3)), p0, p1)

    far_a, d1, near_a = go(across_a, "y"), go(d0, "x"), go(p1, "c")
    one[1] = [gate(normed_b), near_b, far_b, hop(far_b)]
    qkvo[1], att[1], *sums = attn_fwd(1, one[1])
    p0, p1, p2, p3, far_a, d1, near_a = close(*sums, far_a, d1, near_a)
    across_b, own_b, p1 = close(low(p2, hop(p3)), p0, p1)

    far_b, d3, near_b = go(across_b, "y"), go(d1, "z"), go(p1, "c")
    far_gu = jnp.concatenate([gate(gu0), gu1, gu2, gu3], axis=1)

    def mid_of(s, *addends):
        return whole_call(
            mid_kernel,
            [(tok, f32), (tok, f32), (tok, bf16)],
            [],
            [gate(latent[s]), *addends, gains],
            vmem=8,
            name="mid",
        )

    proj, mid, three, ffn, block_out, mlp_g, gu_g = {}, {}, {}, {}, {}, {}, {}
    proj[0], mid[0], own = mid_of(0, own_a, near_a, far_a)
    three[0] = [own, hop(own)]
    far_b, near_b, d3, far_gu, t0, t1 = close(far_b, near_b, d3, far_gu, *three[0])
    three[0] = [t0, t1]

    far_d = jnp.concatenate([gate(d0), d1, d2, d3], axis=0)
    mlp_weights = [w_gu, far_gu, down_weight, far_d]
    hid_shape = ((2, rows, units), bf16, True)

    def ffn_fwd(s):
        *ffn[s], p0, p1 = whole_call(
            mlp_fwd_kernel, [hid_shape] * 6 + parts(2), [], [*three[s], *mlp_weights], vmem=27, name="mlp_fwd"
        )
        return p0, hop(p1)

    def out_of(s, *addends):
        block_out[s], own, gain[3, s] = whole_call(
            functools.partial(out_kernel, s),
            [(tok, bf16), (tok, bf16), ((1, width), f32)],
            [scal],
            [mid[s], *addends, cot[s], gains],
            vmem=10,
            name="out",
        )
        mlp_g[s] = [own, hop(own)]

    def ffn_bwd(s):
        *gu_g[s], p0, p1 = whole_call(
            mlp_bwd_kernel,
            [hid_shape] * 4 + parts(2),
            [],
            [*mlp_g[s], *mlp_weights, *ffn[s][1:3], *ffn[s][4:6]],
            vmem=27,
            name="mlp_bwd",
        )
        return p0, p1

    mid_grad, attn_g, stacked = {}, {}, {}

    def back_of(s, *addends):
        mid_grad[s], own, gain[1, s], gain[2, s] = whole_call(
            functools.partial(back_kernel, s),
            [(tok, f32), (tok, bf16), ((1, width), f32), ((1, width), f32)],
            [scal],
            [mid[s], proj[s], *addends, cot[s], gains],
            vmem=12,
            name="back",
        )
        return own

    sum_a = ffn_fwd(0)
    proj[1], mid[1], own = mid_of(1, own_b, near_b, far_b)
    three[1] = [own, hop(own)]
    out_of(0, *sum_a)
    sum_b = ffn_fwd(1)
    p0, p1 = ffn_bwd(0)
    sum_a = p0, hop(p1)
    out_of(1, *sum_b)
    grad_a = back_of(0, *sum_a)
    grad_a, b0, b1 = close(grad_a, *mlp_g[1])
    mlp_g[1] = [b0, b1]

    def full_grad(xs, ys):
        xs, ys = [jnp.concatenate([a.reshape(-1, a.shape[-1]) for a in part], 0) for part in (xs, ys)]
        return lax.dot_general(xs, ys, (((0,), (0,)), ((), ())), preferred_element_type=f32).astype(bf16)

    def unit_grad(sets, ys, first):
        ys = [gate(ys[0]), *ys[1:]]
        if fast:
            keep, send0, send1 = grad_units(me, sets, ys, dp, first)
            split = (2, 2) + keep.shape[-2:]
            return keep.reshape((2,) + split), send0.reshape(split), send1.reshape(split)
        own, far = [full_grad(xs, ys) for xs in sets]
        far = jnp.concatenate([lax.dynamic_slice_in_dim(far, (place ^ a) * quarter, quarter, 0) for a in range(4)], axis=0)
        total = low(own, swap(far, "tensor", 2))
        return lax.psum_scatter(total, "dp", scatter_dimension=1, tiled=True).astype(f32)

    far_a, near_a = go(grad_a, "y"), go(grad_a, "c")
    sum_b = ffn_bwd(1)
    flat_three = [b for s in every for b in three[s]]
    flat_mlp = [b for s in every for b in mlp_g[s]]
    flat_one = [b for s in every for b in one[s]]
    hiddens = [[ffn[s][3 * n] for s in every] for n in (0, 1)]
    gates = [[gu_g[s][2 * n] for s in every] for n in (0, 1)]
    ups = [[gu_g[s][2 * n + 1] for s in every] for n in (0, 1)]

    if fast:
        down_keep, down0, down1 = unit_grad(hiddens, flat_mlp, "x")
        p0, p1, far_a, near_a, down0, down1 = close(*sum_b, far_a, near_a, down0, down1)
    else:
        p0, p1, far_a, near_a = close(*sum_b, far_a, near_a)
    grad_b = close(back_of(1, p0, hop(p1)))[0]


    head_f32 = (heads, seq_len, HD)

    def attn_bwd(s, blocks):
        stacked[s], p0, p1, p2, p3 = whole_call(
            functools.partial(attn_bwd_kernel, s),
            [((members, rows, 3 * cols), bf16, True)] + parts(4),
            [scal],
            [*blocks, out_weight, *qkvo[s], turn_rows, turn_blocks, w_qkv],
            scratch=[pltpu.VMEM(head_f32, bf16)] + [pltpu.VMEM(head_f32, f32)] * 3,
            vmem=24,
            name="attn_bwd",
        )
        return p0, p1, p2, p3

    far_b, near_b = go(grad_b, "y"), go(grad_b, "c")
    attn_g[0] = [gate(grad_a), near_a, far_a, hop(far_a)]
    sums = attn_bwd(0, attn_g[0])
    if fast:
        down_got1 = go(down1, "x")
        gate_keep, gate0, gate1 = unit_grad(gates, flat_three, "z")
        p0, p1, p2, p3, far_b, near_b, gate0, gate1, down_got1 = close(*sums, far_b, near_b, gate0, gate1, down_got1)
    else:
        p0, p1, p2, p3, far_b, near_b = close(*sums, far_b, near_b)
    across_a, own_a, p1 = close(low(p2, hop(p3)), p0, p1)

    far_a, near_a = go(across_a, "y"), go(p1, "c")
    attn_g[1] = [gate(grad_b), near_b, far_b, hop(far_b)]
    sums = attn_bwd(1, attn_g[1])
    if fast:
        down_got0, gate_got1 = go(down0, "x"), go(gate1, "z")
        up_keep, up0, up1 = unit_grad(ups, flat_three, "y")
        p0, p1, p2, p3, far_a, near_a, down_got0, gate_got1, up0, up1 = close(
            *sums, far_a, near_a, down_got0, gate_got1, up0, up1
        )
    else:
        p0, p1, p2, p3, far_a, near_a = close(*sums, far_a, near_a)
    across_b, own_b, p1 = close(low(p2, hop(p3)), p0, p1)

    latent_grad = {}

    def last_of(s, *addends):
        latent_grad[s], gain[0, s] = whole_call(
            last_kernel,
            [(tok, bf16), ((1, width), f32)],
            [],
            [gate(latent[s]), *addends, mid_grad[s], gains],
            vmem=10,
            name="last",
        )

    both_me = jnp.concatenate([me, mine.reshape(1)])

    far_b, near_b = go(across_b, "y"), go(p1, "c")
    last_of(0, own_a, near_a, far_a)
    flat_attn = [b for s in every for b in attn_g[s]]
    if fast:
        gate_got0 = go(gate0, "z")
        down_next = low(gate(down_keep)[1], down_got1)
        gate_got2 = swap(low(gate(gate_keep)[1], gate_got1), *moves["x"])
        down_stay = low(gate(down_keep)[0], down_got0)
        first = [gate(flat_one[0]), *flat_one[1:]]
        attn_keep, attn_send = grad_rows(
            me, [(first, [stacked[s] for s in every]), (flat_attn, [att[s] for s in every])], dp, cols
        )
        lead = (2, 2) + attn_keep.shape[1:]
        half = width // dp
        attn_keep, attn_send = attn_keep.reshape(lead), attn_send.reshape(lead)
        far_b, near_b, attn_send, gate_got0, gate_got2, down_next, down_stay = close(
            far_b, near_b, attn_send, gate_got0, gate_got2, down_next, down_stay
        )
    else:
        far_b, near_b = close(far_b, near_b)

    last_of(1, own_b, near_b, far_b)
    grads = [latent_grad[s] for s in every]
    d_gains = jnp.concatenate([sum(gain[g, s] for s in every) for g in range(4)], axis=0)
    if fast:
        up_got1, attn_got, down_got2 = go(up1, "y"), go(attn_send, "x"), go(down_next, "z")
        gate2 = low(low(gate(gate_keep)[0], gate_got0), gate_got2)
        gate_got3 = swap(gate2[1], *moves["y"])
        d_gains = jnp.concatenate([d_gains, jnp.zeros_like(d_gains)], axis=0)
        keep, send = grad_adapter(both_me, tokens_of, grads, d_gains, dp)
        send, up_got1, attn_got, gate_got3, down_got2 = close(send, up_got1, attn_got, gate_got3, down_got2)
        total = close(low(keep, hop(send)))[0]

        part = total.shape[-2]
        ranges = total.reshape(2, 2, 2, 2, part, width)
        orders = ["zxyw", "yxzw"]
        cut = width * 5 // 8
        axes = ["ywzx"] * 2
        state = [ranges[..., :cut], ranges[..., cut:]]

        def adapter_round(r, state):
            kept, got = [], []
            for n in range(2):
                m = orders[n][r]
                at = axes[n].index(m)
                axes[n] = axes[n].replace(m, "")
                kept.append(lax.index_in_dim(state[n], 0, at, keepdims=False))
                got.append(swap(lax.index_in_dim(state[n], 1, at, keepdims=False), *moves[m]))
            return kept, got

        up_got0 = go(up0, "y")
        up_got2 = swap(low(gate(up_keep)[1], up_got1), *moves["x"])
        kept, got = adapter_round(0, state)
        attn = low(gate(attn_keep), attn_got)
        attn_got = swap(attn[:, 1], *moves["w"])
        gate3 = low(gate(gate2[0]), gate_got3)
        grad_in = [
            lax.dot_general(gate(g), adapter_weight, (((1,), (1,)), ((), ())), preferred_element_type=f32).astype(bf16)
            for g in grads
        ]
        out = jnp.stack([gate(block_out[s]) for s in every], axis=1)
        down2 = low(gate(down_stay), down_got2)
        got0, got1, up_got0, up_got2, attn_got, out, down2 = close(*got, up_got0, up_got2, attn_got, out, down2)

        down_got3, gate_got4 = go(down2[1], "y"), go(gate3[1], "w")
        state = [low(k, g) for k, g in zip(kept, (got0, got1))]
        both_x = [[lax.index_in_dim(state[n], i, 2, keepdims=False) for n in range(2)] for i in (0, 1)]
        kept = both_x[0]
        got = [swap(jnp.concatenate(both_x[1], axis=-1), *moves["x"])]
        axes = ["yw", "wz"]
        up2 = low(low(gate(up_keep)[0], up_got0), up_got2)
        up_got3 = swap(up2[1], *moves["z"])
        attn = low(gate(attn)[:, 0], attn_got)
        attn_got = swap(attn[1], *moves["z"])
        got0, up_got3, attn_got, down_got3, gate_got4 = close(*got, up_got3, attn_got, down_got3, gate_got4)
        got0, got1 = got0[..., :cut], got0[..., cut:]

        down3 = low(gate(down2[0]), down_got3)
        down_got4 = swap(down3[1], *moves["w"])
        d_gate = plus(gate(gate3[0]), gate_got4)
        state = [low(k, g) for k, g in zip(kept, (got0, got1))]
        kept, got = adapter_round(2, state)
        up3 = low(gate(up2[0]), up_got3)
        up_got4 = swap(up3[1], *moves["w"])
        attn = plus(gate(attn[0]), attn_got)
        got0, got1, up_got4, down_got4, attn, d_gate = close(*got, up_got4, down_got4, attn, d_gate)

        state = [low(k, g) for k, g in zip(kept, (got0, got1))]
        kept, got = adapter_round(3, state)
        d_up = plus(gate(up3[0]), up_got4)
        d_down = plus(gate(down3[0]), down_got4)
        rows_out = part - 8
        d_adapt = jnp.concatenate([plus(k[:rows_out], g[:rows_out]) for k, g in zip(kept, got)], axis=-1)
        d_gains = plus(kept[0][rows_out : rows_out + 4, :128], got[0][rows_out : rows_out + 4, :128])
        share = 128 // members
        d_gains = lax.dynamic_slice_in_dim(d_gains, mine * share, share, 1)
        d_qkv = attn[:3].transpose(1, 0, 2)
        d_out = jnp.concatenate([attn[3, :, :half], attn[3, :, half:]], axis=0)
    else:
        out = jnp.stack([block_out[s] for s in every], axis=1)
        share = width // (dp * members)
        d_gains = lax.psum(d_gains, ("dp", "tensor"))
        d_gains = lax.dynamic_slice_in_dim(d_gains, (me[0] * members + mine) * share, share, 1)
        d_down = unit_grad(hiddens, flat_mlp, "z")
        d_gate = unit_grad(gates, flat_three, "x")
        d_up = unit_grad(ups, flat_three, "y")

        def reduced(xs, ys, dim):
            return lax.psum_scatter(full_grad(xs, ys), "dp", scatter_dimension=dim, tiled=True).astype(f32)

        d_qkv = reduced(flat_one, [stacked[s] for s in every], 0).reshape(-1, 3, cols)
        d_out = reduced([att[s] for s in every], flat_attn, 1)
        full = full_grad([tokens_of[s] for s in every], grads).astype(f32)
        d_adapt = lax.psum_scatter(full, ("dp", "tensor"), scatter_dimension=0, tiled=True)
        grad_in = [
            lax.dot_general(g, adapter_weight, (((1,), (1,)), ((), ())), preferred_element_type=f32).astype(bf16)
            for g in grads
        ]
    grad_in = jnp.stack(grad_in, axis=1)
    d_gate_up = jnp.stack([d_gate, d_up]).transpose(2, 0, 1)
    return (out, grad_in, d_adapt, d_gains, d_qkv, d_out, d_gate_up, d_down)


def solution(mesh):
    return jax.shard_map(
        body,
        mesh=mesh,
        in_specs=(
            P("tensor", "dp", None),
            P("dp"),
            P("tensor", "dp", None),
            P(),
            P(),
            P(None, None, "tensor"),
            P("tensor", None),
            P(None, None, "tensor"),
            P("tensor", None),
        ),
        out_specs=(
            P("tensor", "dp", None),
            P("tensor", "dp", None),
            P(("dp", "tensor"), None),
            P(None, ("dp", "tensor")),
            P("dp", None, "tensor"),
            P("tensor", "dp"),
            P("dp", None, "tensor"),
            P("tensor", "dp"),
        ),
        check_vma=False,
    )
```

```python
import functools

import jax
import jax.numpy as jnp
import numpy as np
from jax import lax
from jax.experimental import pallas as pl
from jax.experimental.pallas import tpu as pltpu
from jax.sharding import PartitionSpec as P

HD = 128
LOG2E = 1.4426950408889634
EPS = 1e-06
THETA = 50000.0
MASKED = -1e30
f32 = jnp.float32
bf16 = jnp.bfloat16
MIB = 1024 * 1024
LIGHT = pl.CostEstimate(flops=1, bytes_accessed=1, transcendentals=0)


def dot(a, b):
    return jnp.dot(a, b, preferred_element_type=f32)


def dot_nt(a, b):
    return lax.dot_general(a, b, (((1,), (1,)), ((), ())), preferred_element_type=f32)


def dot_tn(a, b):
    return lax.dot_general(a, b, (((0,), (0,)), ((), ())), preferred_element_type=f32)


def full_map(rank):
    return lambda *_: (0,) * rank


def whole_call(kernel, outs, scalars, arrays, scratch=(), vmem=40, name=None):
    smem = pl.BlockSpec(memory_space=pltpu.SMEM)
    vm = pl.BlockSpec(memory_space=pltpu.VMEM)
    return pl.pallas_call(
        kernel,
        out_shape=tuple(pltpu.HBM(o[0], o[1]) if len(o) > 2 else jax.ShapeDtypeStruct(*o) for o in outs),
        in_specs=[smem] * len(scalars) + [vm] * len(arrays),
        out_specs=tuple(pl.BlockSpec(o[0], full_map(len(o[0]))) if len(o) > 2 else vm for o in outs),
        scratch_shapes=list(scratch),
        compiler_params=pltpu.CompilerParams(vmem_limit_bytes=vmem * MIB),
        cost_estimate=LIGHT,
        name=name,
    )(*scalars, *arrays)


def swap(x, axis, bit):
    n = lax.axis_size(axis)
    return lax.ppermute(x, axis, [(i, i ^ bit) for i in range(n)])


def gather_blocks(x):
    far = swap(x, "tensor", 2)
    near = swap(x, "tensor", 1)
    return [x, near, far, swap(far, "tensor", 1)]


def scatter_blocks(p0, p1, p2, p3):
    near = swap(p1, "tensor", 1)
    across = (p2.astype(f32) + swap(p3, "tensor", 1).astype(f32)).astype(bf16)
    return across, (p0, near, swap(across, "tensor", 2))


def in_hbm(x):
    return pltpu.with_memory_space_constraint(x, pltpu.HBM)


def after(x, *others):
    return lax.optimization_barrier((x,) + others)[0]


def turn_tables(turn_rows, turn_blocks, j):
    cr, sr = turn_rows[0], turn_rows[1]
    cb, sb = turn_blocks[0, j : j + 1, :], turn_blocks[1, j : j + 1, :]
    sign = jnp.where(lax.broadcasted_iota(jnp.int32, (1, HD), 1) < HD // 2, -1.0, 1.0)
    return cb * cr - sb * sr, (sb * cr + cb * sr) * sign


def attn_fwd_kernel(seq, scal, x0, x1, x2, x3, w, turn_rows, turn_blocks, wo, q, k, v, o, lse, att, *parts):
    mine, length = scal[0], scal[1 + seq]
    rows = x0.shape[0]
    heads = q.shape[0]
    for j, x in enumerate((x0, x1, x2, x3)):
        base = pl.multiple_of((mine ^ j) * rows, rows)
        c, s = turn_tables(turn_rows, turn_blocks, j)
        for n, ref in ((0, q), (1, k)):
            acc = dot(x[...], w[n])
            for h in range(heads):
                part = acc[:, h * HD : (h + 1) * HD]
                turned = part * c + pltpu.roll(part, HD // 2, 1) * s
                ref[h, pl.ds(base, rows), :] = turned.astype(bf16)
        acc = dot(x[...], w[2]).astype(bf16)
        for h in range(heads):
            v[h, pl.ds(base, rows), :] = acc[:, h * HD : (h + 1) * HD]
    factor = HD**-0.5 * LOG2E

    @pl.loop(0, heads)
    def _(h):
        vt = v[h].T
        for i in range(4):
            keys = (i + 1) * rows
            st = dot_nt(k[h, :keys, :], q[h, i * rows : keys, :]) * factor
            key_id = lax.broadcasted_iota(jnp.int32, st.shape, 0)
            row_id = lax.broadcasted_iota(jnp.int32, st.shape, 1) + i * rows
            st = jnp.where((key_id <= row_id) & (key_id < length), st, MASKED)
            top = jnp.max(st, axis=0, keepdims=True)
            weights = jnp.exp2(st - top)
            total = jnp.sum(weights, axis=0, keepdims=True)
            ot = dot(vt[:, :keys], weights.astype(bf16)) / total
            o[h, i * rows : keys, :] = ot.T.astype(bf16)
            lse[pl.ds(h, 1), i * rows : keys] = top + jnp.log2(total)

    for j in range(4):
        base = pl.multiple_of((mine ^ j) * rows, rows)
        both = jnp.concatenate([o[h, pl.ds(base, rows), :] for h in range(heads)], axis=1)
        att[j] = both
        parts[j][...] = dot(both, wo[...]).astype(bf16)


def attn_bwd_kernel(
    seq, scal, g0, g1, g2, g3, wo, q, k, v, o, lse, turn_rows, turn_blocks, w, st_out, p0, p1, p2, p3, dout, dq, dk, dv
):
    parts = (p0, p1, p2, p3)
    mine, length = scal[0], scal[1 + seq]
    rows = g0.shape[0]
    heads = q.shape[0]
    cols = heads * HD
    for j, g in enumerate((g0, g1, g2, g3)):
        mixed = dot_nt(g[...], wo[...]).astype(bf16)
        base = pl.multiple_of((mine ^ j) * rows, rows)
        for h in range(heads):
            dout[h, pl.ds(base, rows), :] = mixed[:, h * HD : (h + 1) * HD]
    scale = HD**-0.5
    factor = scale * LOG2E
    ones = jnp.ones((8, HD), f32)
    for h in range(heads):
        for i in (3, 2, 1, 0):
            keys = (i + 1) * rows
            here = slice(i * rows, keys)
            qi, di = q[h, here, :], dout[h, here, :]
            st = dot_nt(k[h, :keys, :], qi) * factor
            key_id = lax.broadcasted_iota(jnp.int32, st.shape, 0)
            row_id = lax.broadcasted_iota(jnp.int32, st.shape, 1) + i * rows
            st = jnp.where((key_id <= row_id) & (key_id < length), st, MASKED)
            probs = jnp.exp2(st - lse[h : h + 1, here])
            prob_grad = dot_nt(v[h, :keys, :], di)
            product = di.astype(f32) * o[h, here, :].astype(f32)
            inner = lax.dot_general(
                ones, product, (((1,), (1,)), ((), ())), precision=lax.Precision.HIGHEST, preferred_element_type=f32
            )[0:1, :]
            sg = (probs * (prob_grad - inner)).astype(bf16)
            new_v = dot(probs.astype(bf16), di)
            new_k = dot(sg, qi)
            if i == 3:
                dv[h] = new_v
                dk[h] = new_k
            else:
                dv[h, :keys, :] += new_v
                dk[h, :keys, :] += new_k
            dq[h, here, :] = dot_tn(sg, k[h, :keys, :])
    for j in range(4):
        base = pl.multiple_of((mine ^ j) * rows, rows)
        c, s = turn_tables(turn_rows, turn_blocks, j)
        c, s = c * scale, s * scale
        total = None
        for n, ref in enumerate((dq, dk, dv)):
            pieces = []
            for h in range(heads):
                part = ref[h, pl.ds(base, rows), :]
                if n < 2:
                    part = part * c - pltpu.roll(part, HD // 2, 1) * s
                pieces.append(part.astype(bf16))
            piece = jnp.concatenate(pieces, axis=1)
            st_out[j, :, n * cols : (n + 1) * cols] = piece
            add = dot_nt(piece, w[n])
            total = add if total is None else total + add
        parts[j][...] = total.astype(bf16)


def mlp_fwd_kernel(x0, x1, wgu0, wgu1, wd0, wd1, *outs):
    kept, parts = outs[:6], outs[6:]
    rows = x0.shape[0]
    x = jnp.concatenate([x0[...], x1[...]], axis=0)
    total = None
    for n, (wgu, wd) in enumerate(((wgu0, wd0), (wgu1, wd1))):
        hid, fa, fb = kept[3 * n : 3 * n + 3]
        gate = dot_nt(x, wgu[0])
        up = dot_nt(x, wgu[1])
        sig = jax.nn.sigmoid(gate)
        act = gate * sig
        hidden = (act * up).astype(bf16)
        a = act.astype(bf16)
        b = (up * sig * (1.0 + gate * (1.0 - sig))).astype(bf16)
        for j in range(2):
            here = slice(j * rows, (j + 1) * rows)
            hid[j], fa[j], fb[j] = hidden[here], a[here], b[here]
        add = dot(hidden, wd[...])
        total = add if total is None else total + add
    for j in range(2):
        parts[j][...] = total[j * rows : (j + 1) * rows].astype(bf16)


def mlp_bwd_kernel(g0, g1, wgu0, wgu1, wd0, wd1, fa0, fb0, fa1, fb1, gg0, gu0, gg1, gu1, *parts):
    rows = g0.shape[0]
    g = jnp.concatenate([g0[...], g1[...]], axis=0)
    total = None
    for wgu, wd, fa, fb, gg, gu in ((wgu0, wd0, fa0, fb0, gg0, gu0), (wgu1, wd1, fa1, fb1, gg1, gu1)):
        hidden_grad = dot_nt(g, wd[...])
        a = jnp.concatenate([fa[0], fa[1]], axis=0).astype(f32)
        b = jnp.concatenate([fb[0], fb[1]], axis=0).astype(f32)
        gate_grad = (hidden_grad * b).astype(bf16)
        up_grad = (hidden_grad * a).astype(bf16)
        for j in range(2):
            here = slice(j * rows, (j + 1) * rows)
            gg[j], gu[j] = gate_grad[here], up_grad[here]
        add = dot(gate_grad, wgu[0]) + dot(up_grad, wgu[1])
        total = add if total is None else total + add
    for j in range(2):
        parts[j][...] = total[j * rows : (j + 1) * rows].astype(bf16)


def factor_of(v):
    return lax.rsqrt(jnp.mean(v * v, axis=-1, keepdims=True) + EPS)


def norm_back(v, r, gain, e):
    scaled = e * gain
    inner = jnp.mean(scaled * v, axis=-1, keepdims=True)
    grad = r * (scaled - v * (r * r * inner))
    return grad, jnp.sum(e * v * r, axis=0, keepdims=True)


def summed(*addends):
    total = addends[0][...].astype(f32)
    for a in addends[1:]:
        total = total + a[...].astype(f32)
    return total


def mid_kernel(latent, p0, near, far, gains, proj_out, mid_out, normed_out):
    proj = summed(p0, near, far)
    mid = latent[...] + proj * factor_of(proj) * gains[1:2, :]
    proj_out[...] = proj
    mid_out[...] = mid
    normed_out[...] = (mid * factor_of(mid) * gains[2:3, :]).astype(bf16)


def live_grad(seq, scal, cot):
    rows = cot.shape[0]
    row_id = lax.broadcasted_iota(jnp.int32, (rows, 1), 0) + scal[0] * rows
    return jnp.where(row_id < scal[1 + seq], cot[...].astype(f32), 0.0)


def out_kernel(seq, scal, mid, p0, near, cot, gains, out, grad_out, gain_out):
    proj = summed(p0, near)
    r = factor_of(proj)
    gain = gains[3:4, :]
    out[...] = (mid[...] + proj * r * gain).astype(bf16)
    grad, gain_grad = norm_back(proj, r, gain, live_grad(seq, scal, cot))
    grad_out[...] = grad.astype(bf16)
    gain_out[...] = gain_grad


def back_kernel(seq, scal, mid, proj, p0, near, cot, gains, mid_grad_out, grad_out, gain_two, gain_three):
    three = summed(p0, near)
    m = mid[...]
    part, g3 = norm_back(m, factor_of(m), gains[2:3, :], three)
    mid_grad = live_grad(seq, scal, cot) + part
    pr = proj[...]
    grad, g2 = norm_back(pr, factor_of(pr), gains[1:2, :], mid_grad)
    mid_grad_out[...] = mid_grad
    grad_out[...] = grad.astype(bf16)
    gain_two[...] = g2
    gain_three[...] = g3


def last_kernel(latent, p0, near, far, mid_grad, gains, grad_out, gain_out):
    one = summed(p0, near, far)
    la = latent[...]
    part, g1 = norm_back(la, factor_of(la), gains[0:1, :], one)
    grad_out[...] = (mid_grad[...] + part).astype(bf16)
    gain_out[...] = g1


def first_kernel(x, w, gains, *refs):
    outs, acc = refs[:-1], refs[-1]
    seqs = len(outs) // 2
    whole = dot(x[...], w[...])
    rows, tiles = acc.shape[1] // seqs, acc.shape[0]
    for c in range(tiles):
        acc[c] = whole[:, c * 128 : (c + 1) * 128]
    for s in range(seqs):
        latent = jnp.concatenate([acc[c, pl.ds(s, rows, stride=seqs), :] for c in range(tiles)], axis=1)
        outs[s][...] = latent
        outs[seqs + s][...] = (latent * factor_of(latent) * gains[0:1, :]).astype(bf16)


def reversed_bits(index, bits):
    out = 0
    for b in range(bits):
        out = out + (((index >> b) & 1) << (bits - 1 - b))
    return out


def pair_block(g, me, pairs):
    return (me[0] >> 1) ^ reversed_bits(g, pairs.bit_length() - 1)


def grad_call(kernel, me, fixed, sliced, out, pairs, scratch=()):
    rows, d = sliced[0].shape
    wide = d // pairs
    shape = pltpu.HBM((pairs,) + out, bf16)
    spec = pl.BlockSpec((1,) + out, lambda g, m: (g,) + (0,) * len(out))

    def full_map(a):
        return lambda g, m: (0,) * a.ndim

    return pl.pallas_call(
        kernel,
        out_shape=(shape, shape),
        grid_spec=pltpu.PrefetchScalarGridSpec(
            num_scalar_prefetch=1,
            grid=(pairs,),
            in_specs=[pl.BlockSpec(a.shape, full_map(a)) for a in fixed]
            + [pl.BlockSpec((rows, wide), lambda g, m: (0, pair_block(g, m, pairs))) for _ in sliced],
            out_specs=(spec, spec),
            scratch_shapes=list(scratch),
        ),
        compiler_params=pltpu.CompilerParams(vmem_limit_bytes=20 * MIB),
        cost_estimate=LIGHT,
        name="weight_grad",
    )(me, *[in_hbm(a) for a in fixed], *[in_hbm(a) for a in sliced])


def grad_rows(me, groups, dp, cols):
    pairs = dp // 2
    half = groups[0][0][0].shape[1] // dp
    fixed = [y for _, ys in groups for y in ys]
    sliced = [x for xs, _ in groups for x in xs]
    count = sum(ys[0].shape[-1] // cols for _, ys in groups)

    def kernel(me_ref, *refs):
        yr, xr, (keep, send) = refs[: len(fixed)], refs[len(fixed) : -2], refs[-2:]
        odd = (me_ref[0] & 1) == 1
        n = y0 = x0 = 0
        for group, (xs, ys) in enumerate(groups):
            lhs = jnp.concatenate([x[...] for x in xr[x0 : x0 + len(xs)]], axis=0)
            rhs = jnp.concatenate([y[b] for y in yr[y0 : y0 + len(ys)] for b in range(y.shape[0])], axis=0)
            x0, y0 = x0 + len(xs), y0 + len(ys)
            acc = dot_tn(lhs, rhs)
            stay = jnp.where(odd, acc[half:], acc[:half]).astype(bf16)
            go = jnp.where(odd, acc[:half], acc[half:]).astype(bf16)
            if group == len(groups) - 1:
                for ref, value in ((keep, stay), (send, go)):
                    value = value.T
                    for c in range(0, cols, half):
                        ref[0, n, :, c : c + half] = value[c : c + half]
                continue
            for c in range(0, acc.shape[1], cols):
                keep[0, n] = stay[:, c : c + cols]
                send[0, n] = go[:, c : c + cols]
                n += 1

    return grad_call(kernel, me, fixed, sliced, (count, half, cols), pairs)


def grad_units(me, sets, ys, dp, first):
    rows, d = ys[0].shape
    pairs = dp // 2
    wide = d // pairs
    half = wide // 2
    units = sets[0][0].shape[-1]
    quarter = units // 4
    tokens = len(ys) * rows
    count = len(sets[0])
    inner = pairs // 2

    def kernel(me_ref, *refs):
        xr, yr = refs[: 2 * count], refs[2 * count : 2 * count + len(ys)]
        keep, send0, send1, turned = refs[2 * count + len(ys) :]
        sends = (send0, send1)
        step = pl.program_id(0)

        @pl.when(step == 0)
        def _():
            for n in range(2):
                block = jnp.concatenate([x[b] for x in xr[n * count : (n + 1) * count] for b in range(x.shape[0])], axis=0).T
                if n == 0:
                    turned[:units, :] = block
                else:
                    for r in range(4):
                        base = pl.multiple_of(units + ((me_ref[0] & 3) ^ r) * quarter, quarter)
                        turned[pl.ds(base, quarter), :] = block[r * quarter : (r + 1) * quarter]

        acc = dot(turned[...], jnp.concatenate([y[...] for y in yr], axis=0))
        odd = (me_ref[0] & 1) == 1
        same = jnp.where(odd, acc[:, half:], acc[:, :half]).astype(bf16)
        other = jnp.where(odd, acc[:, :half], acc[:, half:]).astype(bf16)
        if first == "y":
            for x, part in ((0, same), (1, other)):
                keep[x, 0] = part[:units]
                sends[x][0] = part[units:]
        elif first == "x":
            for n in range(2):
                keep[0, n, 0] = same[n * units : (n + 1) * units]
            for ref, when in ((send0, step < inner), (send1, step >= inner)):

                @pl.when(when)
                def _():
                    for n in range(2):
                        ref[n, 0] = other[n * units : (n + 1) * units]
        else:

            @pl.when(step < inner)
            def _():
                for n in range(2):
                    keep[0, n, 0] = same[n * units : (n + 1) * units]
                    keep[1, n, 0] = other[n * units : (n + 1) * units]

            @pl.when(step >= inner)
            def _():
                for n in range(2):
                    sends[0][n, 0] = same[n * units : (n + 1) * units]
                    sends[1][n, 0] = other[n * units : (n + 1) * units]

    def early(g):
        return jnp.minimum(g, inner - 1)

    def late(g):
        return jnp.maximum(g - inner, 0)

    if first == "y":
        outs = [((2, pairs), (2, 1), lambda g, m: (0, g, 0, 0))] + [((pairs,), (1,), lambda g, m: (g, 0, 0))] * 2
    elif first == "x":
        outs = [
            ((2, 2, inner), (1, 2, 1), lambda g, m: (g // inner, 0, g % inner, 0, 0)),
            ((2, inner), (2, 1), lambda g, m: (0, early(g), 0, 0)),
            ((2, inner), (2, 1), lambda g, m: (0, late(g), 0, 0)),
        ]
    else:
        outs = [((2, 2, inner), (2, 2, 1), lambda g, m: (0, 0, early(g), 0, 0))] + [
            ((2, inner), (2, 1), lambda g, m: (0, late(g), 0, 0))
        ] * 2
    fixed = [a for one_set in sets for a in one_set]
    return pl.pallas_call(
        kernel,
        out_shape=tuple(pltpu.HBM(shape + (units, half), bf16) for shape, _, _ in outs),
        grid_spec=pltpu.PrefetchScalarGridSpec(
            num_scalar_prefetch=1,
            grid=(pairs,),
            in_specs=[pl.BlockSpec(a.shape, lambda g, m: (0, 0, 0)) for a in fixed]
            + [pl.BlockSpec((rows, wide), lambda g, m: (0, pair_block(g, m, pairs))) for _ in ys],
            out_specs=tuple(pl.BlockSpec(block + (units, half), f) for _, block, f in outs),
            scratch_shapes=[pltpu.VMEM((2 * units, tokens), bf16)],
        ),
        compiler_params=pltpu.CompilerParams(vmem_limit_bytes=20 * MIB),
        cost_estimate=LIGHT,
        name="grad_units",
    )(me, *[in_hbm(a) for a in fixed], *[in_hbm(a) for a in ys])


def grad_adapter(me, xs, grads, gains, dp):
    rows, joined = xs[0].shape
    width = grads[0].shape[1]
    wide = joined // dp
    part = wide // 4
    count = len(xs)

    def kernel(me_ref, *refs):
        xr, gr, (gain, keep, send, grad, acc) = refs[:count], refs[count : 2 * count], refs[2 * count :]

        @pl.when(pl.program_id(0) == 0)
        def _():
            for n in range(count):
                grad[n * rows : (n + 1) * rows, :] = gr[n][...]

        acc[...] = dot_tn(jnp.concatenate([x[...] for x in xr], axis=0), grad[...])
        rest = jnp.zeros((8, width - 128), bf16)
        extra = jnp.concatenate([gain[...].astype(bf16), rest], axis=1)
        for far in (0, 1):
            for near, ref in ((0, keep), (1, send)):
                base = pl.multiple_of((me_ref[1] ^ (2 * far + near)) * part, part)
                ref[far, 0, :part, :] = acc[pl.ds(base, part), :].astype(bf16)
                ref[far, 0, part:, :] = extra

    shape = jax.ShapeDtypeStruct((2, dp, part + 8, width), bf16)
    spec = pl.BlockSpec((2, 1, part + 8, width), lambda g, m: (0, g, 0, 0))
    return pl.pallas_call(
        kernel,
        out_shape=(shape, shape),
        grid_spec=pltpu.PrefetchScalarGridSpec(
            num_scalar_prefetch=1,
            grid=(dp,),
            in_specs=[pl.BlockSpec((rows, wide), lambda g, m: (0, m[0] ^ g)) for _ in xs]
            + [pl.BlockSpec((rows, width), lambda g, m: (0, 0)) for _ in grads]
            + [pl.BlockSpec((8, 128), lambda g, m: (0, m[0] ^ g))],
            out_specs=(spec, spec),
            scratch_shapes=[pltpu.VMEM((count * rows, width), bf16), pltpu.VMEM((wide, width), f32)],
        ),
        compiler_params=pltpu.CompilerParams(vmem_limit_bytes=20 * MIB),
        cost_estimate=LIGHT,
        name="grad_adapter",
    )(me, *[in_hbm(x) for x in xs], *grads, gains)


def plus(a, *others):
    total = a.astype(f32)
    for o in others:
        total = total + o.astype(f32)
    return total


def low(a, *others):
    return plus(a, *others).astype(bf16)


def body(adapter_in, lengths, cotangent, adapter_weight, gains, qkv_weight, out_weight, gate_up_weight, down_weight):
    rows, seqs = adapter_in.shape[0], adapter_in.shape[1]
    width = adapter_weight.shape[1]
    cols = qkv_weight.shape[2]
    heads = cols // HD
    units = down_weight.shape[0]
    members = lax.axis_size("tensor")
    dp = lax.axis_size("dp")
    seq_len = rows * members
    fast = dp == 8 and (width // dp) % 128 == 0
    mine = lax.axis_index("tensor").astype(jnp.int32)
    me = lax.axis_index("dp").astype(jnp.int32).reshape(1)
    scal = jnp.concatenate([mine.reshape(1), lengths])

    lane = jnp.arange(HD, dtype=jnp.int32) % (HD // 2)
    freq = THETA ** (-(lane.astype(f32) * 2.0 / HD))
    inner = jnp.arange(rows, dtype=jnp.int32).astype(f32)[:, None] * freq[None, :]
    owner = (mine ^ jnp.arange(members, dtype=jnp.int32)) * rows
    outer = owner.astype(f32)[:, None] * freq[None, :]
    turn_rows = jnp.stack([jnp.cos(inner), jnp.sin(inner)])
    turn_blocks = jnp.stack([jnp.cos(outer), jnp.sin(outer)])

    every = range(seqs)
    x_in = adapter_in.reshape(rows * seqs, -1)
    x_first = x_in
    tok = (rows, width)

    def parts(n):
        return [(tok, bf16)] * n

    gain = {}

    clock = [None]

    def gate(x):
        return x if clock[0] is None else after(x, clock[0])

    def close(*values):
        values = lax.optimization_barrier(tuple(values))
        clock[0] = values[0]
        return values

    moves = {"c": ("tensor", 1), "y": ("tensor", 2), "x": ("dp", 1), "z": ("dp", 2), "w": ("dp", 4)}

    def go(x, m):
        return swap(gate(x), *moves[m])

    def hop(x):
        return swap(x, "tensor", 1)

    place = me[0] & 3
    w_gu = gate_up_weight.transpose(1, 2, 0)
    w_qkv = qkv_weight.transpose(1, 0, 2)
    quarter = units // 4
    gu0 = swap(lax.dynamic_slice_in_dim(w_gu, place * quarter, quarter, 1), "tensor", 2)
    latent_a, latent_b, normed_a, normed_b = whole_call(
        first_kernel,
        [(tok, f32, True)] * seqs + [(tok, bf16)] * seqs,
        [],
        [in_hbm(x_in), in_hbm(adapter_weight), gains],
        scratch=[pltpu.VMEM((width // 128, rows * seqs, 128), f32)],
        vmem=24,
        name="first",
    )
    latent = [latent_a, latent_b]
    normed_a, normed_b, gu0, turn_rows, turn_blocks = close(normed_a, normed_b, gu0, turn_rows, turn_blocks)

    far_a, near_a = go(normed_a, "y"), go(normed_a, "c")
    d0 = go(lax.dynamic_slice_in_dim(down_weight, place * quarter, quarter, 0), "y")
    gu1, gu2 = go(gu0, "x"), go(gu0, "z")
    early = gate(cotangent)
    cot = [early[:, s] for s in every]
    tokens_of = gate(adapter_in)
    tokens_of = [tokens_of[:, s] for s in every]
    far_a, near_a, d0, gu1, gu2, *both = close(far_a, near_a, d0, gu1, gu2, *cot, *tokens_of)
    cot, tokens_of = both[:seqs], both[seqs:]

    head_shape = ((heads, seq_len, HD), bf16, True)

    def attn_fwd(s, blocks):
        *kept, at, p0, p1, p2, p3 = whole_call(
            functools.partial(attn_fwd_kernel, s),
            [head_shape] * 4 + [((8, seq_len), f32, True), ((members, rows, cols), bf16, True)] + parts(4),
            [scal],
            [*blocks, w_qkv, turn_rows, turn_blocks, out_weight],
            vmem=16,
            name="attn_fwd",
        )
        return kept, at, p0, p1, p2, p3

    far_b, near_b = go(normed_b, "y"), go(normed_b, "c")
    gu3, d2 = go(gu2, "x"), go(d0, "z")
    one = {0: [normed_a, near_a, far_a, hop(far_a)]}
    qkvo, att = {}, {}
    qkvo[0], att[0], *sums = attn_fwd(0, one[0])
    p0, p1, p2, p3, far_b, near_b, gu3, d2 = close(*sums, far_b, near_b, gu3, d2)
    across_a, own_a, p1 = close(low(p2, hop(p3)), p0, p1)

    far_a, d1, near_a = go(across_a, "y"), go(d0, "x"), go(p1, "c")
    one[1] = [gate(normed_b), near_b, far_b, hop(far_b)]
    qkvo[1], att[1], *sums = attn_fwd(1, one[1])
    p0, p1, p2, p3, far_a, d1, near_a = close(*sums, far_a, d1, near_a)
    across_b, own_b, p1 = close(low(p2, hop(p3)), p0, p1)

    far_b, d3, near_b = go(across_b, "y"), go(d1, "z"), go(p1, "c")
    far_gu = jnp.concatenate([gate(gu0), gu1, gu2, gu3], axis=1)

    def mid_of(s, *addends):
        return whole_call(
            mid_kernel,
            [(tok, f32), (tok, f32), (tok, bf16)],
            [],
            [gate(latent[s]), *addends, gains],
            vmem=8,
            name="mid",
        )

    proj, mid, three, ffn, block_out, mlp_g, gu_g = {}, {}, {}, {}, {}, {}, {}
    proj[0], mid[0], own = mid_of(0, own_a, near_a, far_a)
    three[0] = [own, hop(own)]
    far_b, near_b, d3, far_gu, t0, t1 = close(far_b, near_b, d3, far_gu, *three[0])
    three[0] = [t0, t1]

    far_d = jnp.concatenate([gate(d0), d1, d2, d3], axis=0)
    mlp_weights = [w_gu, far_gu, down_weight, far_d]
    hid_shape = ((2, rows, units), bf16, True)

    def ffn_fwd(s):
        *ffn[s], p0, p1 = whole_call(
            mlp_fwd_kernel, [hid_shape] * 6 + parts(2), [], [*three[s], *mlp_weights], vmem=25, name="mlp_fwd"
        )
        return p0, hop(p1)

    def out_of(s, *addends):
        block_out[s], own, gain[3, s] = whole_call(
            functools.partial(out_kernel, s),
            [(tok, bf16), (tok, bf16), ((1, width), f32)],
            [scal],
            [mid[s], *addends, cot[s], gains],
            vmem=10,
            name="out",
        )
        mlp_g[s] = [own, hop(own)]

    def ffn_bwd(s):
        *gu_g[s], p0, p1 = whole_call(
            mlp_bwd_kernel,
            [hid_shape] * 4 + parts(2),
            [],
            [*mlp_g[s], *mlp_weights, *ffn[s][1:3], *ffn[s][4:6]],
            vmem=25,
            name="mlp_bwd",
        )
        return p0, p1

    mid_grad, attn_g, stacked = {}, {}, {}

    def back_of(s, *addends):
        mid_grad[s], own, gain[1, s], gain[2, s] = whole_call(
            functools.partial(back_kernel, s),
            [(tok, f32), (tok, bf16), ((1, width), f32), ((1, width), f32)],
            [scal],
            [mid[s], proj[s], *addends, cot[s], gains],
            vmem=12,
            name="back",
        )
        return own

    sum_a = ffn_fwd(0)
    proj[1], mid[1], own = mid_of(1, own_b, near_b, far_b)
    three[1] = [own, hop(own)]
    out_of(0, *sum_a)
    sum_b = ffn_fwd(1)
    p0, p1 = ffn_bwd(0)
    sum_a = p0, hop(p1)
    out_of(1, *sum_b)
    grad_a = back_of(0, *sum_a)
    grad_a, b0, b1 = close(grad_a, *mlp_g[1])
    mlp_g[1] = [b0, b1]

    def full_grad(xs, ys):
        xs, ys = [jnp.concatenate([a.reshape(-1, a.shape[-1]) for a in part], 0) for part in (xs, ys)]
        return lax.dot_general(xs, ys, (((0,), (0,)), ((), ())), preferred_element_type=f32).astype(bf16)

    def unit_grad(sets, ys, first):
        ys = [gate(ys[0]), *ys[1:]]
        if fast:
            keep, send0, send1 = grad_units(me, sets, ys, dp, first)
            split = (2, 2) + keep.shape[-2:]
            return keep.reshape((2,) + split), send0.reshape(split), send1.reshape(split)
        own, far = [full_grad(xs, ys) for xs in sets]
        far = jnp.concatenate([lax.dynamic_slice_in_dim(far, (place ^ a) * quarter, quarter, 0) for a in range(4)], axis=0)
        total = low(own, swap(far, "tensor", 2))
        return lax.psum_scatter(total, "dp", scatter_dimension=1, tiled=True).astype(f32)

    far_a, near_a = go(grad_a, "y"), go(grad_a, "c")
    sum_b = ffn_bwd(1)
    flat_three = [b for s in every for b in three[s]]
    flat_mlp = [b for s in every for b in mlp_g[s]]
    flat_one = [b for s in every for b in one[s]]
    hiddens = [[ffn[s][3 * n] for s in every] for n in (0, 1)]
    gates = [[gu_g[s][2 * n] for s in every] for n in (0, 1)]
    ups = [[gu_g[s][2 * n + 1] for s in every] for n in (0, 1)]

    if fast:
        down_keep, down0, down1 = unit_grad(hiddens, flat_mlp, "x")
        p0, p1, far_a, near_a, down0, down1 = close(*sum_b, far_a, near_a, down0, down1)
    else:
        p0, p1, far_a, near_a = close(*sum_b, far_a, near_a)
    grad_b = close(back_of(1, p0, hop(p1)))[0]


    head_f32 = (heads, seq_len, HD)

    def attn_bwd(s, blocks):
        stacked[s], p0, p1, p2, p3 = whole_call(
            functools.partial(attn_bwd_kernel, s),
            [((members, rows, 3 * cols), bf16, True)] + parts(4),
            [scal],
            [*blocks, out_weight, *qkvo[s], turn_rows, turn_blocks, w_qkv],
            scratch=[pltpu.VMEM(head_f32, bf16)] + [pltpu.VMEM(head_f32, f32)] * 3,
            vmem=19,
            name="attn_bwd",
        )
        return p0, p1, p2, p3

    far_b, near_b = go(grad_b, "y"), go(grad_b, "c")
    attn_g[0] = [gate(grad_a), near_a, far_a, hop(far_a)]
    sums = attn_bwd(0, attn_g[0])
    if fast:
        down_got1 = go(down1, "x")
        gate_keep, gate0, gate1 = unit_grad(gates, flat_three, "z")
        p0, p1, p2, p3, far_b, near_b, gate0, gate1, down_got1 = close(*sums, far_b, near_b, gate0, gate1, down_got1)
    else:
        p0, p1, p2, p3, far_b, near_b = close(*sums, far_b, near_b)
    across_a, own_a, p1 = close(low(p2, hop(p3)), p0, p1)

    far_a, near_a = go(across_a, "y"), go(p1, "c")
    attn_g[1] = [gate(grad_b), near_b, far_b, hop(far_b)]
    sums = attn_bwd(1, attn_g[1])
    if fast:
        down_got0, gate_got1 = go(down0, "x"), go(gate1, "z")
        up_keep, up0, up1 = unit_grad(ups, flat_three, "y")
        p0, p1, p2, p3, far_a, near_a, down_got0, gate_got1, up0, up1 = close(
            *sums, far_a, near_a, down_got0, gate_got1, up0, up1
        )
    else:
        p0, p1, p2, p3, far_a, near_a = close(*sums, far_a, near_a)
    across_b, own_b, p1 = close(low(p2, hop(p3)), p0, p1)

    latent_grad = {}

    def last_of(s, *addends):
        latent_grad[s], gain[0, s] = whole_call(
            last_kernel,
            [(tok, bf16), ((1, width), f32)],
            [],
            [gate(latent[s]), *addends, mid_grad[s], gains],
            vmem=10,
            name="last",
        )

    both_me = jnp.concatenate([me, mine.reshape(1)])

    far_b, near_b = go(across_b, "y"), go(p1, "c")
    last_of(0, own_a, near_a, far_a)
    flat_attn = [b for s in every for b in attn_g[s]]
    if fast:
        gate_got0 = go(gate0, "z")
        down_next = low(gate(down_keep)[1], down_got1)
        gate_got2 = swap(low(gate(gate_keep)[1], gate_got1), *moves["x"])
        down_stay = low(gate(down_keep)[0], down_got0)
        first = [gate(flat_one[0]), *flat_one[1:]]
        attn_keep, attn_send = grad_rows(
            me, [(first, [stacked[s] for s in every]), (flat_attn, [att[s] for s in every])], dp, cols
        )
        lead = (2, 2) + attn_keep.shape[1:]
        half = width // dp
        attn_keep, attn_send = attn_keep.reshape(lead), attn_send.reshape(lead)
        far_b, near_b, attn_send, gate_got0, gate_got2, down_next, down_stay = close(
            far_b, near_b, attn_send, gate_got0, gate_got2, down_next, down_stay
        )
    else:
        far_b, near_b = close(far_b, near_b)

    last_of(1, own_b, near_b, far_b)
    grads = [latent_grad[s] for s in every]
    d_gains = jnp.concatenate([sum(gain[g, s] for s in every) for g in range(4)], axis=0)
    if fast:
        up_got1, attn_got, down_got2 = go(up1, "y"), go(attn_send, "x"), go(down_next, "z")
        gate2 = low(low(gate(gate_keep)[0], gate_got0), gate_got2)
        gate_got3 = swap(gate2[1], *moves["y"])
        d_gains = jnp.concatenate([d_gains, jnp.zeros_like(d_gains)], axis=0)
        keep, send = grad_adapter(both_me, tokens_of, grads, d_gains, dp)
        send, up_got1, attn_got, gate_got3, down_got2 = close(send, up_got1, attn_got, gate_got3, down_got2)
        total = close(low(keep, hop(send)))[0]

        part = total.shape[-2]
        ranges = total.reshape(2, 2, 2, 2, part, width)
        orders = ["zxyw", "yxzw"]
        cut = width * 5 // 8
        axes = ["ywzx"] * 2
        state = [ranges[..., :cut], ranges[..., cut:]]

        def adapter_round(r, state):
            kept, got = [], []
            for n in range(2):
                m = orders[n][r]
                at = axes[n].index(m)
                axes[n] = axes[n].replace(m, "")
                kept.append(lax.index_in_dim(state[n], 0, at, keepdims=False))
                got.append(swap(lax.index_in_dim(state[n], 1, at, keepdims=False), *moves[m]))
            return kept, got

        up_got0 = go(up0, "y")
        up_got2 = swap(low(gate(up_keep)[1], up_got1), *moves["x"])
        kept, got = adapter_round(0, state)
        attn = low(gate(attn_keep), attn_got)
        attn_got = swap(attn[:, 1], *moves["w"])
        gate3 = low(gate(gate2[0]), gate_got3)
        grad_in = [
            lax.dot_general(gate(g), adapter_weight, (((1,), (1,)), ((), ())), preferred_element_type=f32).astype(bf16)
            for g in grads
        ]
        out = jnp.stack([gate(block_out[s]) for s in every], axis=1)
        down2 = low(gate(down_stay), down_got2)
        got0, got1, up_got0, up_got2, attn_got, out, down2 = close(*got, up_got0, up_got2, attn_got, out, down2)

        down_got3, gate_got4 = go(down2[1], "y"), go(gate3[1], "w")
        state = [low(k, g) for k, g in zip(kept, (got0, got1))]
        both_x = [[lax.index_in_dim(state[n], i, 2, keepdims=False) for n in range(2)] for i in (0, 1)]
        kept = both_x[0]
        got = [swap(jnp.concatenate(both_x[1], axis=-1), *moves["x"])]
        axes = ["yw", "wz"]
        up2 = low(low(gate(up_keep)[0], up_got0), up_got2)
        up_got3 = swap(up2[1], *moves["z"])
        attn = low(gate(attn)[:, 0], attn_got)
        attn_got = swap(attn[1], *moves["z"])
        got0, up_got3, attn_got, down_got3, gate_got4 = close(*got, up_got3, attn_got, down_got3, gate_got4)
        got0, got1 = got0[..., :cut], got0[..., cut:]

        down3 = low(gate(down2[0]), down_got3)
        down_got4 = swap(down3[1], *moves["w"])
        d_gate = plus(gate(gate3[0]), gate_got4)
        state = [low(k, g) for k, g in zip(kept, (got0, got1))]
        kept, got = adapter_round(2, state)
        up3 = low(gate(up2[0]), up_got3)
        up_got4 = swap(up3[1], *moves["w"])
        attn = plus(gate(attn[0]), attn_got)
        got0, got1, up_got4, down_got4, attn, d_gate = close(*got, up_got4, down_got4, attn, d_gate)

        state = [low(k, g) for k, g in zip(kept, (got0, got1))]
        kept, got = adapter_round(3, state)
        d_up = plus(gate(up3[0]), up_got4)
        d_down = plus(gate(down3[0]), down_got4)
        rows_out = part - 8
        d_adapt = jnp.concatenate([plus(k[:rows_out], g[:rows_out]) for k, g in zip(kept, got)], axis=-1)
        d_gains = plus(kept[0][rows_out : rows_out + 4, :128], got[0][rows_out : rows_out + 4, :128])
        share = 128 // members
        d_gains = lax.dynamic_slice_in_dim(d_gains, mine * share, share, 1)
        d_qkv = attn[:3].transpose(1, 0, 2)
        d_out = jnp.concatenate([attn[3, :, :half], attn[3, :, half:]], axis=0)
    else:
        out = jnp.stack([block_out[s] for s in every], axis=1)
        share = width // (dp * members)
        d_gains = lax.psum(d_gains, ("dp", "tensor"))
        d_gains = lax.dynamic_slice_in_dim(d_gains, (me[0] * members + mine) * share, share, 1)
        d_down = unit_grad(hiddens, flat_mlp, "z")
        d_gate = unit_grad(gates, flat_three, "x")
        d_up = unit_grad(ups, flat_three, "y")

        def reduced(xs, ys, dim):
            return lax.psum_scatter(full_grad(xs, ys), "dp", scatter_dimension=dim, tiled=True).astype(f32)

        d_qkv = reduced(flat_one, [stacked[s] for s in every], 0).reshape(-1, 3, cols)
        d_out = reduced([att[s] for s in every], flat_attn, 1)
        full = full_grad([tokens_of[s] for s in every], grads).astype(f32)
        d_adapt = lax.psum_scatter(full, ("dp", "tensor"), scatter_dimension=0, tiled=True)
        grad_in = [
            lax.dot_general(g, adapter_weight, (((1,), (1,)), ((), ())), preferred_element_type=f32).astype(bf16)
            for g in grads
        ]
    grad_in = jnp.stack(grad_in, axis=1)
    d_gate_up = jnp.stack([d_gate, d_up]).transpose(2, 0, 1)
    return (out, grad_in, d_adapt, d_gains, d_qkv, d_out, d_gate_up, d_down)


def solution(mesh):
    return jax.shard_map(
        body,
        mesh=mesh,
        in_specs=(
            P("tensor", "dp", None),
            P("dp"),
            P("tensor", "dp", None),
            P(),
            P(),
            P(None, None, "tensor"),
            P("tensor", None),
            P(None, None, "tensor"),
            P("tensor", None),
        ),
        out_specs=(
            P("tensor", "dp", None),
            P("tensor", "dp", None),
            P(("dp", "tensor"), None),
            P(None, ("dp", "tensor")),
            P("dp", None, "tensor"),
            P("tensor", "dp"),
            P("dp", None, "tensor"),
            P("tensor", "dp"),
        ),
        check_vma=False,
    )
```
